256 devices in a mesh: gx: 16 (over x_lo, z), gy: 16 (over y, x_hi, core).
Axes of the slice: x: 4 (x_hi: 2, x_lo: 2; x = x_hi * 2 + x_lo), y: 4, z: 8, core: 2. Of those that a mesh axis runs over, the one named last changes fastest.
Arguments:
- polar: float32 [1024, 12288], P('gx', 'gy'), may hold values from -3.140625 to 3.140625
- azimuth: float32 [1024, 12288], P('gx', 'gy'), may hold values from -3.140625 to 3.140625
- grains: int32 [1024, 12288], P('gx', 'gy'), may hold values from 0 to 255, as said below
- stiffness: float32 [256], replicated, may hold values from 0.5 to 2
- anisotropy: float32 [256], replicated, may hold values from 0.2 to 2
- axis_polar: float32 [256], replicated, may hold values from -3.140625 to 3.140625
- axis_azimuth: float32 [256], replicated, may hold values from -3.140625 to 3.140625
- applied_field: float32 [3], replicated, may hold values from -3 to 3
Outputs:
- moment: float32 [3, 1024, 12288], P(None, 'gx', 'gy')
- spin_flip: float32 [1024, 1024], P(('gx', 'gy'))
- non_flip: float32 [1024, 1024], P(('gx', 'gy'))
The draws below stay inside these ranges and needn't reach their ends.
Inputs may be any that keep to these rules, and one draw needn't show every extreme that they name: `grains`: grain label of each cell, a row of the grain tables.
All inputs are finite; a program needn't handle non-finite values.
Results may differ from the reference program's by a relative error of at most 0.0003.
Values sent between devices are 32-bit elements; how exact they have to be, the bound alone decides.
No kernel may reach another device: no remote copies, remote signals or barrier semaphores. Data moves between devices by JAX's collectives and lax.ppermute only.
A program may use at most 128 MiB of HBM per device.

```python
import math
import jax
import jax.numpy as jnp
from jax import lax

NZ = 12
STEPS = 4
NGRAIN = 256
NX = 1024
NY = 1024


def grain_index(key, length):
    bits = jax.random.randint(key, (length,), 0, 2).astype(jnp.int32)
    start = jnp.zeros((1,), jnp.int32)
    return jnp.concatenate([start, jnp.cumsum(bits[:-1]).astype(jnp.int32)])


def draw_grains(key, part):
    key_x, key_y, key_z, key_label = jax.random.split(key, 4)
    index_x = grain_index(key_x, NX)
    index_y = grain_index(key_y, NY)
    index_z = grain_index(key_z, NZ)
    labels = jax.random.randint(key_label, (NX, NY, NZ), 0, NGRAIN).astype(jnp.int32)
    fine = labels[index_x[:, None, None], index_y[None, :, None], index_z[None, None, :]]
    return fine.reshape(NX, NY * NZ).astype(jnp.int32)


def bell_draw(own_key, shape, scale, reach, kind=jnp.bfloat16):
    entries = scale * jax.random.normal(own_key, shape, jnp.float32)
    return jnp.clip(entries, min=-reach, max=reach).astype(kind)


def setup_inputs(seed: int = 0) -> dict:
    key_list = jax.random.split(jax.random.key(seed), 9)
    polar = jnp.clip(jax.random.uniform(key_list[0], (NX, NY * NZ), jnp.float32, -3.140625, 3.140625), -3.140625, 3.140625)
    azimuth = jnp.clip(jax.random.uniform(key_list[1], (NX, NY * NZ), jnp.float32, -3.140625, 3.140625), -3.140625, 3.140625)
    grains = draw_grains(jax.random.fold_in(key_list[8], 71), 0)
    stiffness = jnp.clip(jnp.exp(jax.random.uniform(key_list[3], (NGRAIN,), jnp.float32, math.log(0.5), math.log(2.0))), 0.5, 2.0)
    anisotropy = jnp.clip(jnp.exp(jax.random.uniform(key_list[4], (NGRAIN,), jnp.float32, math.log(0.2), math.log(2.0))), 0.2, 2.0)
    axis_polar = jnp.clip(jax.random.uniform(key_list[5], (NGRAIN,), jnp.float32, -3.140625, 3.140625), -3.140625, 3.140625)
    axis_azimuth = jnp.clip(jax.random.uniform(key_list[6], (NGRAIN,), jnp.float32, -3.140625, 3.140625), -3.140625, 3.140625)
    applied_field = bell_draw(key_list[7], (3,), 0.5, 3.0, jnp.float32)
    return dict(polar=polar, azimuth=azimuth, grains=grains, stiffness=stiffness, anisotropy=anisotropy, axis_polar=axis_polar, axis_azimuth=axis_azimuth, applied_field=applied_field)


damping = 0.5
time_step = 0.12

def couple(left, right):
    return 2.0 * left * right / (left + right)

def cross(first, second):
    return jnp.stack([first[1] * second[2] - first[2] * second[1], first[2] * second[0] - first[0] * second[2], first[0] * second[1] - first[1] * second[0]])

def advance(center, plus_x, minus_x, plus_y, minus_y, weight, weight_px, weight_mx, weight_py, weight_my, strength, easy_axis, applied):
    field = couple(weight, weight_px) * (plus_x - center) + couple(weight, weight_mx) * (minus_x - center)
    field = field + couple(weight, weight_py) * (plus_y - center) + couple(weight, weight_my) * (minus_y - center)
    flux = couple(weight[1:], weight[:-1]) * (center[:, 1:] - center[:, :-1])
    zeros = jnp.zeros_like(center[:, :1])
    field = field + jnp.concatenate([flux, zeros], axis=1) - jnp.concatenate([zeros, flux], axis=1)
    project = easy_axis[0] * center[0] + easy_axis[1] * center[1] + easy_axis[2] * center[2]
    field = field + strength * project * easy_axis + applied.reshape(3, 1, 1, 1)
    torque = cross(center, field)
    damped = cross(center, torque)
    moved = center - time_step / (1.0 + damping * damping) * (torque + damping * damped)
    return moved / jnp.sqrt(moved[0] * moved[0] + moved[1] * moved[1] + moved[2] * moved[2])

def cross_sections(real_part, imag_part, wave_x, wave_y):
    squared = wave_x * wave_x + wave_y * wave_y
    inverse = 1.0 / jnp.sqrt(jnp.maximum(squared, 1.0))
    beam_stop = jnp.where(squared > 0.5, 1.0, 0.0).astype(real_part.dtype)
    unit_x = wave_x * inverse
    unit_y = wave_y * inverse
    pieces = []
    for part in (real_part, imag_part):
        along = unit_x * part[0] + unit_y * part[1]
        pieces.append((part[0] - unit_x * along, part[1] - unit_y * along, part[2]))
    non_flip = pieces[0][0] * pieces[0][0] + pieces[1][0] * pieces[1][0]
    spin_flip = pieces[0][1] * pieces[0][1] + pieces[1][1] * pieces[1][1] + pieces[0][2] * pieces[0][2] + pieces[1][2] * pieces[1][2]
    return (spin_flip * beam_stop, non_flip * beam_stop)

def signed_waves(length):
    counter = jnp.arange(length, dtype=jnp.int32)
    return jnp.where(counter < length // 2, counter, counter - length).astype(jnp.float32)

def to_volume(array):
    return jnp.transpose(array.reshape(NX, NY, NZ), (2, 0, 1))

def reference(polar, azimuth, grains, stiffness, anisotropy, axis_polar, axis_azimuth, applied_field):
    polar = to_volume(polar)
    azimuth = to_volume(azimuth)
    grains = to_volume(grains)
    moment = jnp.stack([jnp.sin(polar) * jnp.cos(azimuth), jnp.sin(polar) * jnp.sin(azimuth), jnp.cos(polar)])
    weight = stiffness[grains]
    strength = anisotropy[grains]
    easy_x = jnp.sin(axis_polar) * jnp.cos(axis_azimuth)
    easy_y = jnp.sin(axis_polar) * jnp.sin(axis_azimuth)
    easy_z = jnp.cos(axis_polar)
    easy_axis = jnp.stack([easy_x[grains], easy_y[grains], easy_z[grains]])
    weight_px = jnp.roll(weight, -1, axis=1)
    weight_mx = jnp.roll(weight, 1, axis=1)
    weight_py = jnp.roll(weight, -1, axis=2)
    weight_my = jnp.roll(weight, 1, axis=2)
    for turn_index in range(STEPS):
        moment = advance(moment, jnp.roll(moment, -1, axis=2), jnp.roll(moment, 1, axis=2), jnp.roll(moment, -1, axis=3), jnp.roll(moment, 1, axis=3), weight, weight_px, weight_mx, weight_py, weight_my, strength, easy_axis, applied_field)
    layer = lax.optimization_barrier(jnp.sum(moment, axis=1)) / math.sqrt(NZ)
    spectrum = jnp.fft.fft2(layer, axes=(1, 2))
    scale = math.sqrt(NX * NY)
    real_part = jnp.real(spectrum).astype(jnp.float32) / scale
    imag_part = jnp.imag(spectrum).astype(jnp.float32) / scale
    spin_flip, non_flip = cross_sections(real_part, imag_part, signed_waves(NX)[:, None], signed_waves(NY)[None, :])
    flat_moment = jnp.transpose(moment, (0, 2, 3, 1)).reshape(3, NX, NY * NZ)
    return (flat_moment, spin_flip, non_flip)
```

```python
import math

import jax
import jax.numpy as jnp
import numpy as np
from jax import lax
from jax.experimental import pallas as pl
from jax.experimental.pallas import tpu as pltpu
from jax.sharding import PartitionSpec as P

NZ = 12
STEPS = 4
DAMPING = 0.5
TIME_STEP = 0.12
GAIN = TIME_STEP / (1.0 + DAMPING * DAMPING)

WX = 64
WY = 64
COLS = WY * NZ
LANES = COLS + 128
ROWS = WX + 8
STRIPS = ROWS // 8
NGRAIN = 256

COS_POLY = (
    1.0,
    -0.5,
    0.0416666641831398,
    -0.0013888862449675798,
    2.4800550818326883e-05,
    -2.753476167072222e-07,
    2.060329462594268e-09,
    -9.721622812319808e-12,
)
SIN_POLY = (
    1.0,
    -0.1666666567325592,
    0.008333321660757065,
    -0.00019840530876535922,
    2.7535795652511297e-06,
    -2.472832427713456e-08,
    1.361144114087054e-10,
)


def poly(coefs, t):
    acc = coefs[-1] * t + coefs[-2]
    for c in coefs[-3::-1]:
        acc = acc * t + c
    return acc


def sincos(x):
    t = x * x
    return x * poly(SIN_POLY, t), poly(COS_POLY, t)


def split(x):
    hi = x.astype(jnp.bfloat16)
    lo = (x - hi.astype(jnp.float32)).astype(jnp.bfloat16)
    return hi, lo


def mm(a, b):
    return jnp.dot(a, b, preferred_element_type=jnp.float32)


def iota(shape, dim):
    return lax.broadcasted_iota(jnp.int32, shape, dim)


def llg_kernel(
    polar, azimuth, grains, halo_y, halo_xh, halo_xl, tables, applied, sum_z,
    moment, payload,
    pe, ae, ge, m0, m1, wt, cx, cxd, cy, cz, ks, ux, uy, uz,
):
    for i, (src, dst) in enumerate(((polar, pe), (azimuth, ae), (grains, ge))):
        dst[0:WX, 0:COLS] = src[...].astype(jnp.float32)
        dst[0:WX, COLS:LANES] = halo_y[i * WX : (i + 1) * WX, :]
        sub = iota((8, LANES), 0)
        dst[WX:ROWS, :] = jnp.where(
            sub < 4, halo_xh[8 * i : 8 * i + 8, :], halo_xl[8 * i : 8 * i + 8, :]
        )
    tabs = [
        [jnp.broadcast_to(tables[r : r + 1, h * 128 : h * 128 + 128], (8, 128)) for h in range(2)]
        for r in range(5)
    ]

    def strip(ref, s, *lead):
        start = pl.multiple_of(s * 8, 8)
        return ref[(*lead, pl.ds(start, 8), slice(None))]

    def put(ref, s, value, *lead):
        start = pl.multiple_of(s * 8, 8)
        ref[(*lead, pl.ds(start, 8), slice(None))] = value

    def nxt(s):
        return jnp.where(s == STRIPS - 1, 0, s + 1)

    def prv(s):
        return jnp.where(s == 0, STRIPS - 1, s - 1)

    def up(cur, following):
        return pltpu.roll(jnp.where(iota(cur.shape, 0) == 0, following, cur), 7, 0)

    def down(cur, previous):
        return pltpu.roll(jnp.where(iota(cur.shape, 0) == 7, previous, cur), 1, 0)

    def setup(s, carry):
        sp, cp = sincos(strip(pe, s))
        sa, ca = sincos(strip(ae, s))
        put(m0, s, sp * ca, 0)
        put(m0, s, sp * sa, 1)
        put(m0, s, cp, 2)
        labels = strip(ge, s).astype(jnp.int32)
        low = labels & 127
        first = labels < 128
        for r, ref in enumerate((wt, ks, ux, uy, uz)):
            parts = []
            for t in range(LANES // 128):
                sl = slice(128 * t, 128 * t + 128)
                a = jnp.take_along_axis(tabs[r][0], low[:, sl], axis=1, mode="promise_in_bounds")
                b = jnp.take_along_axis(tabs[r][1], low[:, sl], axis=1, mode="promise_in_bounds")
                parts.append(jnp.where(first[:, sl], a, b))
            put(ref, s, jnp.concatenate(parts, axis=1))
        return carry

    lax.fori_loop(0, STRIPS, setup, 0)

    def couple(p, q):
        return 2.0 * p * q / (p + q)

    def couplings(s, carry):
        w = strip(wt, s)
        put(cx, s, couple(w, up(w, strip(wt, nxt(s)))))
        put(cxd, s, couple(w, down(w, strip(wt, prv(s)))))
        put(cy, s, couple(w, pltpu.roll(w, LANES - NZ, 1)))
        lane = iota(w.shape, 1)
        depth = jnp.where(lane < COLS + 64, lane, lane - LANES + 6 * NZ + COLS) % NZ
        linked = depth != NZ - 1
        put(cz, s, jnp.where(linked, couple(w, pltpu.roll(w, LANES - 1, 1)), 0.0))
        return carry

    lax.fori_loop(0, STRIPS, couplings, 0)

    def step(src, dst, s):
        after, before = nxt(s), prv(s)
        m = [strip(src, s, c) for c in range(3)]
        u = [strip(r, s) for r in (ux, uy, uz)]
        kx, kxd, ky, kz = strip(cx, s), strip(cxd, s), strip(cy, s), strip(cz, s)
        proj = strip(ks, s) * (u[0] * m[0] + u[1] * m[1] + u[2] * m[2])
        h = []
        for c in range(3):
            f = kx * (up(m[c], strip(src, after, c)) - m[c])
            f = f + kxd * (down(m[c], strip(src, before, c)) - m[c])
            fy = ky * (pltpu.roll(m[c], LANES - NZ, 1) - m[c])
            f = f + fy - pltpu.roll(fy, NZ, 1)
            fz = kz * (pltpu.roll(m[c], LANES - 1, 1) - m[c])
            f = f + fz - pltpu.roll(fz, 1, 1)
            h.append(f + proj * u[c] + applied[c])
        t = cross(m, h)
        d = cross(m, t)
        v = [m[c] - GAIN * (t[c] + DAMPING * d[c]) for c in range(3)]
        r = lax.rsqrt(v[0] * v[0] + v[1] * v[1] + v[2] * v[2])
        for c in range(3):
            put(dst, s, v[c] * r, c)

    def one(src, dst, count):
        def body(s, carry):
            step(src, dst, s)
            return carry

        lax.fori_loop(0, count, body, 0)

    one(m0, m1, STRIPS)
    one(m1, m0, STRIPS)
    one(m0, m1, STRIPS)
    one(m1, m0, STRIPS - 1)

    for c in range(3):
        moment[c] = m0[c, 0:WX, 0:COLS]

    m = jnp.concatenate([m0[c, 0:WX, 0:COLS] for c in range(3)], axis=0)
    hi, lo = split(m)
    out = mm(hi, sum_z[...]) + mm(lo, sum_z[...])
    lane = iota((WX, 128), 1)
    sides = []
    for half in range(2):
        o = [out[c * WX : (c + 1) * WX, half * 128 : half * 128 + 128] for c in range(3)]
        sides.append(jnp.where(lane < 32, o[0], jnp.where(lane < 64, o[1], o[2])))
    turned = jnp.concatenate(sides, axis=0).T
    for cp in range(8):
        payload[pl.ds(cp, 16, stride=8), :] = turned[cp * 16 : cp * 16 + 16, :]


def cross(first, second):
    return [
        first[1] * second[2] - first[2] * second[1],
        first[2] * second[0] - first[0] * second[2],
        first[0] * second[1] - first[1] * second[0],
    ]


def x_kernel(got, twiddle, waves_hi, waves_lo, out):
    f = [got[8 * i : 8 * i + 8, :] for i in range(16)]
    even = [f[i] + f[16 - i] for i in range(1, 8)]
    odd = [f[i] - f[16 - i] for i in range(1, 8)]
    real, imag = [], []
    for r in range(9):
        acc = f[0] + f[8] if r % 2 == 0 else f[0] - f[8]
        for i in range(1, 8):
            w = math.cos(2.0 * math.pi * ((r * i) % 16) / 16)
            acc = acc + even[i - 1] * w
        real.append(acc)
        acc = None
        if r not in (0, 8):
            for i in range(1, 8):
                w = -math.sin(2.0 * math.pi * ((r * i) % 16) / 16)
                acc = odd[i - 1] * w if acc is None else acc + odd[i - 1] * w
        imag.append(acc)
    rows_re, rows_im = [], []
    for r in range(16):
        gr = real[r] if r <= 8 else real[16 - r]
        gi = imag[r] if r <= 8 else -imag[16 - r]
        c = twiddle[r : r + 1, :]
        s = twiddle[16 + r : 17 + r, :]
        if gi is None:
            rows_re.append(gr * c)
            rows_im.append(-gr * s)
        else:
            rows_re.append(gr * c + gi * s)
            rows_im.append(gi * c - gr * s)
    order = []
    for top in range(4):
        order += [rows_re[4 * top + low] for low in range(4)]
        order += [rows_im[4 * top + low] for low in range(4)]
    turned = jnp.concatenate(order, axis=0).T
    lane = iota((WX, 128), 1)
    imaginary = lane % 64 >= 32
    full = []
    for h in range(2):
        hi, lo = split(turned[h * 64 : h * 64 + 64, :])
        both = mm(waves_hi[...], hi) + (mm(waves_hi[...], lo) + mm(waves_lo[...], hi))
        tiles = []
        for t in range(2):
            p = both[0:64, t * 128 : t * 128 + 128]
            q = both[64:128, t * 128 : t * 128 + 128]
            tiles.append(
                p + jnp.where(imaginary, -pltpu.roll(q, 32, 1), pltpu.roll(q, 96, 1))
            )
        full.append(tiles)
    for top in range(4):
        a, b = full[0][top // 2], full[1][top // 2]
        if top % 2 == 0:
            b = pltpu.roll(b, 64, 1)
        else:
            a = pltpu.roll(a, 64, 1)
        out[pl.ds(top, 64, stride=4), :] = jnp.where(lane < 64, a, b)


def y_kernel(first_row, got, waves_hi, waves_lo, twiddle, spin_flip, non_flip, turned):
    for t in range(2):
        turned[t] = got[128 * t : 128 * t + 128, :].T
    tiles = []
    for h in range(2):
        for p in range(2):
            for c in range(3):
                rows = pl.ds(h * 64 + 2 * c + p, 8, stride=8)
                tiles.append(jnp.concatenate([turned[t, rows, :] for t in range(2)], axis=1))
    hi, lo = split(jnp.concatenate(tiles, axis=0))
    both = mm(hi, waves_hi[...]) + (mm(lo, waves_hi[...]) + mm(hi, waves_lo[...]))
    width = 256
    sign = jnp.where(iota((8, width), 0) < 4, 1.0, -1.0)

    def spin(z):
        return pltpu.roll(z, 4, 0) * sign

    parts = {}
    for h in range(2):
        for p in range(2):
            b = 2 * p + h
            for c in range(3):
                row = ((h * 2 + p) * 3 + c) * 8
                z = both[row : row + 8, 0:width] + spin(both[row : row + 8, width : 2 * width])
                if b:
                    z = z * twiddle[b : b + 1, :] + spin(z) * twiddle[4 + b : 5 + b, :]
                parts[h, p, c] = z
    spectrum = [[None] * 3 for _ in range(4)]
    for c in range(3):
        plus = [parts[h, 0, c] + parts[h, 1, c] for h in range(2)]
        minus = [parts[h, 0, c] - parts[h, 1, c] for h in range(2)]
        turn = spin(minus[1])
        spectrum[0][c] = plus[0] + plus[1]
        spectrum[2][c] = plus[0] - plus[1]
        spectrum[1][c] = minus[0] + turn
        spectrum[3][c] = minus[0] - turn
    kx = first_row[0] + iota((8, width), 0) % 4
    wave_x = jnp.where(kx < 512, kx, kx - 1024).astype(jnp.float32)
    scale = 1.0 / (NZ * 1024.0 * 1024.0)
    for d in range(4):
        ky = iota((8, width), 1) + 256 * d
        wave_y = jnp.where(ky < 512, ky, ky - 1024).astype(jnp.float32)
        squared = wave_x * wave_x + wave_y * wave_y
        inverse = lax.rsqrt(jnp.maximum(squared, 1.0))
        unit_x = wave_x * inverse
        unit_y = wave_y * inverse
        stop = jnp.where(squared > 0.5, scale, 0.0)
        sx, sy, sz = spectrum[d]
        along = unit_x * sx + unit_y * sy
        px = sx - unit_x * along
        py = sy - unit_y * along
        nf = px * px
        sf = py * py + sz * sz
        nf = (nf + pltpu.roll(nf, 4, 0)) * stop
        sf = (sf + pltpu.roll(sf, 4, 0)) * stop
        non_flip[:, width * d : width * d + width] = nf[0:4, :]
        spin_flip[:, width * d : width * d + width] = sf[0:4, :]


def pieces(x):
    hi = x.astype(jnp.bfloat16)
    lo = (x - hi.astype(np.float64)).astype(jnp.bfloat16)
    return jnp.asarray(hi), jnp.asarray(lo)


def sum_matrix():
    y = np.arange(COLS) // NZ
    col = np.arange(256)
    h, p, j = col // 128, col % 32 // 16, col % 16
    return jnp.asarray((y[:, None] == (4 * j + 2 * p + h)[None, :]).astype(jnp.bfloat16))


def x_tables():
    r = np.arange(16)[:, None]
    x = (np.arange(128) % 64)[None, :]
    phase = 2.0 * np.pi * (r * x) / 1024.0
    twiddle = jnp.asarray(np.concatenate([np.cos(phase), np.sin(phase)]).astype(np.float32))
    q = np.arange(64)
    phase = 2.0 * np.pi * (np.outer(q, q) % 64) / 64.0
    return (twiddle, *pieces(np.concatenate([np.cos(phase), np.sin(phase)])))


def y_tables():
    s = np.arange(256)
    a = 16 * (s % 16) + s // 16
    k = np.arange(256)
    phase = 2.0 * np.pi * (np.outer(a, k) % 256) / 256.0
    waves = pieces(np.concatenate([np.cos(phase), np.sin(phase)], axis=1))
    phase = 2.0 * np.pi * np.outer(np.arange(4), k) / 1024.0
    twiddle = np.concatenate([np.cos(phase), np.sin(phase)]).astype(np.float32)
    return (*waves, jnp.asarray(twiddle))


def f32(*shape):
    return jax.ShapeDtypeStruct(shape, jnp.float32)


def vmem(n):
    return [pl.BlockSpec(memory_space=pltpu.VMEM)] * n


def shards(polar, azimuth, grains, stiffness, anisotropy, axis_polar, axis_azimuth, applied_field):
    count_x = lax.axis_size("gx")
    count_y = lax.axis_size("gy")
    forward_x = [(i, (i + 1) % count_x) for i in range(count_x)]
    backward_x = [(t, s) for s, t in forward_x]
    forward_y = [(i, (i + 1) % count_y) for i in range(count_y)]
    backward_y = [(t, s) for s, t in forward_y]
    fields = (polar, azimuth, grains)
    low_edge = jnp.concatenate([f[:, :128].astype(jnp.float32) for f in fields], axis=0)
    high_edge = jnp.concatenate(
        [f[:, COLS - 128 :].astype(jnp.float32) for f in fields], axis=0
    )
    from_high = lax.ppermute(low_edge, "gy", backward_y)
    from_low = lax.ppermute(high_edge, "gy", forward_y)
    lane = lax.broadcasted_iota(jnp.int32, (3 * WX, 128), 1)
    halo_y = jnp.where(lane < 64, from_high, from_low)

    def edge(start):
        return jnp.concatenate(
            [
                jnp.concatenate(
                    [
                        f[start : start + 8].astype(jnp.float32),
                        halo_y[i * WX + start : i * WX + start + 8],
                    ],
                    axis=1,
                )
                for i, f in enumerate(fields)
            ],
            axis=0,
        )

    halo_xh = lax.ppermute(edge(0), "gx", backward_x)
    halo_xl = lax.ppermute(edge(WX - 8), "gx", forward_x)
    tables = jnp.stack(
        [
            stiffness,
            anisotropy,
            jnp.sin(axis_polar) * jnp.cos(axis_azimuth),
            jnp.sin(axis_polar) * jnp.sin(axis_azimuth),
            jnp.cos(axis_polar),
        ],
        axis=0,
    )
    wide = pltpu.VMEM((ROWS, LANES), jnp.float32)
    triple = pltpu.VMEM((3, ROWS, LANES), jnp.float32)
    in_specs = vmem(7) + [pl.BlockSpec(memory_space=pltpu.SMEM)] + vmem(1)
    moment, payload = pl.pallas_call(
        llg_kernel,
        out_shape=(f32(3, WX, COLS), f32(128, 128)),
        in_specs=in_specs,
        out_specs=tuple(vmem(2)),
        scratch_shapes=[wide] * 3 + [triple] * 2 + [wide] * 9,
        compiler_params=pltpu.CompilerParams(vmem_limit_bytes=32 << 20),
        name="llg",
    )(polar, azimuth, grains, halo_y, halo_xh, halo_xl, tables, applied_field, sum_matrix())

    columns = lax.all_to_all(
        payload.reshape(16, 8, 128), "gx", split_axis=0, concat_axis=0, tiled=True
    ).reshape(128, 128)
    rows = pl.pallas_call(
        x_kernel,
        out_shape=f32(256, 128),
        in_specs=vmem(4),
        out_specs=vmem(1)[0],
        name="along_x",
    )(columns, *x_tables())
    mine = lax.all_to_all(
        rows.reshape(256, 1, 128), ("gx", "gy"), split_axis=0, concat_axis=0, tiled=True
    ).reshape(256, 128)
    first_row = (lax.axis_index("gx") * WX + lax.axis_index("gy") * 4).astype(jnp.int32)
    spin_flip, non_flip = pl.pallas_call(
        y_kernel,
        out_shape=(f32(4, 1024), f32(4, 1024)),
        in_specs=[pl.BlockSpec(memory_space=pltpu.SMEM)] + vmem(4),
        out_specs=tuple(vmem(2)),
        scratch_shapes=[pltpu.VMEM((2, 128, 128), jnp.float32)],
        name="along_y",
    )(first_row.reshape(1), mine, *y_tables())
    return (moment, spin_flip, non_flip)


def solution(mesh):
    in_specs = (P("gx", "gy"), P("gx", "gy"), P("gx", "gy"), P(), P(), P(), P(), P())
    out_specs = (P(None, "gx", "gy"), P(("gx", "gy"), None), P(("gx", "gy"), None))
    return jax.shard_map(shards, mesh=mesh, in_specs=in_specs, out_specs=out_specs, check_vma=False)
```

```python
import math

import jax
import jax.numpy as jnp
import numpy as np
from jax import lax
from jax.experimental import pallas as pl
from jax.experimental.pallas import tpu as pltpu
from jax.sharding import PartitionSpec as P

NZ = 12
STEPS = 4
DAMPING = 0.5
TIME_STEP = 0.12
GAIN = TIME_STEP / (1.0 + DAMPING * DAMPING)

WX = 64
WY = 64
COLS = WY * NZ
LANES = COLS + 128
ROWS = WX + 8
STRIPS = ROWS // 8
NGRAIN = 256

COS_POLY = (
    1.0,
    -0.5,
    0.0416666641831398,
    -0.0013888862449675798,
    2.4800550818326883e-05,
    -2.753476167072222e-07,
    2.060329462594268e-09,
    -9.721622812319808e-12,
)
SIN_POLY = (
    1.0,
    -0.1666666567325592,
    0.008333321660757065,
    -0.00019840530876535922,
    2.7535795652511297e-06,
    -2.472832427713456e-08,
    1.361144114087054e-10,
)


def poly(coefs, t):
    acc = coefs[-1] * t + coefs[-2]
    for c in coefs[-3::-1]:
        acc = acc * t + c
    return acc


def sincos(x):
    t = x * x
    return x * poly(SIN_POLY, t), poly(COS_POLY, t)


def split(x):
    hi = x.astype(jnp.bfloat16)
    lo = (x - hi.astype(jnp.float32)).astype(jnp.bfloat16)
    return hi, lo


def mm(a, b):
    return jnp.dot(a, b, preferred_element_type=jnp.float32)


def iota(shape, dim):
    return lax.broadcasted_iota(jnp.int32, shape, dim)


def strip(ref, s, *lead):
    return ref[(*lead, pl.ds(pl.multiple_of(s * 8, 8), 8), slice(None))]


def put(ref, s, value, *lead):
    ref[(*lead, pl.ds(pl.multiple_of(s * 8, 8), 8), slice(None))] = value


def up(cur, following):
    return pltpu.roll(jnp.where(iota(cur.shape, 0) == 0, following, cur), 7, 0)


def down(cur, previous):
    return pltpu.roll(jnp.where(iota(cur.shape, 0) == 7, previous, cur), 1, 0)


def grain_tables(rows):
    return [
        [jnp.broadcast_to(row[:, h * 128 : h * 128 + 128], (8, 128)) for h in range(2)]
        for row in rows
    ]


def look_up(pair, labels):
    low = labels & 127
    first = labels < 128
    parts = []
    for t in range(labels.shape[1] // 128):
        sl = slice(128 * t, 128 * t + 128)
        a = jnp.take_along_axis(pair[0], low[:, sl], axis=1, mode="promise_in_bounds")
        b = jnp.take_along_axis(pair[1], low[:, sl], axis=1, mode="promise_in_bounds")
        parts.append(jnp.where(first[:, sl], a, b))
    return jnp.concatenate(parts, axis=1)


def start_cells(polar, azimuth):
    sp, cp = sincos(polar)
    sa, ca = sincos(azimuth)
    return sp * ca, sp * sa, cp


def couple(p, q):
    return (2.0 * GAIN) * p * q / (p + q)


def edges_kernel(p_low, a_low, g_low, p_high, a_high, g_high, low, high):
    for dst, refs in ((low, (p_low, a_low, g_low)), (high, (p_high, a_high, g_high))):
        for i, ref in enumerate(refs):
            dst[i * WX : (i + 1) * WX, :] = ref[...].astype(jnp.float32)


def cells_kernel(
    polar, azimuth, grains, stiffness, anisotropy, axis_polar, axis_azimuth, cells, props, tables
):
    ax, ay, az = start_cells(axis_polar[...], axis_azimuth[...])
    rows = [stiffness[...], GAIN * anisotropy[...], ax, ay, az]
    for r, row in enumerate(rows):
        tables[r : r + 1, :] = row
    tabs = grain_tables(rows)

    def body(s, carry):
        start = start_cells(strip(polar, s), strip(azimuth, s))
        for c in range(3):
            put(cells, s, start[c], c)
        labels = strip(grains, s)
        for r in range(5):
            put(props, s, look_up(tabs[r], labels), r)
        return carry

    lax.fori_loop(0, WX // 8, body, 0, unroll=2)


def steps_kernel(
    cells, props, halo_y, halo_xh, halo_xl, tables, applied, sum_z,
    moment, payload,
    m0, m1, wt, cxu, cxd, cyu, cyd, czu, czd, ks, ux, uy, uz,
):
    tabs = grain_tables([tables[r : r + 1, :] for r in range(5)])
    for c in range(3):
        m0[c, 0:WX, 0:COLS] = cells[c]
    for r, ref in enumerate((wt, ks, ux, uy, uz)):
        ref[0:WX, 0:COLS] = props[r]

    def fill(rows, cols, polar, azimuth, labels):
        start = start_cells(polar, azimuth)
        for c in range(3):
            m0[c, rows, cols] = start[c]
        labels = labels.astype(jnp.int32)
        for r, ref in enumerate((wt, ks, ux, uy, uz)):
            ref[rows, cols] = look_up(tabs[r], labels)

    def side(s, carry):
        rows = pl.ds(pl.multiple_of(s * 8, 8), 8)
        fill(rows, slice(COLS, LANES), *(strip(halo_y, s + i * (WX // 8)) for i in range(3)))
        return carry

    lax.fori_loop(0, WX // 8, side, 0, unroll=4)
    upper = iota((8, LANES), 0) < 4
    fill(
        slice(WX, ROWS),
        slice(0, LANES),
        *(
            jnp.where(upper, halo_xh[8 * i : 8 * i + 8, :], halo_xl[8 * i : 8 * i + 8, :])
            for i in range(3)
        ),
    )

    def nxt(s):
        return jnp.where(s == STRIPS - 1, 0, s + 1)

    def prv(s):
        return jnp.where(s == 0, STRIPS - 1, s - 1)

    def couplings(s, carry):
        w = strip(wt, s)
        put(cxu, s, couple(w, up(w, strip(wt, nxt(s)))))
        put(cxd, s, couple(w, down(w, strip(wt, prv(s)))))
        y = couple(w, pltpu.roll(w, LANES - NZ, 1))
        put(cyu, s, y)
        put(cyd, s, pltpu.roll(y, NZ, 1))
        lane = iota(w.shape, 1)
        depth = jnp.where(lane < COLS + 64, lane, lane - LANES + 6 * NZ + COLS) % NZ
        z = jnp.where(depth != NZ - 1, couple(w, pltpu.roll(w, LANES - 1, 1)), 0.0)
        put(czu, s, z)
        put(czd, s, pltpu.roll(z, 1, 1))
        return carry

    lax.fori_loop(0, STRIPS, couplings, 0, unroll=3)
    field = [GAIN * applied[c] for c in range(3)]

    def step(src, dst, s):
        after, before = nxt(s), prv(s)
        m = [strip(src, s, c) for c in range(3)]
        u = [strip(r, s) for r in (ux, uy, uz)]
        xu, xd, yu, yd, zu, zd = (strip(r, s) for r in (cxu, cxd, cyu, cyd, czu, czd))
        proj = strip(ks, s) * (u[0] * m[0] + u[1] * m[1] + u[2] * m[2])
        h = []
        for c in range(3):
            f = yu * (pltpu.roll(m[c], LANES - NZ, 1) - m[c])
            f = f + yd * (pltpu.roll(m[c], NZ, 1) - m[c])
            f = f + zu * (pltpu.roll(m[c], LANES - 1, 1) - m[c])
            f = f + zd * (pltpu.roll(m[c], 1, 1) - m[c])
            f = f + xu * (up(m[c], strip(src, after, c)) - m[c])
            f = f + xd * (down(m[c], strip(src, before, c)) - m[c])
            h.append(f + proj * u[c] + field[c])
        t = cross(m, h)
        d = cross(m, t)
        v = [m[c] - (t[c] + DAMPING * d[c]) for c in range(3)]
        r = lax.rsqrt(v[0] * v[0] + v[1] * v[1] + v[2] * v[2])
        for c in range(3):
            put(dst, s, v[c] * r, c)

    def one(src, dst, count, unroll):
        def body(s, carry):
            step(src, dst, s)
            return carry

        lax.fori_loop(0, count, body, 0, unroll=unroll)

    one(m0, m1, STRIPS, 3)
    one(m1, m0, STRIPS, 3)
    one(m0, m1, STRIPS, 3)
    one(m1, m0, STRIPS - 1, 4)

    for c in range(3):
        moment[c] = m0[c, 0:WX, 0:COLS]

    m = jnp.concatenate([m0[c, 0:WX, 0:COLS] for c in range(3)], axis=0)
    hi, lo = split(m)
    out = mm(hi, sum_z[...]) + mm(lo, sum_z[...])
    block = iota((16, 128), 1) // 32
    for half in range(2):
        for c in range(3):
            rows = [
                out[c * WX + 16 * g : c * WX + 16 * g + 16, half * 128 : half * 128 + 128]
                for g in range(4)
            ]
            merged = rows[3]
            for g in range(3):
                merged = jnp.where(block == (g + c) % 4, rows[g], merged)
            for peer in range(half, 16, 2):
                payload[peer * 48 + 16 * c : peer * 48 + 16 * c + 16, :] = merged


def cross(first, second):
    return [
        first[1] * second[2] - first[2] * second[1],
        first[2] * second[0] - first[0] * second[2],
        first[0] * second[1] - first[1] * second[0],
    ]


def x_kernel(pair, got, waves_hi, waves_lo, out, d_hi, d_lo):
    turn = (pair[0] * iota((8, 128), 0) + 4) % 8 - 4
    sine, cosine = sincos(turn.astype(jnp.float32) * (math.pi / 4.0))
    sine = jnp.concatenate([sine] * 2, axis=0)
    cosine = jnp.concatenate([cosine] * 2, axis=0)
    block = iota((16, 128), 1) // 32

    def unpack(source, carry):
        parts = []
        for c in range(3):
            start = pl.multiple_of(source * 48 + 16 * c, 16)
            parts.append(got[pl.ds(start, 16), :])
        for g in range(4):
            d = jnp.where(
                block == g, parts[0], jnp.where(block == (g + 1) % 4, parts[1], parts[2])
            )
            if g:
                d = pltpu.roll(d, 128 - 32 * g, 1)
            start = pl.multiple_of(source * 64 + 16 * g, 16)
            for i, factor in enumerate((cosine, sine)):
                hi, lo = split(d * factor)
                d_hi[pl.ds(start, 16), 128 * i : 128 * i + 128] = hi
                d_lo[pl.ds(start, 16), 128 * i : 128 * i + 128] = lo
        return carry

    lax.fori_loop(0, 16, unpack, 0, unroll=2)
    both = mm(waves_hi[...], d_hi[...]) + (
        mm(waves_hi[...], d_lo[...]) + mm(waves_lo[...], d_hi[...])
    )
    sign = jnp.where(iota((8, 128), 0) < 4, 1.0, -1.0)
    for t in range(32):
        rows = slice(8 * t, 8 * t + 8)
        out[rows, :] = both[rows, 0:128] + sign * pltpu.roll(both[rows, 128:256], 4, 0)


def y_kernel(
    first_row, got, waves_hi, waves_lo, twiddle, last_hi, last_lo,
    spin_flip, non_flip, flat, placed,
):
    parts = []
    for ri in range(2):
        rows = [got[pl.ds(4 * ri + low, 32, stride=8), :] for low in range(4)]
        hi, lo = split(jnp.concatenate(rows, axis=0).T[0:96, :])
        parts.append(
            mm(hi, waves_hi[...]) + (mm(lo, waves_hi[...]) + mm(hi, waves_lo[...]))
        )
    re = parts[0][:, 0:128] + parts[1][:, 128:256]
    im = parts[1][:, 0:128] - parts[0][:, 128:256]
    cosine, sine = twiddle[0:32, :], twiddle[32:64, :]
    turned = []
    for c in range(3):
        r, i = re[32 * c : 32 * c + 32, :], im[32 * c : 32 * c + 32, :]
        turned.append(
            jnp.concatenate([r * cosine + i * sine, i * cosine - r * sine], axis=0)
        )
    hi, lo = split(jnp.concatenate(turned, axis=1))
    full = mm(last_hi[...], hi) + (mm(last_hi[...], lo) + mm(last_lo[...], hi))
    lane = iota((32, 128), 1)
    kx = first_row[0] + lane // 32
    ky = iota((32, 128), 0) * 32 + lane % 32
    wave_x = jnp.where(kx < 512, kx, kx - 1024).astype(jnp.float32)
    wave_y = jnp.where(ky < 512, ky, ky - 1024).astype(jnp.float32)
    squared = wave_x * wave_x + wave_y * wave_y
    inverse = lax.rsqrt(jnp.maximum(squared, 1.0))
    unit_x = wave_x * inverse
    unit_y = wave_y * inverse
    stop = jnp.where(squared > 0.5, 1.0 / (NZ * 1024.0 * 1024.0), 0.0)
    nf = sf = 0.0
    for ri in range(2):
        sx, sy, sz = (full[32 * ri : 32 * ri + 32, 128 * c : 128 * c + 128] for c in range(3))
        along = unit_x * sx + unit_y * sy
        px = sx - unit_x * along
        py = sy - unit_y * along
        nf = nf + px * px
        sf = sf + (py * py + sz * sz)
    block = iota((8, 128), 1) // 32
    for value, dst in ((sf, spin_flip), (nf, non_flip)):
        flat[...] = value * stop
        for low in range(4):
            row = None
            for u in range(4):
                piece = flat[pl.ds(u, 8, stride=4), :]
                if u != low:
                    piece = pltpu.roll(piece, (u - low) % 4 * 32, 1)
                row = piece if row is None else jnp.where(block == u, piece, row)
            placed[pl.ds(low, 8, stride=4), :] = row
        for t in range(8):
            dst[:, 128 * t : 128 * t + 128] = placed[4 * t : 4 * t + 4, :]


def pieces(x):
    hi = x.astype(jnp.bfloat16)
    lo = (x - hi.astype(np.float64)).astype(jnp.bfloat16)
    return jnp.asarray(hi), jnp.asarray(lo)


def sum_matrix():
    y = np.arange(COLS) // NZ
    col = np.arange(256)
    return jnp.asarray(
        (y[:, None] == (col // 128 * 32 + col % 32)[None, :]).astype(jnp.bfloat16)
    )


def x_tables():
    row = np.arange(256)
    k = row // 8 * 4 + row % 4
    phase = 2.0 * np.pi * (np.outer(k, np.arange(1024)) % 1024) / 1024.0
    real = (row % 8 < 4)[:, None]
    return pieces(np.where(real, np.cos(phase), -np.sin(phase)))


def y_tables():
    lane = np.arange(128)
    block = 2 * (lane % 16) + lane % 32 // 16
    k = np.arange(128)
    phase = 2.0 * np.pi * (np.outer(block, k % 32) % 32) / 32.0
    same = (lane // 32)[:, None] == (k // 32)[None, :]
    waves = pieces(
        np.concatenate([np.where(same, np.cos(phase), 0.0), np.where(same, np.sin(phase), 0.0)], axis=1)
    )
    q = np.arange(32)
    phase = 2.0 * np.pi * np.outer(q, k % 32) / 1024.0
    twiddle = np.concatenate([np.cos(phase), np.sin(phase)]).astype(np.float32)
    phase = 2.0 * np.pi * (np.outer(q, q) % 32) / 32.0
    c, s = np.cos(phase), np.sin(phase)
    return (*waves, jnp.asarray(twiddle), *pieces(np.block([[c, s], [-s, c]])))


def f32(*shape):
    return jax.ShapeDtypeStruct(shape, jnp.float32)


def vmem(n):
    return [pl.BlockSpec(memory_space=pltpu.VMEM)] * n


def shards(polar, azimuth, grains, stiffness, anisotropy, axis_polar, axis_azimuth, applied_field):
    count_x = lax.axis_size("gx")
    count_y = lax.axis_size("gy")
    forward_x = [(i, (i + 1) % count_x) for i in range(count_x)]
    backward_x = [(t, s) for s, t in forward_x]
    forward_y = [(i, (i + 1) % count_y) for i in range(count_y)]
    backward_y = [(t, s) for s, t in forward_y]
    fields = (polar, azimuth, grains)
    first = pl.BlockSpec((WX, 128), lambda i: (0, 0))
    last = pl.BlockSpec((WX, 128), lambda i: (0, COLS // 128 - 1))
    low_edge, high_edge = pl.pallas_call(
        edges_kernel,
        grid=(1,),
        out_shape=(f32(3 * WX, 128), f32(3 * WX, 128)),
        in_specs=[first] * 3 + [last] * 3,
        out_specs=(pl.BlockSpec((3 * WX, 128), lambda i: (0, 0)),) * 2,
        name="edges",
    )(*fields, *fields)
    from_high = lax.ppermute(low_edge, "gy", backward_y)
    from_low = lax.ppermute(high_edge, "gy", forward_y)
    lane = lax.broadcasted_iota(jnp.int32, (3 * WX, 128), 1)
    halo_y = jnp.where(lane < 64, from_high, from_low)

    def edge(start):
        return jnp.concatenate(
            [
                jnp.concatenate(
                    [
                        f[start : start + 8].astype(jnp.float32),
                        halo_y[i * WX + start : i * WX + start + 8],
                    ],
                    axis=1,
                )
                for i, f in enumerate(fields)
            ],
            axis=0,
        )

    halo_xh = lax.ppermute(edge(0), "gx", backward_x)
    halo_xl = lax.ppermute(edge(WX - 8), "gx", forward_x)
    per_grain = [
        v.reshape(1, NGRAIN) for v in (stiffness, anisotropy, axis_polar, axis_azimuth)
    ]
    params = pltpu.CompilerParams(vmem_limit_bytes=32 << 20)
    cells, props, tables = pl.pallas_call(
        cells_kernel,
        out_shape=(f32(3, WX, COLS), f32(5, WX, COLS), f32(8, NGRAIN)),
        in_specs=vmem(7),
        out_specs=tuple(vmem(3)),
        compiler_params=params,
        name="cells",
    )(*fields, *per_grain)
    moment, payload = pl.pallas_call(
        steps_kernel,
        out_shape=(f32(3, WX, COLS), f32(16 * 48, 128)),
        in_specs=vmem(6) + [pl.BlockSpec(memory_space=pltpu.SMEM)] + vmem(1),
        out_specs=tuple(vmem(2)),
        scratch_shapes=[pltpu.VMEM((3, ROWS, LANES), jnp.float32)] * 2
        + [pltpu.VMEM((ROWS, LANES), jnp.float32)] * 11,
        compiler_params=params,
        name="steps",
    )(cells, props, halo_y, halo_xh, halo_xl, tables, applied_field, sum_matrix())

    columns = lax.all_to_all(
        payload.reshape(16, 48, 128), "gx", split_axis=0, concat_axis=0, tiled=True
    ).reshape(16 * 48, 128)
    at_x = lax.axis_index("gx").astype(jnp.int32)
    at_y = lax.axis_index("gy").astype(jnp.int32)
    smem = [pl.BlockSpec(memory_space=pltpu.SMEM)]
    rows = pl.pallas_call(
        x_kernel,
        out_shape=f32(256, 128),
        in_specs=smem + vmem(3),
        out_specs=vmem(1)[0],
        scratch_shapes=[pltpu.VMEM((1024, 256), jnp.bfloat16)] * 2,
        compiler_params=params,
        name="along_x",
    )((at_x // 2).reshape(1), columns, *x_tables())
    groups = [
        [gx * 16 + gy for gx in (base, base + 1) for gy in range(16)] for base in range(0, 16, 2)
    ]
    mine = lax.all_to_all(
        rows.reshape(32, 8, 128), ("gx", "gy"), split_axis=0, concat_axis=0, tiled=True,
        axis_index_groups=groups,
    ).reshape(256, 128)
    spin_flip, non_flip = pl.pallas_call(
        y_kernel,
        out_shape=(f32(4, 1024), f32(4, 1024)),
        in_specs=smem + vmem(6),
        out_specs=tuple(vmem(2)),
        scratch_shapes=[pltpu.VMEM((32, 128), jnp.float32)] * 2,
        name="along_y",
    )((at_x * WX + at_y * 4).reshape(1), mine, *y_tables())
    return (moment, spin_flip, non_flip)


def solution(mesh):
    in_specs = (P("gx", "gy"), P("gx", "gy"), P("gx", "gy"), P(), P(), P(), P(), P())
    out_specs = (P(None, "gx", "gy"), P(("gx", "gy"), None), P(("gx", "gy"), None))
    return jax.shard_map(shards, mesh=mesh, in_specs=in_specs, out_specs=out_specs, check_vma=False)
```

```python
import math

import jax
import jax.numpy as jnp
import numpy as np
from jax import lax
from jax.experimental import pallas as pl
from jax.experimental.pallas import tpu as pltpu
from jax.sharding import PartitionSpec as P

NZ = 12
STEPS = 4
DAMPING = 0.5
TIME_STEP = 0.12
GAIN = TIME_STEP / (1.0 + DAMPING * DAMPING)

WX = 64
WY = 64
COLS = WY * NZ
LANES = COLS + 128
ROWS = WX + 8
STRIPS = ROWS // 8
NGRAIN = 256

COS_POLY = (
    1.0,
    -0.5,
    0.0416666641831398,
    -0.0013888862449675798,
    2.4800550818326883e-05,
    -2.753476167072222e-07,
    2.060329462594268e-09,
    -9.721622812319808e-12,
)
SIN_POLY = (
    1.0,
    -0.1666666567325592,
    0.008333321660757065,
    -0.00019840530876535922,
    2.7535795652511297e-06,
    -2.472832427713456e-08,
    1.361144114087054e-10,
)


def poly(coefs, t):
    acc = coefs[-1] * t + coefs[-2]
    for c in coefs[-3::-1]:
        acc = acc * t + c
    return acc


def sincos(x):
    t = x * x
    return x * poly(SIN_POLY, t), poly(COS_POLY, t)


def split(x):
    hi = x.astype(jnp.bfloat16)
    lo = (x - hi.astype(jnp.float32)).astype(jnp.bfloat16)
    return hi, lo


def mm(a, b):
    return jnp.dot(a, b, preferred_element_type=jnp.float32)


def iota(shape, dim):
    return lax.broadcasted_iota(jnp.int32, shape, dim)


def strip(ref, s, *lead):
    return ref[(*lead, pl.ds(pl.multiple_of(s * 8, 8), 8), slice(None))]


def put(ref, s, value, *lead):
    ref[(*lead, pl.ds(pl.multiple_of(s * 8, 8), 8), slice(None))] = value


def up(cur, following):
    return pltpu.roll(jnp.where(iota(cur.shape, 0) == 0, following, cur), 7, 0)


def down(cur, previous):
    return pltpu.roll(jnp.where(iota(cur.shape, 0) == 7, previous, cur), 1, 0)


def grain_tables(rows):
    return [
        [jnp.broadcast_to(row[:, h * 128 : h * 128 + 128], (8, 128)) for h in range(2)]
        for row in rows
    ]


def look_up(pair, labels):
    low = labels & 127
    first = labels < 128
    parts = []
    for t in range(labels.shape[1] // 128):
        sl = slice(128 * t, 128 * t + 128)
        a = jnp.take_along_axis(pair[0], low[:, sl], axis=1, mode="promise_in_bounds")
        b = jnp.take_along_axis(pair[1], low[:, sl], axis=1, mode="promise_in_bounds")
        parts.append(jnp.where(first[:, sl], a, b))
    return jnp.concatenate(parts, axis=1)


def start_cells(polar, azimuth):
    sp, cp = sincos(polar)
    sa, ca = sincos(azimuth)
    return sp * ca, sp * sa, cp


def couple(p, q):
    return (2.0 * GAIN) * p * q / (p + q)


def edges_kernel(p_low, a_low, g_low, p_high, a_high, g_high, low, high):
    half = WX // 2
    lane = iota((half, 128), 1)
    for i, src in enumerate((p_low, a_low, g_low)):
        v = src[...].astype(jnp.float32)
        low[i * half : (i + 1) * half, :] = jnp.where(
            lane < 48, v[0:half, :], pltpu.roll(v[half:WX, :], 48, 1)
        )
    for i, src in enumerate((p_high, a_high, g_high)):
        v = src[...].astype(jnp.float32)
        high[i * half : (i + 1) * half, :] = jnp.where(
            lane >= 80, v[0:half, :], pltpu.roll(v[half:WX, :], 80, 1)
        )


def cells_kernel(
    polar, azimuth, grains, stiffness, anisotropy, axis_polar, axis_azimuth, applied,
    cells, props, tables,
):
    ax, ay, az = start_cells(axis_polar[...], axis_azimuth[...])
    rows = [stiffness[...], GAIN * anisotropy[...], ax, ay, az]
    for r, row in enumerate(rows):
        tables[r : r + 1, :] = row
    for c in range(3):
        tables[5 + c : 6 + c, :] = jnp.full((1, NGRAIN), GAIN * applied[c])
    tabs = grain_tables(rows)

    def body(s, carry):
        start = start_cells(strip(polar, s), strip(azimuth, s))
        for c in range(3):
            put(cells, s, start[c], c)
        labels = strip(grains, s)
        for r in range(5):
            put(props, s, look_up(tabs[r], labels), r)
        return carry

    lax.fori_loop(0, WX // 8, body, 0, unroll=2)


def steps_kernel(
    cells, props, from_high, from_low, halo_xh, halo_xl, tables, sum_z,
    moment, payload,
    m0, m1, wt, cxu, cxd, cyu, cyd, czu, czd, ks, ux, uy, uz, raw,
):
    tabs = grain_tables([tables[r : r + 1, :] for r in range(5)])
    for c in range(3):
        m0[c, 0:WX, 0:COLS] = cells[c]
    for r, ref in enumerate((wt, ks, ux, uy, uz)):
        ref[0:WX, 0:COLS] = props[r]

    def fill(rows, cols, polar, azimuth, labels):
        start = start_cells(polar, azimuth)
        for c in range(3):
            m0[c, rows, cols] = start[c]
        labels = labels.astype(jnp.int32)
        for r, ref in enumerate((wt, ks, ux, uy, uz)):
            ref[rows, cols] = look_up(tabs[r], labels)

    near = iota((8, 128), 1) < 64

    def side(bottom):
        def body(s, carry):
            values = []
            for i in range(3):
                high = strip(from_high, s + i * (WX // 16))
                low = strip(from_low, s + i * (WX // 16))
                if bottom:
                    high, low = pltpu.roll(high, 80, 1), pltpu.roll(low, 48, 1)
                values.append(jnp.where(near, high, low))
            start = s + (WX // 16 if bottom else 0)
            rows = pl.ds(pl.multiple_of(start * 8, 8), 8)
            fill(rows, slice(COLS, LANES), *values)
            return carry

        lax.fori_loop(0, WX // 16, body, 0, unroll=4)

    side(False)
    side(True)
    for i in range(3):
        raw[i, 0:4, :] = halo_xh[i]
        raw[i, 4:8, :] = halo_xl[i]
    fill(slice(WX, ROWS), slice(0, LANES), raw[0], raw[1], raw[2])

    def nxt(s):
        return jnp.where(s == STRIPS - 1, 0, s + 1)

    def prv(s):
        return jnp.where(s == 0, STRIPS - 1, s - 1)

    def couplings(s, carry):
        w = strip(wt, s)
        put(cxu, s, couple(w, up(w, strip(wt, nxt(s)))))
        put(cxd, s, couple(w, down(w, strip(wt, prv(s)))))
        y = couple(w, pltpu.roll(w, LANES - NZ, 1))
        put(cyu, s, y)
        put(cyd, s, pltpu.roll(y, NZ, 1))
        lane = iota(w.shape, 1)
        depth = jnp.where(lane < COLS + 64, lane, lane - LANES + 6 * NZ + COLS) % NZ
        z = jnp.where(depth != NZ - 1, couple(w, pltpu.roll(w, LANES - 1, 1)), 0.0)
        put(czu, s, z)
        put(czd, s, pltpu.roll(z, 1, 1))
        return carry

    lax.fori_loop(0, STRIPS, couplings, 0, unroll=3)
    field = [jnp.broadcast_to(tables[5 + c : 6 + c, 0:1], (8, LANES)) for c in range(3)]

    def step(src, dst, s):
        after, before = nxt(s), prv(s)
        m = [strip(src, s, c) for c in range(3)]
        u = [strip(r, s) for r in (ux, uy, uz)]
        xu, xd, yu, yd, zu, zd = (strip(r, s) for r in (cxu, cxd, cyu, cyd, czu, czd))
        proj = strip(ks, s) * (u[0] * m[0] + u[1] * m[1] + u[2] * m[2])
        h = []
        for c in range(3):
            f = yu * (pltpu.roll(m[c], LANES - NZ, 1) - m[c])
            f = f + yd * (pltpu.roll(m[c], NZ, 1) - m[c])
            f = f + zu * (pltpu.roll(m[c], LANES - 1, 1) - m[c])
            f = f + zd * (pltpu.roll(m[c], 1, 1) - m[c])
            f = f + xu * (up(m[c], strip(src, after, c)) - m[c])
            f = f + xd * (down(m[c], strip(src, before, c)) - m[c])
            h.append(f + proj * u[c] + field[c])
        t = cross(m, h)
        d = cross(m, t)
        v = [m[c] - (t[c] + DAMPING * d[c]) for c in range(3)]
        r = lax.rsqrt(v[0] * v[0] + v[1] * v[1] + v[2] * v[2])
        for c in range(3):
            put(dst, s, v[c] * r, c)

    def one(src, dst, count, unroll):
        def body(s, carry):
            step(src, dst, s)
            return carry

        lax.fori_loop(0, count, body, 0, unroll=unroll)

    one(m0, m1, STRIPS, 3)
    one(m1, m0, STRIPS, 3)
    one(m0, m1, STRIPS, 3)
    one(m1, m0, STRIPS - 1, 4)

    for c in range(3):
        moment[c] = m0[c, 0:WX, 0:COLS]

    m = jnp.concatenate([m0[c, 0:WX, 0:COLS] for c in range(3)], axis=0)
    hi, lo = split(m)
    out = mm(hi, sum_z[...]) + mm(lo, sum_z[...])
    block = iota((16, 128), 1) // 32
    for half in range(2):
        for c in range(3):
            rows = [
                out[c * WX + 16 * g : c * WX + 16 * g + 16, half * 128 : half * 128 + 128]
                for g in range(4)
            ]
            merged = rows[3]
            for g in range(3):
                merged = jnp.where(block == (g + c) % 4, rows[g], merged)
            for peer in range(half, 16, 2):
                payload[peer * 48 + 16 * c : peer * 48 + 16 * c + 16, :] = merged


def cross(first, second):
    return [
        first[1] * second[2] - first[2] * second[1],
        first[2] * second[0] - first[0] * second[2],
        first[0] * second[1] - first[1] * second[0],
    ]


def x_kernel(pair, got, waves_hi, waves_lo, out, d_hi, d_lo):
    turn = (pair[0] * iota((8, 128), 0) + 4) % 8 - 4
    sine, cosine = sincos(turn.astype(jnp.float32) * (math.pi / 4.0))
    sine = jnp.concatenate([sine] * 2, axis=0)
    cosine = jnp.concatenate([cosine] * 2, axis=0)
    block = iota((16, 128), 1) // 32

    def unpack(source, carry):
        parts = []
        for c in range(3):
            start = pl.multiple_of(source * 48 + 16 * c, 16)
            parts.append(got[pl.ds(start, 16), :])
        for g in range(4):
            d = jnp.where(
                block == g, parts[0], jnp.where(block == (g + 1) % 4, parts[1], parts[2])
            )
            if g:
                d = pltpu.roll(d, 128 - 32 * g, 1)
            start = pl.multiple_of(source * 64 + 16 * g, 16)
            for i, factor in enumerate((cosine, sine)):
                hi, lo = split(d * factor)
                d_hi[pl.ds(start, 16), 128 * i : 128 * i + 128] = hi
                d_lo[pl.ds(start, 16), 128 * i : 128 * i + 128] = lo
        return carry

    lax.fori_loop(0, 16, unpack, 0, unroll=2)
    both = mm(waves_hi[...], d_hi[...]) + (
        mm(waves_hi[...], d_lo[...]) + mm(waves_lo[...], d_hi[...])
    )
    sign = jnp.where(iota((8, 128), 0) < 4, 1.0, -1.0)
    for t in range(32):
        rows = slice(8 * t, 8 * t + 8)
        out[rows, :] = both[rows, 0:128] + sign * pltpu.roll(both[rows, 128:256], 4, 0)


def y_kernel(
    first_row, got, waves_hi, waves_lo, twiddle, last_hi, last_lo,
    spin_flip, non_flip, flat, placed,
):
    parts = []
    for ri in range(2):
        rows = [got[pl.ds(4 * ri + low, 32, stride=8), :] for low in range(4)]
        hi, lo = split(jnp.concatenate(rows, axis=0).T[0:96, :])
        parts.append(
            mm(hi, waves_hi[...]) + (mm(lo, waves_hi[...]) + mm(hi, waves_lo[...]))
        )
    re = parts[0][:, 0:128] + parts[1][:, 128:256]
    im = parts[1][:, 0:128] - parts[0][:, 128:256]
    cosine, sine = twiddle[0:32, :], twiddle[32:64, :]
    turned = []
    for c in range(3):
        r, i = re[32 * c : 32 * c + 32, :], im[32 * c : 32 * c + 32, :]
        turned.append(
            jnp.concatenate([r * cosine + i * sine, i * cosine - r * sine], axis=0)
        )
    hi, lo = split(jnp.concatenate(turned, axis=1))
    full = mm(last_hi[...], hi) + (mm(last_hi[...], lo) + mm(last_lo[...], hi))
    lane = iota((32, 128), 1)
    kx = first_row[0] + lane // 32
    ky = iota((32, 128), 0) * 32 + lane % 32
    wave_x = jnp.where(kx < 512, kx, kx - 1024).astype(jnp.float32)
    wave_y = jnp.where(ky < 512, ky, ky - 1024).astype(jnp.float32)
    squared = wave_x * wave_x + wave_y * wave_y
    inverse = lax.rsqrt(jnp.maximum(squared, 1.0))
    unit_x = wave_x * inverse
    unit_y = wave_y * inverse
    stop = jnp.where(squared > 0.5, 1.0 / (NZ * 1024.0 * 1024.0), 0.0)
    nf = sf = 0.0
    for ri in range(2):
        sx, sy, sz = (full[32 * ri : 32 * ri + 32, 128 * c : 128 * c + 128] for c in range(3))
        along = unit_x * sx + unit_y * sy
        px = sx - unit_x * along
        py = sy - unit_y * along
        nf = nf + px * px
        sf = sf + (py * py + sz * sz)
    block = iota((8, 128), 1) // 32
    for value, dst in ((sf, spin_flip), (nf, non_flip)):
        flat[...] = value * stop
        for low in range(4):
            row = None
            for u in range(4):
                piece = flat[pl.ds(u, 8, stride=4), :]
                if u != low:
                    piece = pltpu.roll(piece, (u - low) % 4 * 32, 1)
                row = piece if row is None else jnp.where(block == u, piece, row)
            placed[pl.ds(low, 8, stride=4), :] = row
        for t in range(8):
            dst[:, 128 * t : 128 * t + 128] = placed[4 * t : 4 * t + 4, :]


def pieces(x):
    hi = x.astype(jnp.bfloat16)
    lo = (x - hi.astype(np.float64)).astype(jnp.bfloat16)
    return jnp.asarray(hi), jnp.asarray(lo)


def sum_matrix():
    y = np.arange(COLS) // NZ
    col = np.arange(256)
    return jnp.asarray(
        (y[:, None] == (col // 128 * 32 + col % 32)[None, :]).astype(jnp.bfloat16)
    )


def x_tables():
    row = np.arange(256)
    k = row // 8 * 4 + row % 4
    phase = 2.0 * np.pi * (np.outer(k, np.arange(1024)) % 1024) / 1024.0
    real = (row % 8 < 4)[:, None]
    return pieces(np.where(real, np.cos(phase), -np.sin(phase)))


def y_tables():
    lane = np.arange(128)
    block = 2 * (lane % 16) + lane % 32 // 16
    k = np.arange(128)
    phase = 2.0 * np.pi * (np.outer(block, k % 32) % 32) / 32.0
    same = (lane // 32)[:, None] == (k // 32)[None, :]
    waves = pieces(
        np.concatenate([np.where(same, np.cos(phase), 0.0), np.where(same, np.sin(phase), 0.0)], axis=1)
    )
    q = np.arange(32)
    phase = 2.0 * np.pi * np.outer(q, k % 32) / 1024.0
    twiddle = np.concatenate([np.cos(phase), np.sin(phase)]).astype(np.float32)
    phase = 2.0 * np.pi * (np.outer(q, q) % 32) / 32.0
    c, s = np.cos(phase), np.sin(phase)
    return (*waves, jnp.asarray(twiddle), *pieces(np.block([[c, s], [-s, c]])))


def f32(*shape):
    return jax.ShapeDtypeStruct(shape, jnp.float32)


def vmem(n):
    return [pl.BlockSpec(memory_space=pltpu.VMEM)] * n


def shards(polar, azimuth, grains, stiffness, anisotropy, axis_polar, axis_azimuth, applied_field):
    count_x = lax.axis_size("gx")
    count_y = lax.axis_size("gy")
    forward_x = [(i, (i + 1) % count_x) for i in range(count_x)]
    backward_x = [(t, s) for s, t in forward_x]
    forward_y = [(i, (i + 1) % count_y) for i in range(count_y)]
    backward_y = [(t, s) for s, t in forward_y]
    fields = (polar, azimuth, grains)
    params = pltpu.CompilerParams(vmem_limit_bytes=32 << 20)
    smem = [pl.BlockSpec(memory_space=pltpu.SMEM)]
    first = pl.BlockSpec((WX, 128), lambda i: (0, 0))
    last = pl.BlockSpec((WX, 128), lambda i: (0, COLS // 128 - 1))
    low_edge, high_edge = pl.pallas_call(
        edges_kernel,
        grid=(1,),
        out_shape=(f32(3 * WX // 2, 128), f32(3 * WX // 2, 128)),
        in_specs=[first] * 3 + [last] * 3,
        out_specs=tuple(vmem(2)),
        name="edges",
    )(*fields, *fields)
    from_high = lax.ppermute(low_edge, "gy", backward_y)
    from_low = lax.ppermute(high_edge, "gy", forward_y)

    def edge(start, row, high, low):
        blank = jnp.zeros((4, 32), jnp.float32)
        parts = []
        for i, f in enumerate(fields):
            halo = slice(i * WX // 2 + row, i * WX // 2 + row + 4)
            parts.append(
                jnp.concatenate(
                    [
                        f[start : start + 4].astype(jnp.float32),
                        from_high[halo, high : high + 48],
                        blank,
                        from_low[halo, low : low + 48],
                    ],
                    axis=1,
                )
            )
        return jnp.stack(parts)

    halo_xh = lax.ppermute(edge(0, 0, 0, 80), "gx", backward_x)
    halo_xl = lax.ppermute(edge(WX - 4, WX // 2 - 4, 48, 32), "gx", forward_x)
    per_grain = [
        v.reshape(1, NGRAIN) for v in (stiffness, anisotropy, axis_polar, axis_azimuth)
    ]
    cells, props, tables = pl.pallas_call(
        cells_kernel,
        out_shape=(f32(3, WX, COLS), f32(5, WX, COLS), f32(8, NGRAIN)),
        in_specs=vmem(7) + smem,
        out_specs=tuple(vmem(3)),
        compiler_params=params,
        name="cells",
    )(*fields, *per_grain, applied_field)
    moment, payload = pl.pallas_call(
        steps_kernel,
        out_shape=(f32(3, WX, COLS), f32(16 * 48, 128)),
        in_specs=vmem(8),
        out_specs=tuple(vmem(2)),
        scratch_shapes=[pltpu.VMEM((3, ROWS, LANES), jnp.float32)] * 2
        + [pltpu.VMEM((ROWS, LANES), jnp.float32)] * 11
        + [pltpu.VMEM((3, 8, LANES), jnp.float32)],
        compiler_params=params,
        name="steps",
    )(cells, props, from_high, from_low, halo_xh, halo_xl, tables, sum_matrix())

    columns = lax.all_to_all(
        payload.reshape(16, 48, 128), "gx", split_axis=0, concat_axis=0, tiled=True
    ).reshape(16 * 48, 128)
    at_x = lax.axis_index("gx").astype(jnp.int32)
    at_y = lax.axis_index("gy").astype(jnp.int32)
    rows = pl.pallas_call(
        x_kernel,
        out_shape=f32(256, 128),
        in_specs=smem + vmem(3),
        out_specs=vmem(1)[0],
        scratch_shapes=[pltpu.VMEM((1024, 256), jnp.bfloat16)] * 2,
        compiler_params=params,
        name="along_x",
    )((at_x // 2).reshape(1), columns, *x_tables())
    groups = [
        [gx * 16 + gy for gx in (base, base + 1) for gy in range(16)] for base in range(0, 16, 2)
    ]
    mine = lax.all_to_all(
        rows.reshape(32, 8, 128), ("gx", "gy"), split_axis=0, concat_axis=0, tiled=True,
        axis_index_groups=groups,
    ).reshape(256, 128)
    spin_flip, non_flip = pl.pallas_call(
        y_kernel,
        out_shape=(f32(4, 1024), f32(4, 1024)),
        in_specs=smem + vmem(6),
        out_specs=tuple(vmem(2)),
        scratch_shapes=[pltpu.VMEM((32, 128), jnp.float32)] * 2,
        compiler_params=params,
        name="along_y",
    )((at_x * WX + at_y * 4).reshape(1), mine, *y_tables())
    return (moment, spin_flip, non_flip)


def solution(mesh):
    in_specs = (P("gx", "gy"), P("gx", "gy"), P("gx", "gy"), P(), P(), P(), P(), P())
    out_specs = (P(None, "gx", "gy"), P(("gx", "gy"), None), P(("gx", "gy"), None))
    return jax.shard_map(shards, mesh=mesh, in_specs=in_specs, out_specs=out_specs, check_vma=False)
```

```python
import math

import jax
import jax.numpy as jnp
import numpy as np
from jax import lax
from jax.experimental import pallas as pl
from jax.experimental.pallas import tpu as pltpu
from jax.sharding import PartitionSpec as P

NZ = 12
STEPS = 4
DAMPING = 0.5
TIME_STEP = 0.12
GAIN = TIME_STEP / (1.0 + DAMPING * DAMPING)

WX = 64
WY = 64
COLS = WY * NZ
LANES = COLS + 128
ROWS = WX + 8
STRIPS = ROWS // 8
NGRAIN = 256

COS_POLY = (
    1.0,
    -0.5,
    0.0416666641831398,
    -0.0013888862449675798,
    2.4800550818326883e-05,
    -2.753476167072222e-07,
    2.060329462594268e-09,
    -9.721622812319808e-12,
)
SIN_POLY = (
    1.0,
    -0.1666666567325592,
    0.008333321660757065,
    -0.00019840530876535922,
    2.7535795652511297e-06,
    -2.472832427713456e-08,
    1.361144114087054e-10,
)


def poly(coefs, t):
    acc = coefs[-1] * t + coefs[-2]
    for c in coefs[-3::-1]:
        acc = acc * t + c
    return acc


def sincos(x):
    t = x * x
    return x * poly(SIN_POLY, t), poly(COS_POLY, t)


def split(x):
    hi = x.astype(jnp.bfloat16)
    lo = (x - hi.astype(jnp.float32)).astype(jnp.bfloat16)
    return hi, lo


def mm(a, b):
    return jnp.dot(a, b, preferred_element_type=jnp.float32)


def iota(shape, dim):
    return lax.broadcasted_iota(jnp.int32, shape, dim)


def strip(ref, s, *lead):
    return ref[(*lead, pl.ds(pl.multiple_of(s * 8, 8), 8), slice(None))]


def put(ref, s, value, *lead):
    ref[(*lead, pl.ds(pl.multiple_of(s * 8, 8), 8), slice(None))] = value


def up(cur, following):
    return pltpu.roll(jnp.where(iota(cur.shape, 0) == 0, following, cur), 7, 0)


def down(cur, previous):
    return pltpu.roll(jnp.where(iota(cur.shape, 0) == 7, previous, cur), 1, 0)


def grain_tables(rows):
    return [
        [jnp.broadcast_to(row[:, h * 128 : h * 128 + 128], (8, 128)) for h in range(2)]
        for row in rows
    ]


def look_up(pair, labels):
    low = labels & 127
    first = labels < 128
    parts = []
    for t in range(labels.shape[1] // 128):
        sl = slice(128 * t, 128 * t + 128)
        a = jnp.take_along_axis(pair[0], low[:, sl], axis=1, mode="promise_in_bounds")
        b = jnp.take_along_axis(pair[1], low[:, sl], axis=1, mode="promise_in_bounds")
        parts.append(jnp.where(first[:, sl], a, b))
    return jnp.concatenate(parts, axis=1)


def start_cells(polar, azimuth):
    sp, cp = sincos(polar)
    sa, ca = sincos(azimuth)
    return sp * ca, sp * sa, cp


def couple(p, q):
    return (2.0 * GAIN) * p * q / (p + q)


def edges_kernel(is_even, p_low, a_low, g_low, p_high, a_high, g_high, first, second):
    half = WX // 2
    lane = iota((half, 128), 1)
    even = is_even[0] == 1
    for i, (l, h) in enumerate(((p_low, p_high), (a_low, a_high), (g_low, g_high))):
        l, h = l[...].astype(jnp.float32), h[...].astype(jnp.float32)
        l = jnp.where(lane < 48, l[0:half, :], pltpu.roll(l[half:WX, :], 48, 1))
        h = jnp.where(lane >= 80, h[0:half, :], pltpu.roll(h[half:WX, :], 80, 1))
        first[i * half : (i + 1) * half, :] = jnp.where(even, h, l)
        second[i * half : (i + 1) * half, :] = jnp.where(even, l, h)


def cells_kernel(
    polar, azimuth, grains, stiffness, anisotropy, axis_polar, axis_azimuth, applied,
    cells, props, tables,
):
    ax, ay, az = start_cells(axis_polar[...], axis_azimuth[...])
    root = jnp.sqrt(GAIN * anisotropy[...])
    rows = [stiffness[...], root * ax, root * ay, root * az]
    for r, row in enumerate(rows):
        tables[r : r + 1, :] = row
    for c in range(3):
        tables[4 + c : 5 + c, :] = jnp.full((1, NGRAIN), GAIN * applied[c])
    tabs = grain_tables(rows)

    def body(s, carry):
        start = start_cells(strip(polar, s), strip(azimuth, s))
        for c in range(3):
            put(cells, s, start[c], c)
        labels = strip(grains, s)
        for r in range(4):
            put(props, s, look_up(tabs[r], labels), r)
        return carry

    lax.fori_loop(0, WX // 8, body, 0, unroll=2)


def steps_kernel(
    cells, props, from_high, from_low, halo_xh, halo_xl, tables, sum_z,
    moment, payload,
    m0, m1, wt, cxu, cxd, cyu, cyd, czu, czd, cs, ux, uy, uz, raw,
):
    tabs = grain_tables([tables[r : r + 1, :] for r in range(4)])
    for c in range(3):
        m0[c, 0:WX, 0:COLS] = cells[c]
    for r, ref in enumerate((wt, ux, uy, uz)):
        ref[0:WX, 0:COLS] = props[r]

    def fill(rows, cols, polar, azimuth, labels):
        start = start_cells(polar, azimuth)
        for c in range(3):
            m0[c, rows, cols] = start[c]
        labels = labels.astype(jnp.int32)
        for r, ref in enumerate((wt, ux, uy, uz)):
            ref[rows, cols] = look_up(tabs[r], labels)

    near = iota((8, 128), 1) < 64

    def side(bottom):
        def body(s, carry):
            values = []
            for i in range(3):
                high = strip(from_high, s + i * (WX // 16))
                low = strip(from_low, s + i * (WX // 16))
                if bottom:
                    high, low = pltpu.roll(high, 80, 1), pltpu.roll(low, 48, 1)
                values.append(jnp.where(near, high, low))
            start = s + (WX // 16 if bottom else 0)
            rows = pl.ds(pl.multiple_of(start * 8, 8), 8)
            fill(rows, slice(COLS, LANES), *values)
            return carry

        lax.fori_loop(0, WX // 16, body, 0, unroll=4)

    side(False)
    side(True)
    for i in range(3):
        raw[i, 0:4, :] = halo_xh[i]
        raw[i, 4:8, :] = halo_xl[i]
    fill(slice(WX, ROWS), slice(0, LANES), raw[0], raw[1], raw[2])

    def nxt(s):
        return jnp.where(s == STRIPS - 1, 0, s + 1)

    def prv(s):
        return jnp.where(s == 0, STRIPS - 1, s - 1)

    def couplings(s, carry):
        w = strip(wt, s)
        xu = couple(w, up(w, strip(wt, nxt(s))))
        xd = couple(w, down(w, strip(wt, prv(s))))
        yu = couple(w, pltpu.roll(w, LANES - NZ, 1))
        yd = pltpu.roll(yu, NZ, 1)
        lane = iota(w.shape, 1)
        depth = jnp.where(lane < COLS + 64, lane, lane - LANES + 6 * NZ + COLS) % NZ
        zu = jnp.where(depth != NZ - 1, couple(w, pltpu.roll(w, LANES - 1, 1)), 0.0)
        zd = pltpu.roll(zu, 1, 1)
        for ref, value in zip((cxu, cxd, cyu, cyd, czu, czd), (xu, xd, yu, yd, zu, zd)):
            put(ref, s, value)
        put(cs, s, (xu + xd) + (yu + yd) + (zu + zd))
        return carry

    lax.fori_loop(0, STRIPS, couplings, 0, unroll=3)
    field = [jnp.broadcast_to(tables[4 + c : 5 + c, 0:1], (8, LANES)) for c in range(3)]

    def step(src, dst, s, width):
        after, before = nxt(s), prv(s)
        whole = [strip(src, s, c) for c in range(3)]
        m = [v[:, 0:width] for v in whole]
        u = [strip(r, s)[:, 0:width] for r in (ux, uy, uz)]
        xu, xd, yu, yd, zu, zd, total = (
            strip(r, s)[:, 0:width] for r in (cxu, cxd, cyu, cyd, czu, czd, cs)
        )
        proj = u[0] * m[0] + u[1] * m[1] + u[2] * m[2]
        h = []
        for c in range(3):
            f = yu * pltpu.roll(whole[c], LANES - NZ, 1)[:, 0:width]
            f = f + yd * pltpu.roll(whole[c], NZ, 1)[:, 0:width]
            f = f + zu * pltpu.roll(whole[c], LANES - 1, 1)[:, 0:width]
            f = f + zd * pltpu.roll(whole[c], 1, 1)[:, 0:width]
            f = f + xu * up(m[c], strip(src, after, c)[:, 0:width])
            f = f + xd * down(m[c], strip(src, before, c)[:, 0:width])
            h.append(f - total * m[c] + proj * u[c] + field[c][:, 0:width])
        t = cross(m, h)
        d = cross(m, t)
        v = [m[c] - (t[c] + DAMPING * d[c]) for c in range(3)]
        r = lax.rsqrt(v[0] * v[0] + v[1] * v[1] + v[2] * v[2])
        for c in range(3):
            put(dst, s, v[c] * r, c)

    def one(src, dst, count, unroll, width=LANES):
        def body(s, carry):
            step(src, dst, s, width)
            return carry

        lax.fori_loop(0, count, body, 0, unroll=unroll)

    one(m0, m1, STRIPS, 3)
    one(m1, m0, STRIPS, 3)
    one(m0, m1, STRIPS, 3)
    one(m1, moment, STRIPS - 1, 4, COLS)

    m = jnp.concatenate([moment[c] for c in range(3)], axis=0)
    hi, lo = split(m)
    out = mm(hi, sum_z[...]) + mm(lo, sum_z[...])
    block = iota((16, 128), 1) // 32
    for half in range(2):
        for c in range(3):
            rows = [
                out[c * WX + 16 * g : c * WX + 16 * g + 16, half * 128 : half * 128 + 128]
                for g in range(4)
            ]
            merged = rows[3]
            for g in range(3):
                merged = jnp.where(block == (g + c) % 4, rows[g], merged)
            for peer in range(half, 16, 2):
                payload[peer * 48 + 16 * c : peer * 48 + 16 * c + 16, :] = merged


def cross(first, second):
    return [
        first[1] * second[2] - first[2] * second[1],
        first[2] * second[0] - first[0] * second[2],
        first[0] * second[1] - first[1] * second[0],
    ]


def x_kernel(pair, got, waves_hi, waves_lo, out, d_hi, d_lo):
    turn = (pair[0] * iota((8, 128), 0) + 4) % 8 - 4
    sine, cosine = sincos(turn.astype(jnp.float32) * (math.pi / 4.0))
    sine = jnp.concatenate([sine] * 2, axis=0)
    cosine = jnp.concatenate([cosine] * 2, axis=0)
    block = iota((16, 128), 1) // 32

    def unpack(source, carry):
        parts = []
        for c in range(3):
            start = pl.multiple_of(source * 48 + 16 * c, 16)
            parts.append(got[pl.ds(start, 16), :])
        for g in range(4):
            d = jnp.where(
                block == g, parts[0], jnp.where(block == (g + 1) % 4, parts[1], parts[2])
            )
            if g:
                d = pltpu.roll(d, 128 - 32 * g, 1)
            start = pl.multiple_of(source * 64 + 16 * g, 16)
            for i, factor in enumerate((cosine, sine)):
                hi, lo = split(d * factor)
                d_hi[pl.ds(start, 16), 128 * i : 128 * i + 128] = hi
                d_lo[pl.ds(start, 16), 128 * i : 128 * i + 128] = lo
        return carry

    lax.fori_loop(0, 16, unpack, 0, unroll=4)
    both = mm(waves_hi[...], d_hi[...]) + (
        mm(waves_hi[...], d_lo[...]) + mm(waves_lo[...], d_hi[...])
    )
    sign = jnp.where(iota((8, 128), 0) < 4, 1.0, -1.0)
    for t in range(32):
        rows = slice(8 * t, 8 * t + 8)
        out[rows, :] = both[rows, 0:128] + sign * pltpu.roll(both[rows, 128:256], 4, 0)


def y_kernel(
    first_row, got, waves_hi, waves_lo, twiddle, last_hi, last_lo,
    spin_flip, non_flip, flat, placed,
):
    parts = []
    for ri in range(2):
        rows = [got[pl.ds(4 * ri + low, 32, stride=8), :] for low in range(4)]
        hi, lo = split(jnp.concatenate(rows, axis=0).T[0:96, :])
        parts.append(
            mm(hi, waves_hi[...]) + (mm(lo, waves_hi[...]) + mm(hi, waves_lo[...]))
        )
    re = parts[0][:, 0:128] + parts[1][:, 128:256]
    im = parts[1][:, 0:128] - parts[0][:, 128:256]
    cosine, sine = twiddle[0:32, :], twiddle[32:64, :]
    turned = []
    for c in range(3):
        r, i = re[32 * c : 32 * c + 32, :], im[32 * c : 32 * c + 32, :]
        turned.append(
            jnp.concatenate([r * cosine + i * sine, i * cosine - r * sine], axis=0)
        )
    hi, lo = split(jnp.concatenate(turned, axis=1))
    full = mm(last_hi[...], hi) + (mm(last_hi[...], lo) + mm(last_lo[...], hi))
    lane = iota((32, 128), 1)
    kx = first_row[0] + lane // 32
    ky = iota((32, 128), 0) * 32 + lane % 32
    wave_x = jnp.where(kx < 512, kx, kx - 1024).astype(jnp.float32)
    wave_y = jnp.where(ky < 512, ky, ky - 1024).astype(jnp.float32)
    squared = wave_x * wave_x + wave_y * wave_y
    inverse = lax.rsqrt(jnp.maximum(squared, 1.0))
    unit_x = wave_x * inverse
    unit_y = wave_y * inverse
    stop = jnp.where(squared > 0.5, 1.0 / (NZ * 1024.0 * 1024.0), 0.0)
    nf = sf = 0.0
    for ri in range(2):
        sx, sy, sz = (full[32 * ri : 32 * ri + 32, 128 * c : 128 * c + 128] for c in range(3))
        along = unit_x * sx + unit_y * sy
        px = sx - unit_x * along
        py = sy - unit_y * along
        nf = nf + px * px
        sf = sf + (py * py + sz * sz)
    block = iota((8, 128), 1) // 32
    for value, dst in ((sf, spin_flip), (nf, non_flip)):
        flat[...] = value * stop
        for low in range(4):
            row = None
            for u in range(4):
                piece = flat[pl.ds(u, 8, stride=4), :]
                if u != low:
                    piece = pltpu.roll(piece, (u - low) % 4 * 32, 1)
                row = piece if row is None else jnp.where(block == u, piece, row)
            placed[pl.ds(low, 8, stride=4), :] = row
        for t in range(8):
            dst[:, 128 * t : 128 * t + 128] = placed[4 * t : 4 * t + 4, :]


def pieces(x):
    hi = x.astype(jnp.bfloat16)
    lo = (x - hi.astype(np.float64)).astype(jnp.bfloat16)
    return jnp.asarray(hi), jnp.asarray(lo)


def sum_matrix():
    y = np.arange(COLS) // NZ
    col = np.arange(256)
    return jnp.asarray(
        (y[:, None] == (col // 128 * 32 + col % 32)[None, :]).astype(jnp.bfloat16)
    )


def x_tables():
    row = np.arange(256)
    k = row // 8 * 4 + row % 4
    phase = 2.0 * np.pi * (np.outer(k, np.arange(1024)) % 1024) / 1024.0
    real = (row % 8 < 4)[:, None]
    return pieces(np.where(real, np.cos(phase), -np.sin(phase)))


def y_tables():
    lane = np.arange(128)
    block = 2 * (lane % 16) + lane % 32 // 16
    k = np.arange(128)
    phase = 2.0 * np.pi * (np.outer(block, k % 32) % 32) / 32.0
    same = (lane // 32)[:, None] == (k // 32)[None, :]
    waves = pieces(
        np.concatenate([np.where(same, np.cos(phase), 0.0), np.where(same, np.sin(phase), 0.0)], axis=1)
    )
    q = np.arange(32)
    phase = 2.0 * np.pi * np.outer(q, k % 32) / 1024.0
    twiddle = np.concatenate([np.cos(phase), np.sin(phase)]).astype(np.float32)
    phase = 2.0 * np.pi * (np.outer(q, q) % 32) / 32.0
    c, s = np.cos(phase), np.sin(phase)
    return (*waves, jnp.asarray(twiddle), *pieces(np.block([[c, s], [-s, c]])))


def f32(*shape):
    return jax.ShapeDtypeStruct(shape, jnp.float32)


def vmem(n):
    return [pl.BlockSpec(memory_space=pltpu.VMEM)] * n


def shards(polar, azimuth, grains, stiffness, anisotropy, axis_polar, axis_azimuth, applied_field):
    even_pairs = [(i, i ^ 1) for i in range(16)]
    odd_pairs = [(i, (i + 1) % 16) if i % 2 else (i, (i - 1) % 16) for i in range(16)]
    at_x = lax.axis_index("gx").astype(jnp.int32)
    at_y = lax.axis_index("gy").astype(jnp.int32)
    even_x = at_x % 2 == 0
    even_y = at_y % 2 == 0
    fields = (polar, azimuth, grains)
    params = pltpu.CompilerParams(vmem_limit_bytes=16 << 20)
    smem = [pl.BlockSpec(memory_space=pltpu.SMEM)]
    first = pl.BlockSpec((WX, 128), lambda i: (0, 0))
    last = pl.BlockSpec((WX, 128), lambda i: (0, COLS // 128 - 1))
    to_first, to_second = pl.pallas_call(
        edges_kernel,
        grid=(1,),
        out_shape=(f32(3 * WX // 2, 128), f32(3 * WX // 2, 128)),
        in_specs=smem + [first] * 3 + [last] * 3,
        out_specs=tuple(vmem(2)),
        name="edges",
    )(even_y.astype(jnp.int32).reshape(1), *fields, *fields)
    got_second = lax.ppermute(to_second, "gy", odd_pairs)
    got_first = lax.ppermute(to_first, "gy", even_pairs)
    from_high = jnp.where(even_y, got_first, got_second)
    from_low = jnp.where(even_y, got_second, got_first)

    def edge(start, row, high, low):
        blank = jnp.zeros((4, 32), jnp.float32)
        parts = []
        for i, f in enumerate(fields):
            halo = slice(i * WX // 2 + row, i * WX // 2 + row + 4)
            parts.append(
                jnp.concatenate(
                    [
                        f[start : start + 4].astype(jnp.float32),
                        from_high[halo, high : high + 48],
                        blank,
                        from_low[halo, low : low + 48],
                    ],
                    axis=1,
                )
            )
        return jnp.stack(parts)

    low_edge = edge(0, 0, 0, 80)
    high_edge = edge(WX - 4, WX // 2 - 4, 48, 32)
    got_second = lax.ppermute(jnp.where(even_x, low_edge, high_edge), "gx", odd_pairs)
    got_first = lax.ppermute(jnp.where(even_x, high_edge, low_edge), "gx", even_pairs)
    halo_xh = jnp.where(even_x, got_first, got_second)
    halo_xl = jnp.where(even_x, got_second, got_first)
    per_grain = [
        v.reshape(1, NGRAIN) for v in (stiffness, anisotropy, axis_polar, axis_azimuth)
    ]
    cells, props, tables = pl.pallas_call(
        cells_kernel,
        out_shape=(f32(3, WX, COLS), f32(4, WX, COLS), f32(8, NGRAIN)),
        in_specs=vmem(7) + smem,
        out_specs=tuple(vmem(3)),
        compiler_params=params,
        name="cells",
    )(*fields, *per_grain, applied_field)
    moment, payload = pl.pallas_call(
        steps_kernel,
        out_shape=(f32(3, WX, COLS), f32(16 * 48, 128)),
        in_specs=vmem(8),
        out_specs=tuple(vmem(2)),
        scratch_shapes=[pltpu.VMEM((3, ROWS, LANES), jnp.float32)] * 2
        + [pltpu.VMEM((ROWS, LANES), jnp.float32)] * 11
        + [pltpu.VMEM((3, 8, LANES), jnp.float32)],
        compiler_params=params,
        name="steps",
    )(cells, props, from_high, from_low, halo_xh, halo_xl, tables, sum_matrix())

    columns = lax.all_to_all(
        payload.reshape(16, 48, 128), "gx", split_axis=0, concat_axis=0, tiled=True
    ).reshape(16 * 48, 128)
    rows = pl.pallas_call(
        x_kernel,
        out_shape=f32(256, 128),
        in_specs=smem + vmem(3),
        out_specs=vmem(1)[0],
        scratch_shapes=[pltpu.VMEM((1024, 256), jnp.bfloat16)] * 2,
        compiler_params=params,
        name="along_x",
    )((at_x // 2).reshape(1), columns, *x_tables())
    groups = [
        [gx * 16 + gy for gx in (base, base + 1) for gy in range(16)] for base in range(0, 16, 2)
    ]
    mine = lax.all_to_all(
        rows.reshape(32, 8, 128), ("gx", "gy"), split_axis=0, concat_axis=0, tiled=True,
        axis_index_groups=groups,
    ).reshape(256, 128)
    spin_flip, non_flip = pl.pallas_call(
        y_kernel,
        out_shape=(f32(4, 1024), f32(4, 1024)),
        in_specs=smem + vmem(6),
        out_specs=tuple(vmem(2)),
        scratch_shapes=[pltpu.VMEM((32, 128), jnp.float32)] * 2,
        compiler_params=params,
        name="along_y",
    )((at_x * WX + at_y * 4).reshape(1), mine, *y_tables())
    return (moment, spin_flip, non_flip)


def solution(mesh):
    in_specs = (P("gx", "gy"), P("gx", "gy"), P("gx", "gy"), P(), P(), P(), P(), P())
    out_specs = (P(None, "gx", "gy"), P(("gx", "gy"), None), P(("gx", "gy"), None))
    return jax.shard_map(shards, mesh=mesh, in_specs=in_specs, out_specs=out_specs, check_vma=False)
```

```python
import math

import jax
import jax.numpy as jnp
import numpy as np
from jax import lax
from jax.experimental import pallas as pl
from jax.experimental.pallas import tpu as pltpu
from jax.sharding import PartitionSpec as P

NZ = 12
STEPS = 4
DAMPING = 0.5
TIME_STEP = 0.12
GAIN = TIME_STEP / (1.0 + DAMPING * DAMPING)

WX = 64
WY = 64
COLS = WY * NZ
LANES = COLS + 128
ROWS = WX + 8
STRIPS = ROWS // 8
NGRAIN = 256

COS_POLY = (
    1.0,
    -0.5,
    0.0416666641831398,
    -0.0013888862449675798,
    2.4800550818326883e-05,
    -2.753476167072222e-07,
    2.060329462594268e-09,
    -9.721622812319808e-12,
)
SIN_POLY = (
    1.0,
    -0.1666666567325592,
    0.008333321660757065,
    -0.00019840530876535922,
    2.7535795652511297e-06,
    -2.472832427713456e-08,
    1.361144114087054e-10,
)


def poly(coefs, t):
    acc = coefs[-1] * t + coefs[-2]
    for c in coefs[-3::-1]:
        acc = acc * t + c
    return acc


def sincos(x):
    t = x * x
    return x * poly(SIN_POLY, t), poly(COS_POLY, t)


def split(x):
    hi = x.astype(jnp.bfloat16)
    lo = (x - hi.astype(jnp.float32)).astype(jnp.bfloat16)
    return hi, lo


def mm(a, b):
    return jnp.dot(a, b, preferred_element_type=jnp.float32)


def iota(shape, dim):
    return lax.broadcasted_iota(jnp.int32, shape, dim)


def strip(ref, s, *lead):
    return ref[(*lead, pl.ds(pl.multiple_of(s * 8, 8), 8), slice(None))]


def put(ref, s, value, *lead):
    ref[(*lead, pl.ds(pl.multiple_of(s * 8, 8), 8), slice(None))] = value


def up(cur, following):
    return pltpu.roll(jnp.where(iota(cur.shape, 0) == 0, following, cur), 7, 0)


def down(cur, previous):
    return pltpu.roll(jnp.where(iota(cur.shape, 0) == 7, previous, cur), 1, 0)


def grain_tables(rows):
    return [
        [jnp.broadcast_to(row[:, h * 128 : h * 128 + 128], (8, 128)) for h in range(2)]
        for row in rows
    ]


def look_up(pair, labels):
    low = labels & 127
    first = labels < 128
    parts = []
    for t in range(labels.shape[1] // 128):
        sl = slice(128 * t, 128 * t + 128)
        a = jnp.take_along_axis(pair[0], low[:, sl], axis=1, mode="promise_in_bounds")
        b = jnp.take_along_axis(pair[1], low[:, sl], axis=1, mode="promise_in_bounds")
        parts.append(jnp.where(first[:, sl], a, b))
    return jnp.concatenate(parts, axis=1)


def start_cells(polar, azimuth):
    sp, cp = sincos(polar)
    sa, ca = sincos(azimuth)
    return sp * ca, sp * sa, cp


def couple(p, q):
    return (2.0 * GAIN) * p * q / (p + q)


def edges_kernel(p_low, a_low, g_low, p_high, a_high, g_high, first, second):
    half = WX // 2
    lane = iota((half, 128), 1)
    even = lax.axis_index("gy") % 2 == 0
    for i, (l, h) in enumerate(((p_low, p_high), (a_low, a_high), (g_low, g_high))):
        l, h = l[...].astype(jnp.float32), h[...].astype(jnp.float32)
        l = jnp.where(lane < 48, l[0:half, :], pltpu.roll(l[half:WX, :], 48, 1))
        h = jnp.where(lane >= 80, h[0:half, :], pltpu.roll(h[half:WX, :], 80, 1))
        first[i * half : (i + 1) * half, :] = jnp.where(even, h, l)
        second[i * half : (i + 1) * half, :] = jnp.where(even, l, h)


def cells_kernel(
    polar, azimuth, grains, stiffness, anisotropy, axis_polar, axis_azimuth, applied,
    cells, props, tables,
):
    ax, ay, az = start_cells(axis_polar[...], axis_azimuth[...])
    root = jnp.sqrt(GAIN * anisotropy[...])
    rows = [stiffness[...], root * ax, root * ay, root * az]
    for r, row in enumerate(rows):
        tables[r : r + 1, :] = row
    for c in range(3):
        tables[4 + c : 5 + c, :] = jnp.full((1, NGRAIN), GAIN * applied[c])
    tabs = grain_tables(rows)

    def body(s, carry):
        start = start_cells(strip(polar, s), strip(azimuth, s))
        for c in range(3):
            put(cells, s, start[c], c)
        labels = strip(grains, s)
        for r in range(4):
            put(props, s, look_up(tabs[r], labels), r)
        return carry

    lax.fori_loop(0, WX // 8, body, 0, unroll=2)


def steps_kernel(
    cells, props, from_high, from_low, halo_xh, halo_xl, tables, sum_z, *rest
):
    (
        moment, payload, m0, m1, wt, cxu, cxd, cyu, cyd, czu, czd, cs, ux, uy, uz, raw,
    ) = rest[-16:]
    tabs = grain_tables([tables[r : r + 1, :] for r in range(4)])
    for c in range(3):
        m0[c, 0:WX, 0:COLS] = cells[c]
    for r, ref in enumerate((wt, ux, uy, uz)):
        ref[0:WX, 0:COLS] = props[r]

    def fill(rows, cols, polar, azimuth, labels):
        start = start_cells(polar, azimuth)
        for c in range(3):
            m0[c, rows, cols] = start[c]
        labels = labels.astype(jnp.int32)
        for r, ref in enumerate((wt, ux, uy, uz)):
            ref[rows, cols] = look_up(tabs[r], labels)

    near = iota((8, 128), 1) < 64

    def side(bottom):
        def body(s, carry):
            values = []
            for i in range(3):
                high = strip(from_high, s + i * (WX // 16))
                low = strip(from_low, s + i * (WX // 16))
                if bottom:
                    high, low = pltpu.roll(high, 80, 1), pltpu.roll(low, 48, 1)
                values.append(jnp.where(near, high, low))
            start = s + (WX // 16 if bottom else 0)
            rows = pl.ds(pl.multiple_of(start * 8, 8), 8)
            fill(rows, slice(COLS, LANES), *values)
            return carry

        lax.fori_loop(0, WX // 16, body, 0, unroll=4)

    side(False)
    side(True)
    for i in range(3):
        raw[i, 0:4, :] = halo_xh[i]
        raw[i, 4:8, :] = halo_xl[i]
    fill(slice(WX, ROWS), slice(0, LANES), raw[0], raw[1], raw[2])

    def nxt(s):
        return jnp.where(s == STRIPS - 1, 0, s + 1)

    def prv(s):
        return jnp.where(s == 0, STRIPS - 1, s - 1)

    def couplings(s, carry):
        w = strip(wt, s)
        xu = couple(w, up(w, strip(wt, nxt(s))))
        xd = couple(w, down(w, strip(wt, prv(s))))
        yu = couple(w, pltpu.roll(w, LANES - NZ, 1))
        yd = pltpu.roll(yu, NZ, 1)
        lane = iota(w.shape, 1)
        depth = jnp.where(lane < COLS + 64, lane, lane - LANES + 6 * NZ + COLS) % NZ
        zu = jnp.where(depth != NZ - 1, couple(w, pltpu.roll(w, LANES - 1, 1)), 0.0)
        zd = pltpu.roll(zu, 1, 1)
        for ref, value in zip((cxu, cxd, cyu, cyd, czu, czd), (xu, xd, yu, yd, zu, zd)):
            put(ref, s, value)
        put(cs, s, (xu + xd) + (yu + yd) + (zu + zd))
        return carry

    lax.fori_loop(0, STRIPS, couplings, 0, unroll=3)
    field = [jnp.broadcast_to(tables[4 + c : 5 + c, 0:1], (8, LANES)) for c in range(3)]

    def step(src, dst, s, width):
        after, before = nxt(s), prv(s)
        whole = [strip(src, s, c) for c in range(3)]
        m = [v[:, 0:width] for v in whole]
        u = [strip(r, s)[:, 0:width] for r in (ux, uy, uz)]
        xu, xd, yu, yd, zu, zd, total = (
            strip(r, s)[:, 0:width] for r in (cxu, cxd, cyu, cyd, czu, czd, cs)
        )
        proj = u[0] * m[0] + u[1] * m[1] + u[2] * m[2]
        h = []
        for c in range(3):
            f = yu * pltpu.roll(whole[c], LANES - NZ, 1)[:, 0:width]
            f = f + yd * pltpu.roll(whole[c], NZ, 1)[:, 0:width]
            f = f + zu * pltpu.roll(whole[c], LANES - 1, 1)[:, 0:width]
            f = f + zd * pltpu.roll(whole[c], 1, 1)[:, 0:width]
            f = f + xu * up(m[c], strip(src, after, c)[:, 0:width])
            f = f + xd * down(m[c], strip(src, before, c)[:, 0:width])
            h.append(f - total * m[c] + proj * u[c] + field[c][:, 0:width])
        t = cross(m, h)
        d = cross(m, t)
        v = [m[c] - (t[c] + DAMPING * d[c]) for c in range(3)]
        r = lax.rsqrt(v[0] * v[0] + v[1] * v[1] + v[2] * v[2])
        for c in range(3):
            put(dst, s, v[c] * r, c)

    def one(src, dst, count, unroll, width=LANES):
        def body(s, carry):
            step(src, dst, s, width)
            return carry

        lax.fori_loop(0, count, body, 0, unroll=unroll)

    one(m0, m1, STRIPS, 3)
    one(m1, m0, STRIPS, 3)
    one(m0, m1, STRIPS, 3)
    one(m1, moment, STRIPS - 1, 4, COLS)

    m = jnp.concatenate([moment[c] for c in range(3)], axis=0)
    hi, lo = split(m)
    out = mm(hi, sum_z[...]) + mm(lo, sum_z[...])
    block = iota((16, 128), 1) // 32
    for half in range(2):
        for c in range(3):
            rows = [
                out[c * WX + 16 * g : c * WX + 16 * g + 16, half * 128 : half * 128 + 128]
                for g in range(4)
            ]
            merged = rows[3]
            for g in range(3):
                merged = jnp.where(block == (g + c) % 4, rows[g], merged)
            for peer in range(half, 16, 2):
                payload[peer * 48 + 16 * c : peer * 48 + 16 * c + 16, :] = merged


def cross(first, second):
    return [
        first[1] * second[2] - first[2] * second[1],
        first[2] * second[0] - first[0] * second[2],
        first[0] * second[1] - first[1] * second[0],
    ]


def x_kernel(got, waves_hi, waves_lo, out, d_hi, d_lo):
    pair = lax.axis_index("gx") // 2
    turn = (pair * iota((8, 128), 0) + 4) % 8 - 4
    sine, cosine = sincos(turn.astype(jnp.float32) * (math.pi / 4.0))
    sine = jnp.concatenate([sine] * 2, axis=0)
    cosine = jnp.concatenate([cosine] * 2, axis=0)
    block = iota((16, 128), 1) // 32

    def unpack(source, carry):
        parts = []
        for c in range(3):
            start = pl.multiple_of(source * 48 + 16 * c, 16)
            parts.append(got[pl.ds(start, 16), :])
        for g in range(4):
            d = jnp.where(
                block == g, parts[0], jnp.where(block == (g + 1) % 4, parts[1], parts[2])
            )
            if g:
                d = pltpu.roll(d, 128 - 32 * g, 1)
            start = pl.multiple_of(source * 64 + 16 * g, 16)
            for i, factor in enumerate((cosine, sine)):
                hi, lo = split(d * factor)
                d_hi[pl.ds(start, 16), 128 * i : 128 * i + 128] = hi
                d_lo[pl.ds(start, 16), 128 * i : 128 * i + 128] = lo
        return carry

    lax.fori_loop(0, 16, unpack, 0, unroll=4)
    both = mm(waves_hi[...], d_hi[...]) + (
        mm(waves_hi[...], d_lo[...]) + mm(waves_lo[...], d_hi[...])
    )
    sign = jnp.where(iota((8, 128), 0) < 4, 1.0, -1.0)
    for t in range(32):
        rows = slice(8 * t, 8 * t + 8)
        out[rows, :] = both[rows, 0:128] + sign * pltpu.roll(both[rows, 128:256], 4, 0)


def y_kernel(
    got, waves_hi, waves_lo, twiddle, last_hi, last_lo,
    spin_flip, non_flip, flat, placed,
):
    parts = []
    for ri in range(2):
        rows = [got[pl.ds(4 * ri + low, 32, stride=8), :] for low in range(4)]
        hi, lo = split(jnp.concatenate(rows, axis=0).T[0:96, :])
        parts.append(
            mm(hi, waves_hi[...]) + (mm(lo, waves_hi[...]) + mm(hi, waves_lo[...]))
        )
    re = parts[0][:, 0:128] + parts[1][:, 128:256]
    im = parts[1][:, 0:128] - parts[0][:, 128:256]
    cosine, sine = twiddle[0:32, :], twiddle[32:64, :]
    turned = []
    for c in range(3):
        r, i = re[32 * c : 32 * c + 32, :], im[32 * c : 32 * c + 32, :]
        turned.append(
            jnp.concatenate([r * cosine + i * sine, i * cosine - r * sine], axis=0)
        )
    hi, lo = split(jnp.concatenate(turned, axis=1))
    full = mm(last_hi[...], hi) + (mm(last_hi[...], lo) + mm(last_lo[...], hi))
    lane = iota((32, 128), 1)
    kx = lax.axis_index("gx") * WX + lax.axis_index("gy") * 4 + lane // 32
    ky = iota((32, 128), 0) * 32 + lane % 32
    wave_x = jnp.where(kx < 512, kx, kx - 1024).astype(jnp.float32)
    wave_y = jnp.where(ky < 512, ky, ky - 1024).astype(jnp.float32)
    squared = wave_x * wave_x + wave_y * wave_y
    inverse = lax.rsqrt(jnp.maximum(squared, 1.0))
    unit_x = wave_x * inverse
    unit_y = wave_y * inverse
    stop = jnp.where(squared > 0.5, 1.0 / (NZ * 1024.0 * 1024.0), 0.0)
    nf = sf = 0.0
    for ri in range(2):
        sx, sy, sz = (full[32 * ri : 32 * ri + 32, 128 * c : 128 * c + 128] for c in range(3))
        along = unit_x * sx + unit_y * sy
        px = sx - unit_x * along
        py = sy - unit_y * along
        nf = nf + px * px
        sf = sf + (py * py + sz * sz)
    block = iota((8, 128), 1) // 32
    for value, dst in ((sf, spin_flip), (nf, non_flip)):
        flat[...] = value * stop
        for low in range(4):
            row = None
            for u in range(4):
                piece = flat[pl.ds(u, 8, stride=4), :]
                if u != low:
                    piece = pltpu.roll(piece, (u - low) % 4 * 32, 1)
                row = piece if row is None else jnp.where(block == u, piece, row)
            placed[pl.ds(low, 8, stride=4), :] = row
        for t in range(8):
            dst[:, 128 * t : 128 * t + 128] = placed[4 * t : 4 * t + 4, :]


def pieces(x):
    hi = x.astype(jnp.bfloat16)
    lo = (x - hi.astype(np.float64)).astype(jnp.bfloat16)
    return jnp.asarray(hi), jnp.asarray(lo)


def sum_matrix():
    y = np.arange(COLS) // NZ
    col = np.arange(256)
    return jnp.asarray(
        (y[:, None] == (col // 128 * 32 + col % 32)[None, :]).astype(jnp.bfloat16)
    )


def x_tables():
    row = np.arange(256)
    k = row // 8 * 4 + row % 4
    phase = 2.0 * np.pi * (np.outer(k, np.arange(1024)) % 1024) / 1024.0
    real = (row % 8 < 4)[:, None]
    return pieces(np.where(real, np.cos(phase), -np.sin(phase)))


def y_tables():
    lane = np.arange(128)
    block = 2 * (lane % 16) + lane % 32 // 16
    k = np.arange(128)
    phase = 2.0 * np.pi * (np.outer(block, k % 32) % 32) / 32.0
    same = (lane // 32)[:, None] == (k // 32)[None, :]
    waves = pieces(
        np.concatenate([np.where(same, np.cos(phase), 0.0), np.where(same, np.sin(phase), 0.0)], axis=1)
    )
    q = np.arange(32)
    phase = 2.0 * np.pi * np.outer(q, k % 32) / 1024.0
    twiddle = np.concatenate([np.cos(phase), np.sin(phase)]).astype(np.float32)
    phase = 2.0 * np.pi * (np.outer(q, q) % 32) / 32.0
    c, s = np.cos(phase), np.sin(phase)
    return (*waves, jnp.asarray(twiddle), *pieces(np.block([[c, s], [-s, c]])))


def f32(*shape):
    return jax.ShapeDtypeStruct(shape, jnp.float32)


def vmem(n):
    return [pl.BlockSpec(memory_space=pltpu.VMEM)] * n


def shards(polar, azimuth, grains, stiffness, anisotropy, axis_polar, axis_azimuth, applied_field):
    even_pairs = [(i, i ^ 1) for i in range(16)]
    odd_pairs = [(i, (i + 1) % 16) if i % 2 else (i, (i - 1) % 16) for i in range(16)]
    at_x = lax.axis_index("gx").astype(jnp.int32)
    at_y = lax.axis_index("gy").astype(jnp.int32)
    even_x = at_x % 2 == 0
    even_y = at_y % 2 == 0
    fields = (polar, azimuth, grains)
    params = pltpu.CompilerParams(vmem_limit_bytes=16 << 20)
    smem = [pl.BlockSpec(memory_space=pltpu.SMEM)]
    first = pl.BlockSpec((WX, 128), lambda i: (0, 0))
    last = pl.BlockSpec((WX, 128), lambda i: (0, COLS // 128 - 1))
    to_first, to_second = pl.pallas_call(
        edges_kernel,
        grid=(1,),
        out_shape=(f32(3 * WX // 2, 128), f32(3 * WX // 2, 128)),
        in_specs=[first] * 3 + [last] * 3,
        out_specs=tuple(vmem(2)),
        name="edges",
    )(*fields, *fields)
    got_second = lax.ppermute(to_second, "gy", odd_pairs)
    got_first = lax.ppermute(to_first, "gy", even_pairs)
    from_high = jnp.where(even_y, got_first, got_second)
    from_low = jnp.where(even_y, got_second, got_first)

    def edge(start, row, high, low):
        blank = jnp.zeros((4, 32), jnp.float32)
        parts = []
        for i, f in enumerate(fields):
            halo = slice(i * WX // 2 + row, i * WX // 2 + row + 4)
            parts.append(
                jnp.concatenate(
                    [
                        f[start : start + 4].astype(jnp.float32),
                        from_high[halo, high : high + 48],
                        blank,
                        from_low[halo, low : low + 48],
                    ],
                    axis=1,
                )
            )
        return jnp.stack(parts)

    low_edge = edge(0, 0, 0, 80)
    high_edge = edge(WX - 4, WX // 2 - 4, 48, 32)
    got_second = lax.ppermute(jnp.where(even_x, low_edge, high_edge), "gx", odd_pairs)
    got_first = lax.ppermute(jnp.where(even_x, high_edge, low_edge), "gx", even_pairs)
    halo_xh = jnp.where(even_x, got_first, got_second)
    halo_xl = jnp.where(even_x, got_second, got_first)
    per_grain = [
        v.reshape(1, NGRAIN) for v in (stiffness, anisotropy, axis_polar, axis_azimuth)
    ]
    cells, props, tables = pl.pallas_call(
        cells_kernel,
        out_shape=(f32(3, WX, COLS), f32(4, WX, COLS), f32(8, NGRAIN)),
        in_specs=vmem(7) + smem,
        out_specs=tuple(vmem(3)),
        compiler_params=params,
        name="cells",
    )(*fields, *per_grain, applied_field)
    tables_x, tables_y = x_tables(), y_tables()
    moment, payload = pl.pallas_call(
        steps_kernel,
        out_shape=(f32(3, WX, COLS), f32(16 * 48, 128)),
        in_specs=vmem(8 + len(tables_x) + len(tables_y)),
        out_specs=tuple(vmem(2)),
        scratch_shapes=[pltpu.VMEM((3, ROWS, LANES), jnp.float32)] * 2
        + [pltpu.VMEM((ROWS, LANES), jnp.float32)] * 11
        + [pltpu.VMEM((3, 8, LANES), jnp.float32)],
        compiler_params=params,
        name="steps",
    )(cells, props, from_high, from_low, halo_xh, halo_xl, tables, sum_matrix(), *tables_x, *tables_y)

    columns = lax.all_to_all(
        payload.reshape(16, 48, 128), "gx", split_axis=0, concat_axis=0, tiled=True
    ).reshape(16 * 48, 128)
    rows = pl.pallas_call(
        x_kernel,
        out_shape=f32(256, 128),
        in_specs=vmem(3),
        out_specs=vmem(1)[0],
        scratch_shapes=[pltpu.VMEM((1024, 256), jnp.bfloat16)] * 2,
        compiler_params=params,
        name="along_x",
    )(columns, *tables_x)
    groups = [
        [gx * 16 + gy for gx in (base, base + 1) for gy in range(16)] for base in range(0, 16, 2)
    ]
    mine = lax.all_to_all(
        rows.reshape(32, 8, 128), ("gx", "gy"), split_axis=0, concat_axis=0, tiled=True,
        axis_index_groups=groups,
    ).reshape(256, 128)
    spin_flip, non_flip = pl.pallas_call(
        y_kernel,
        out_shape=(f32(4, 1024), f32(4, 1024)),
        in_specs=vmem(6),
        out_specs=tuple(vmem(2)),
        scratch_shapes=[pltpu.VMEM((32, 128), jnp.float32)] * 2,
        compiler_params=params,
        name="along_y",
    )(mine, *tables_y)
    return (moment, spin_flip, non_flip)


def solution(mesh):
    in_specs = (P("gx", "gy"), P("gx", "gy"), P("gx", "gy"), P(), P(), P(), P(), P())
    out_specs = (P(None, "gx", "gy"), P(("gx", "gy"), None), P(("gx", "gy"), None))
    return jax.shard_map(shards, mesh=mesh, in_specs=in_specs, out_specs=out_specs, check_vma=False)
```

```python
import math

import jax
import jax.numpy as jnp
import numpy as np
from jax import lax
from jax.experimental import pallas as pl
from jax.experimental.pallas import tpu as pltpu
from jax.sharding import PartitionSpec as P

NZ = 12
STEPS = 4
DAMPING = 0.5
TIME_STEP = 0.12
GAIN = TIME_STEP / (1.0 + DAMPING * DAMPING)

WX = 64
WY = 64
COLS = WY * NZ
LANES = COLS + 128
ROWS = WX + 8
STRIPS = ROWS // 8
NGRAIN = 256

COS_POLY = (
    1.0,
    -0.5,
    0.0416666641831398,
    -0.0013888862449675798,
    2.4800550818326883e-05,
    -2.753476167072222e-07,
    2.060329462594268e-09,
    -9.721622812319808e-12,
)
SIN_POLY = (
    1.0,
    -0.1666666567325592,
    0.008333321660757065,
    -0.00019840530876535922,
    2.7535795652511297e-06,
    -2.472832427713456e-08,
    1.361144114087054e-10,
)


def poly(coefs, t):
    acc = coefs[-1] * t + coefs[-2]
    for c in coefs[-3::-1]:
        acc = acc * t + c
    return acc


def sincos(x):
    t = x * x
    return x * poly(SIN_POLY, t), poly(COS_POLY, t)


def split(x):
    hi = x.astype(jnp.bfloat16)
    lo = (x - hi.astype(jnp.float32)).astype(jnp.bfloat16)
    return hi, lo


def mm(a, b):
    return jnp.dot(a, b, preferred_element_type=jnp.float32)


def iota(shape, dim):
    return lax.broadcasted_iota(jnp.int32, shape, dim)


def strip(ref, s, *lead):
    return ref[(*lead, pl.ds(pl.multiple_of(s * 8, 8), 8), slice(None))]


def put(ref, s, value, *lead):
    ref[(*lead, pl.ds(pl.multiple_of(s * 8, 8), 8), slice(None))] = value


def up(cur, following):
    return pltpu.roll(jnp.where(iota(cur.shape, 0) == 0, following, cur), 7, 0)


def down(cur, previous):
    return pltpu.roll(jnp.where(iota(cur.shape, 0) == 7, previous, cur), 1, 0)


def grain_tables(rows):
    return [
        [jnp.broadcast_to(row[:, h * 128 : h * 128 + 128], (8, 128)) for h in range(2)]
        for row in rows
    ]


def look_up(pair, labels):
    low = labels & 127
    first = labels < 128
    parts = []
    for t in range(labels.shape[1] // 128):
        sl = slice(128 * t, 128 * t + 128)
        a = jnp.take_along_axis(pair[0], low[:, sl], axis=1, mode="promise_in_bounds")
        b = jnp.take_along_axis(pair[1], low[:, sl], axis=1, mode="promise_in_bounds")
        parts.append(jnp.where(first[:, sl], a, b))
    return jnp.concatenate(parts, axis=1)


def start_cells(polar, azimuth):
    sp, cp = sincos(polar)
    sa, ca = sincos(azimuth)
    return sp * ca, sp * sa, cp


def couple(p, q):
    return (2.0 * GAIN) * p * q / (p + q)


def edges_kernel(
    p_low, a_low, g_low, p_high, a_high, g_high,
    stiffness, anisotropy, axis_polar, axis_azimuth, applied,
    first, second, tables,
):
    ax, ay, az = start_cells(axis_polar[...], axis_azimuth[...])
    root = jnp.sqrt(GAIN * anisotropy[...])
    for r, row in enumerate((stiffness[...], root * ax, root * ay, root * az)):
        tables[r : r + 1, :] = row
    for c in range(3):
        tables[4 + c : 5 + c, :] = jnp.full((1, NGRAIN), GAIN * applied[c])

    half = WX // 2
    lane = iota((half, 128), 1)
    even = lax.axis_index("gy") % 2 == 0
    for i, (l, h) in enumerate(((p_low, p_high), (a_low, a_high), (g_low, g_high))):
        l, h = l[...].astype(jnp.float32), h[...].astype(jnp.float32)
        l = jnp.where(lane < 48, l[0:half, :], pltpu.roll(l[half:WX, :], 48, 1))
        h = jnp.where(lane >= 80, h[0:half, :], pltpu.roll(h[half:WX, :], 80, 1))
        first[i * half : (i + 1) * half, :] = jnp.where(even, h, l)
        second[i * half : (i + 1) * half, :] = jnp.where(even, l, h)


def cells_kernel(polar, azimuth, grains, tables, cells, props, ends):
    tabs = grain_tables([tables[r : r + 1, :] for r in range(4)])
    for i, src in enumerate((polar, azimuth, grains)):
        ends[0, i] = src[0:4, :].astype(jnp.float32)
        ends[1, i] = src[WX - 4 : WX, :].astype(jnp.float32)

    def body(s, carry):
        start = start_cells(strip(polar, s), strip(azimuth, s))
        for c in range(3):
            put(cells, s, start[c], c)
        labels = strip(grains, s)
        for r in range(4):
            put(props, s, look_up(tabs[r], labels), r)
        return carry

    lax.fori_loop(0, WX // 8, body, 0, unroll=2)


def cell_rows(polar, azimuth, labels, tabs):
    labels = labels.astype(jnp.int32)
    return start_cells(polar, azimuth), [look_up(tab, labels) for tab in tabs]


def coupling_rows(w, after, before):
    xu = couple(w, up(w, after))
    xd = couple(w, down(w, before))
    yu = couple(w, pltpu.roll(w, LANES - NZ, 1))
    yd = pltpu.roll(yu, NZ, 1)
    lane = iota(w.shape, 1)
    depth = jnp.where(lane < COLS + 64, lane, lane - LANES + 6 * NZ + COLS) % NZ
    zu = jnp.where(depth != NZ - 1, couple(w, pltpu.roll(w, LANES - 1, 1)), 0.0)
    zd = pltpu.roll(zu, 1, 1)
    return xu, xd, yu, yd, zu, zd, (xu + xd) + (yu + yd) + (zu + zd)


def applied_rows(tables):
    return [jnp.broadcast_to(tables[4 + c : 5 + c, 0:1], (8, LANES)) for c in range(3)]


def step(src, dst, s, after, before, coefs, row, field, width=LANES):
    whole = [strip(src, s, c) for c in range(3)]
    m = [v[:, 0:width] for v in whole]
    xu, xd, yu, yd, zu, zd, total, *u = (
        strip(coefs, row, r)[:, 0:width] for r in range(1, COEFS)
    )
    proj = u[0] * m[0] + u[1] * m[1] + u[2] * m[2]
    h = []
    for c in range(3):
        f = yu * pltpu.roll(whole[c], LANES - NZ, 1)[:, 0:width]
        f = f + yd * pltpu.roll(whole[c], NZ, 1)[:, 0:width]
        f = f + zu * pltpu.roll(whole[c], LANES - 1, 1)[:, 0:width]
        f = f + zd * pltpu.roll(whole[c], 1, 1)[:, 0:width]
        f = f + xu * up(m[c], strip(src, after, c)[:, 0:width])
        f = f + xd * down(m[c], strip(src, before, c)[:, 0:width])
        h.append(f - total * m[c] + proj * u[c] + field[c][:, 0:width])
    t = cross(m, h)
    d = cross(m, t)
    v = [m[c] - (t[c] + DAMPING * d[c]) for c in range(3)]
    r = lax.rsqrt(v[0] * v[0] + v[1] * v[1] + v[2] * v[2])
    for c in range(3):
        put(dst, s, v[c] * r, c)


COEFS = 11
LAST = WX // 8 - 1


def inner_strips(body):
    def one(s, carry):
        body(s)
        return carry

    lax.fori_loop(1, LAST, one, 0, unroll=3)


def inner_kernel(cells, props, from_high, from_low, tables, m0, m1, coefs):
    tabs = grain_tables([tables[r : r + 1, :] for r in range(4)])
    for c in range(3):
        m0[c, :, 0:COLS] = cells[c]
    for r, i in enumerate((0, 8, 9, 10)):
        coefs[i, :, 0:COLS] = props[r]
    near = iota((8, 128), 1) < 64

    def side(bottom):
        def body(s, carry):
            values = []
            for i in range(3):
                high = strip(from_high, s + i * (WX // 16))
                low = strip(from_low, s + i * (WX // 16))
                if bottom:
                    high, low = pltpu.roll(high, 80, 1), pltpu.roll(low, 48, 1)
                values.append(jnp.where(near, high, low))
            start, found = cell_rows(*values, tabs)
            first = s + (WX // 16 if bottom else 0)
            rows = pl.ds(pl.multiple_of(first * 8, 8), 8)
            for c in range(3):
                m0[c, rows, COLS:LANES] = start[c]
            for r, i in enumerate((0, 8, 9, 10)):
                coefs[i, rows, COLS:LANES] = found[r]
            return carry

        lax.fori_loop(0, WX // 16, body, 0, unroll=4)

    side(False)
    side(True)

    def couplings(s):
        found = coupling_rows(*(strip(coefs, i, 0) for i in (s, s + 1, s - 1)))
        for r, value in enumerate(found):
            put(coefs, s, value, 1 + r)

    inner_strips(couplings)
    field = applied_rows(tables)
    inner_strips(lambda s: step(m0, m1, s, s + 1, s - 1, coefs, s, field))


def steps_kernel(
    first0, first1, coefs, halo_xh, halo_xl, tables, sum_z, *rest
):
    moment, payload, m0, m1, rim, raw = rest[-6:]
    tabs = grain_tables([tables[r : r + 1, :] for r in range(4)])
    for i in range(3):
        raw[i, 0:4, :] = halo_xh[i]
        raw[i, 4:8, :] = halo_xl[i]
    start, found = cell_rows(raw[0], raw[1], raw[2], tabs)
    for c in range(3):
        m0[c, 0:16, :] = first0[c, 0:16, :]
        m0[c, WX - 16 : WX, :] = first0[c, WX - 16 : WX, :]
        m0[c, WX:ROWS, :] = start[c]
        m1[c, 8 : WX - 8, :] = first1[c, 8 : WX - 8, :]
    for r, i in enumerate((0, 8, 9, 10)):
        rim[i, 0:8, :] = coefs[i, WX - 8 : WX, :]
        rim[i, 8:16, :] = found[r]
        rim[i, 16:24, :] = coefs[i, 0:8, :]
    stiff = [coefs[0, WX - 16 : WX - 8, :]]
    stiff += [rim[0, 8 * i : 8 * i + 8, :] for i in range(3)] + [coefs[0, 8:16, :]]
    for i in range(3):
        for r, value in enumerate(coupling_rows(stiff[i + 1], stiff[i + 2], stiff[i])):
            rim[1 + r, 8 * i : 8 * i + 8, :] = value
    field = applied_rows(tables)

    def outer(src, dst, width=LANES):
        for i, s in enumerate((LAST, LAST + 1, 0)):
            if s > LAST and width < LANES:
                continue
            after, before = (s + 1) % STRIPS, (s - 1) % STRIPS
            step(src, dst, s, after, before, rim, i, field, width)

    def inner(src, dst, width=LANES):
        inner_strips(lambda s: step(src, dst, s, s + 1, s - 1, coefs, s, field, width))

    outer(m0, m1)
    for src, dst in ((m1, m0), (m0, m1)):
        outer(src, dst)
        inner(src, dst)
    outer(m1, moment, COLS)
    inner(m1, moment, COLS)

    m = jnp.concatenate([moment[c] for c in range(3)], axis=0)
    hi, lo = split(m)
    out = mm(hi, sum_z[...]) + mm(lo, sum_z[...])
    block = iota((16, 128), 1) // 32
    for half in range(2):
        for c in range(3):
            rows = [
                out[c * WX + 16 * g : c * WX + 16 * g + 16, half * 128 : half * 128 + 128]
                for g in range(4)
            ]
            merged = rows[3]
            for g in range(3):
                merged = jnp.where(block == (g + c) % 4, rows[g], merged)
            for peer in range(half, 16, 2):
                payload[peer * 48 + 16 * c : peer * 48 + 16 * c + 16, :] = merged


def cross(first, second):
    return [
        first[1] * second[2] - first[2] * second[1],
        first[2] * second[0] - first[0] * second[2],
        first[0] * second[1] - first[1] * second[0],
    ]


def x_kernel(got, waves_hi, waves_lo, out, d_hi, d_lo):
    pair = lax.axis_index("gx") // 2
    turn = (pair * iota((8, 128), 0) + 4) % 8 - 4
    sine, cosine = sincos(turn.astype(jnp.float32) * (math.pi / 4.0))
    sine = jnp.concatenate([sine] * 2, axis=0)
    cosine = jnp.concatenate([cosine] * 2, axis=0)
    block = iota((16, 128), 1) // 32

    def unpack(source, carry):
        parts = []
        for c in range(3):
            start = pl.multiple_of(source * 48 + 16 * c, 16)
            parts.append(got[pl.ds(start, 16), :])
        for g in range(4):
            d = jnp.where(
                block == g, parts[0], jnp.where(block == (g + 1) % 4, parts[1], parts[2])
            )
            if g:
                d = pltpu.roll(d, 128 - 32 * g, 1)
            start = pl.multiple_of(source * 64 + 16 * g, 16)
            for i, factor in enumerate((cosine, sine)):
                hi, lo = split(d * factor)
                d_hi[pl.ds(start, 16), 128 * i : 128 * i + 128] = hi
                d_lo[pl.ds(start, 16), 128 * i : 128 * i + 128] = lo
        return carry

    lax.fori_loop(0, 16, unpack, 0, unroll=4)
    both = mm(waves_hi[...], d_hi[...]) + (
        mm(waves_hi[...], d_lo[...]) + mm(waves_lo[...], d_hi[...])
    )
    sign = jnp.where(iota((8, 128), 0) < 4, 1.0, -1.0)
    for t in range(32):
        rows = slice(8 * t, 8 * t + 8)
        out[rows, :] = both[rows, 0:128] + sign * pltpu.roll(both[rows, 128:256], 4, 0)


def y_kernel(
    got, waves_hi, waves_lo, twiddle, last_hi, last_lo,
    spin_flip, non_flip, flat, placed,
):
    parts = []
    for ri in range(2):
        rows = [got[pl.ds(4 * ri + low, 32, stride=8), :] for low in range(4)]
        hi, lo = split(jnp.concatenate(rows, axis=0).T[0:96, :])
        parts.append(
            mm(hi, waves_hi[...]) + (mm(lo, waves_hi[...]) + mm(hi, waves_lo[...]))
        )
    re = parts[0][:, 0:128] + parts[1][:, 128:256]
    im = parts[1][:, 0:128] - parts[0][:, 128:256]
    cosine, sine = twiddle[0:32, :], twiddle[32:64, :]
    turned = []
    for c in range(3):
        r, i = re[32 * c : 32 * c + 32, :], im[32 * c : 32 * c + 32, :]
        turned.append(
            jnp.concatenate([r * cosine + i * sine, i * cosine - r * sine], axis=0)
        )
    hi, lo = split(jnp.concatenate(turned, axis=1))
    full = mm(last_hi[...], hi) + (mm(last_hi[...], lo) + mm(last_lo[...], hi))
    lane = iota((32, 128), 1)
    kx = lax.axis_index("gx") * WX + lax.axis_index("gy") * 4 + lane // 32
    ky = iota((32, 128), 0) * 32 + lane % 32
    wave_x = jnp.where(kx < 512, kx, kx - 1024).astype(jnp.float32)
    wave_y = jnp.where(ky < 512, ky, ky - 1024).astype(jnp.float32)
    squared = wave_x * wave_x + wave_y * wave_y
    inverse = lax.rsqrt(jnp.maximum(squared, 1.0))
    unit_x = wave_x * inverse
    unit_y = wave_y * inverse
    stop = jnp.where(squared > 0.5, 1.0 / (NZ * 1024.0 * 1024.0), 0.0)
    nf = sf = 0.0
    for ri in range(2):
        sx, sy, sz = (full[32 * ri : 32 * ri + 32, 128 * c : 128 * c + 128] for c in range(3))
        along = unit_x * sx + unit_y * sy
        px = sx - unit_x * along
        py = sy - unit_y * along
        nf = nf + px * px
        sf = sf + (py * py + sz * sz)
    block = iota((8, 128), 1) // 32
    for value, dst in ((sf, spin_flip), (nf, non_flip)):
        flat[...] = value * stop
        for low in range(4):
            row = None
            for u in range(4):
                piece = flat[pl.ds(u, 8, stride=4), :]
                if u != low:
                    piece = pltpu.roll(piece, (u - low) % 4 * 32, 1)
                row = piece if row is None else jnp.where(block == u, piece, row)
            placed[pl.ds(low, 8, stride=4), :] = row
        for t in range(8):
            dst[:, 128 * t : 128 * t + 128] = placed[4 * t : 4 * t + 4, :]


def pieces(x):
    hi = x.astype(jnp.bfloat16)
    lo = (x - hi.astype(np.float64)).astype(jnp.bfloat16)
    return jnp.asarray(hi), jnp.asarray(lo)


def sum_matrix():
    y = np.arange(COLS) // NZ
    col = np.arange(256)
    return jnp.asarray(
        (y[:, None] == (col // 128 * 32 + col % 32)[None, :]).astype(jnp.bfloat16)
    )


def x_tables():
    row = np.arange(256)
    k = row // 8 * 4 + row % 4
    phase = 2.0 * np.pi * (np.outer(k, np.arange(1024)) % 1024) / 1024.0
    real = (row % 8 < 4)[:, None]
    return pieces(np.where(real, np.cos(phase), -np.sin(phase)))


def y_tables():
    lane = np.arange(128)
    block = 2 * (lane % 16) + lane % 32 // 16
    k = np.arange(128)
    phase = 2.0 * np.pi * (np.outer(block, k % 32) % 32) / 32.0
    same = (lane // 32)[:, None] == (k // 32)[None, :]
    waves = pieces(
        np.concatenate([np.where(same, np.cos(phase), 0.0), np.where(same, np.sin(phase), 0.0)], axis=1)
    )
    q = np.arange(32)
    phase = 2.0 * np.pi * np.outer(q, k % 32) / 1024.0
    twiddle = np.concatenate([np.cos(phase), np.sin(phase)]).astype(np.float32)
    phase = 2.0 * np.pi * (np.outer(q, q) % 32) / 32.0
    c, s = np.cos(phase), np.sin(phase)
    return (*waves, jnp.asarray(twiddle), *pieces(np.block([[c, s], [-s, c]])))


def f32(*shape):
    return jax.ShapeDtypeStruct(shape, jnp.float32)


def vmem(n):
    return [pl.BlockSpec(memory_space=pltpu.VMEM)] * n


def shards(polar, azimuth, grains, stiffness, anisotropy, axis_polar, axis_azimuth, applied_field):
    even_pairs = [(i, i ^ 1) for i in range(16)]
    odd_pairs = [(i, (i + 1) % 16) if i % 2 else (i, (i - 1) % 16) for i in range(16)]
    at_x = lax.axis_index("gx").astype(jnp.int32)
    at_y = lax.axis_index("gy").astype(jnp.int32)
    even_x = at_x % 2 == 0
    even_y = at_y % 2 == 0
    fields = (polar, azimuth, grains)
    params = pltpu.CompilerParams(vmem_limit_bytes=16 << 20)
    smem = [pl.BlockSpec(memory_space=pltpu.SMEM)]
    per_grain = [
        v.reshape(1, NGRAIN) for v in (stiffness, anisotropy, axis_polar, axis_azimuth)
    ]
    first = pl.BlockSpec((WX, 128), lambda i: (0, 0))
    last = pl.BlockSpec((WX, 128), lambda i: (0, COLS // 128 - 1))
    to_first, to_second, tables = pl.pallas_call(
        edges_kernel,
        grid=(1,),
        out_shape=(f32(3 * WX // 2, 128), f32(3 * WX // 2, 128), f32(8, NGRAIN)),
        in_specs=[first] * 3 + [last] * 3 + vmem(4) + smem,
        out_specs=tuple(vmem(3)),
        name="edges",
    )(*fields, *fields, *per_grain, applied_field)
    got_second = lax.ppermute(to_second, "gy", odd_pairs)
    got_first = lax.ppermute(to_first, "gy", even_pairs)
    from_high = jnp.where(even_y, got_first, got_second)
    from_low = jnp.where(even_y, got_second, got_first)

    cells, props, ends = pl.pallas_call(
        cells_kernel,
        out_shape=(f32(3, WX, COLS), f32(4, WX, COLS), f32(2, 3, 4, COLS)),
        in_specs=vmem(4),
        out_specs=tuple(vmem(3)),
        compiler_params=params,
        name="cells",
    )(*fields, tables)

    def edge(end, row, high, low):
        blank = jnp.zeros((4, 32), jnp.float32)
        parts = []
        for i in range(3):
            halo = slice(i * WX // 2 + row, i * WX // 2 + row + 4)
            parts.append(
                jnp.concatenate(
                    [
                        ends[end, i],
                        from_high[halo, high : high + 48],
                        blank,
                        from_low[halo, low : low + 48],
                    ],
                    axis=1,
                )
            )
        return jnp.stack(parts)

    low_edge = edge(0, 0, 0, 80)
    high_edge = edge(1, WX // 2 - 4, 48, 32)
    got_second = lax.ppermute(jnp.where(even_x, low_edge, high_edge), "gx", odd_pairs)
    got_first = lax.ppermute(jnp.where(even_x, high_edge, low_edge), "gx", even_pairs)
    halo_xh = jnp.where(even_x, got_first, got_second)
    halo_xl = jnp.where(even_x, got_second, got_first)
    first0, first1, coefs = pl.pallas_call(
        inner_kernel,
        out_shape=(f32(3, WX, LANES), f32(3, WX, LANES), f32(COEFS, WX, LANES)),
        in_specs=vmem(5),
        out_specs=tuple(vmem(3)),
        compiler_params=params,
        name="inner",
    )(cells, props, from_high, from_low, tables)
    tables_x, tables_y = x_tables(), y_tables()
    moment, payload = pl.pallas_call(
        steps_kernel,
        out_shape=(f32(3, WX, COLS), f32(16 * 48, 128)),
        in_specs=vmem(7 + len(tables_x) + len(tables_y)),
        out_specs=tuple(vmem(2)),
        scratch_shapes=[pltpu.VMEM((3, ROWS, LANES), jnp.float32)] * 2
        + [pltpu.VMEM((COEFS, 24, LANES), jnp.float32)]
        + [pltpu.VMEM((3, 8, LANES), jnp.float32)],
        compiler_params=params,
        name="steps",
    )(first0, first1, coefs, halo_xh, halo_xl, tables, sum_matrix(), *tables_x, *tables_y)

    columns = lax.all_to_all(
        payload.reshape(16, 48, 128), "gx", split_axis=0, concat_axis=0, tiled=True
    ).reshape(16 * 48, 128)
    rows = pl.pallas_call(
        x_kernel,
        out_shape=f32(256, 128),
        in_specs=vmem(3),
        out_specs=vmem(1)[0],
        scratch_shapes=[pltpu.VMEM((1024, 256), jnp.bfloat16)] * 2,
        compiler_params=params,
        name="along_x",
    )(columns, *tables_x)
    groups = [
        [gx * 16 + gy for gx in (base, base + 1) for gy in range(16)] for base in range(0, 16, 2)
    ]
    mine = lax.all_to_all(
        rows.reshape(32, 8, 128), ("gx", "gy"), split_axis=0, concat_axis=0, tiled=True,
        axis_index_groups=groups,
    ).reshape(256, 128)
    spin_flip, non_flip = pl.pallas_call(
        y_kernel,
        out_shape=(f32(4, 1024), f32(4, 1024)),
        in_specs=vmem(6),
        out_specs=tuple(vmem(2)),
        scratch_shapes=[pltpu.VMEM((32, 128), jnp.float32)] * 2,
        compiler_params=params,
        name="along_y",
    )(mine, *tables_y)
    return (moment, spin_flip, non_flip)


def solution(mesh):
    in_specs = (P("gx", "gy"), P("gx", "gy"), P("gx", "gy"), P(), P(), P(), P(), P())
    out_specs = (P(None, "gx", "gy"), P(("gx", "gy"), None), P(("gx", "gy"), None))
    return jax.shard_map(shards, mesh=mesh, in_specs=in_specs, out_specs=out_specs, check_vma=False)
```

```python
import math

import jax
import jax.numpy as jnp
import numpy as np
from jax import lax
from jax.experimental import pallas as pl
from jax.experimental.pallas import tpu as pltpu
from jax.sharding import PartitionSpec as P

NZ = 12
STEPS = 4
DAMPING = 0.5
TIME_STEP = 0.12
GAIN = TIME_STEP / (1.0 + DAMPING * DAMPING)

WX = 64
WY = 64
COLS = WY * NZ
LANES = COLS + 128
ROWS = WX + 8
STRIPS = ROWS // 8
NGRAIN = 256

COS_POLY = (
    1.0,
    -0.5,
    0.0416666641831398,
    -0.0013888862449675798,
    2.4800550818326883e-05,
    -2.753476167072222e-07,
    2.060329462594268e-09,
    -9.721622812319808e-12,
)
SIN_POLY = (
    1.0,
    -0.1666666567325592,
    0.008333321660757065,
    -0.00019840530876535922,
    2.7535795652511297e-06,
    -2.472832427713456e-08,
    1.361144114087054e-10,
)


def poly(coefs, t):
    acc = coefs[-1] * t + coefs[-2]
    for c in coefs[-3::-1]:
        acc = acc * t + c
    return acc


def sincos(x):
    t = x * x
    return x * poly(SIN_POLY, t), poly(COS_POLY, t)


def split(x):
    hi = x.astype(jnp.bfloat16)
    lo = (x - hi.astype(jnp.float32)).astype(jnp.bfloat16)
    return hi, lo


def mm(a, b):
    return jnp.dot(a, b, preferred_element_type=jnp.float32)


def iota(shape, dim):
    return lax.broadcasted_iota(jnp.int32, shape, dim)


def strip(ref, s, *lead):
    return ref[(*lead, pl.ds(pl.multiple_of(s * 8, 8), 8), slice(None))]


def put(ref, s, value, *lead):
    ref[(*lead, pl.ds(pl.multiple_of(s * 8, 8), 8), slice(None))] = value


def up(cur, following):
    return pltpu.roll(jnp.where(iota(cur.shape, 0) == 0, following, cur), 7, 0)


def down(cur, previous):
    return pltpu.roll(jnp.where(iota(cur.shape, 0) == 7, previous, cur), 1, 0)


def grain_tables(rows):
    return [
        [jnp.broadcast_to(row[:, h * 128 : h * 128 + 128], (8, 128)) for h in range(2)]
        for row in rows
    ]


def look_up(pair, labels):
    low = labels & 127
    first = labels < 128
    parts = []
    for t in range(labels.shape[1] // 128):
        sl = slice(128 * t, 128 * t + 128)
        a = jnp.take_along_axis(pair[0], low[:, sl], axis=1, mode="promise_in_bounds")
        b = jnp.take_along_axis(pair[1], low[:, sl], axis=1, mode="promise_in_bounds")
        parts.append(jnp.where(first[:, sl], a, b))
    return jnp.concatenate(parts, axis=1)


def start_cells(polar, azimuth):
    sp, cp = sincos(polar)
    sa, ca = sincos(azimuth)
    return sp * ca, sp * sa, cp


def couple(p, q):
    return (2.0 * GAIN) * p * q / (p + q)


def edges_kernel(
    p_low, a_low, g_low, p_high, a_high, g_high,
    stiffness, anisotropy, axis_polar, axis_azimuth, applied,
    first, second, tables,
):
    ax, ay, az = start_cells(axis_polar[...], axis_azimuth[...])
    root = jnp.sqrt(GAIN * anisotropy[...])
    for r, row in enumerate((stiffness[...], root * ax, root * ay, root * az)):
        tables[r : r + 1, :] = row
    for c in range(3):
        tables[4 + c : 5 + c, :] = jnp.full((1, NGRAIN), GAIN * applied[c])

    half = WX // 2
    lane = iota((half, 128), 1)
    even = lax.axis_index("gy") % 2 == 0
    for i, (l, h) in enumerate(((p_low, p_high), (a_low, a_high), (g_low, g_high))):
        l, h = l[...].astype(jnp.float32), h[...].astype(jnp.float32)
        l = jnp.where(lane < 48, l[0:half, :], pltpu.roll(l[half:WX, :], 48, 1))
        h = jnp.where(lane >= 80, h[0:half, :], pltpu.roll(h[half:WX, :], 80, 1))
        first[i * half : (i + 1) * half, :] = jnp.where(even, h, l)
        second[i * half : (i + 1) * half, :] = jnp.where(even, l, h)


def cells_kernel(polar, azimuth, grains, tables, cells, props, ends, same_tables):
    same_tables[...] = tables[...]
    tabs = grain_tables([tables[r : r + 1, :] for r in range(4)])
    for i, src in enumerate((polar, azimuth, grains)):
        ends[0, i] = src[0:4, :].astype(jnp.float32)
        ends[1, i] = src[WX - 4 : WX, :].astype(jnp.float32)

    def body(s, carry):
        start = start_cells(strip(polar, s), strip(azimuth, s))
        for c in range(3):
            put(cells, s, start[c], c)
        labels = strip(grains, s)
        for r in range(4):
            put(props, s, look_up(tabs[r], labels), r)
        return carry

    lax.fori_loop(0, WX // 8, body, 0, unroll=2)


def cell_rows(polar, azimuth, labels, tabs):
    labels = labels.astype(jnp.int32)
    return start_cells(polar, azimuth), [look_up(tab, labels) for tab in tabs]


def coupling_rows(w, after, before):
    xu = couple(w, up(w, after))
    xd = couple(w, down(w, before))
    yu = couple(w, pltpu.roll(w, LANES - NZ, 1))
    yd = pltpu.roll(yu, NZ, 1)
    lane = iota(w.shape, 1)
    depth = jnp.where(lane < COLS + 64, lane, lane - LANES + 6 * NZ + COLS) % NZ
    zu = jnp.where(depth != NZ - 1, couple(w, pltpu.roll(w, LANES - 1, 1)), 0.0)
    zd = pltpu.roll(zu, 1, 1)
    return xu, xd, yu, yd, zu, zd, (xu + xd) + (yu + yd) + (zu + zd)


def applied_rows(tables):
    return [jnp.broadcast_to(tables[4 + c : 5 + c, 0:1], (8, LANES)) for c in range(3)]


def step(src, dst, s, after, before, coefs, row, field, width=LANES):
    whole = [strip(src, s, c) for c in range(3)]
    m = [v[:, 0:width] for v in whole]
    xu, xd, yu, yd, zu, zd, total, *u = (
        strip(coefs, row, r)[:, 0:width] for r in range(1, COEFS)
    )
    proj = u[0] * m[0] + u[1] * m[1] + u[2] * m[2]
    h = []
    for c in range(3):
        f = yu * pltpu.roll(whole[c], LANES - NZ, 1)[:, 0:width]
        f = f + yd * pltpu.roll(whole[c], NZ, 1)[:, 0:width]
        f = f + zu * pltpu.roll(whole[c], LANES - 1, 1)[:, 0:width]
        f = f + zd * pltpu.roll(whole[c], 1, 1)[:, 0:width]
        f = f + xu * up(m[c], strip(src, after, c)[:, 0:width])
        f = f + xd * down(m[c], strip(src, before, c)[:, 0:width])
        h.append(f - total * m[c] + proj * u[c] + field[c][:, 0:width])
    t = cross(m, h)
    d = cross(m, t)
    v = [m[c] - (t[c] + DAMPING * d[c]) for c in range(3)]
    r = lax.rsqrt(v[0] * v[0] + v[1] * v[1] + v[2] * v[2])
    for c in range(3):
        put(dst, s, v[c] * r, c)


COEFS = 11
LAST = WX // 8 - 1


def inner_strips(body):
    def one(s, carry):
        body(s)
        return carry

    lax.fori_loop(1, LAST, one, 0, unroll=3)


def inner_kernel(cells, props, from_high, from_low, tables, m0, m1, coefs):
    tabs = grain_tables([tables[r : r + 1, :] for r in range(4)])
    for c in range(3):
        m0[c, :, 0:COLS] = cells[c]
    for r, i in enumerate((0, 8, 9, 10)):
        coefs[i, :, 0:COLS] = props[r]
    near = iota((8, 128), 1) < 64

    def side(bottom):
        def body(s, carry):
            values = []
            for i in range(3):
                high = strip(from_high, s + i * (WX // 16))
                low = strip(from_low, s + i * (WX // 16))
                if bottom:
                    high, low = pltpu.roll(high, 80, 1), pltpu.roll(low, 48, 1)
                values.append(jnp.where(near, high, low))
            start, found = cell_rows(*values, tabs)
            first = s + (WX // 16 if bottom else 0)
            rows = pl.ds(pl.multiple_of(first * 8, 8), 8)
            for c in range(3):
                m0[c, rows, COLS:LANES] = start[c]
            for r, i in enumerate((0, 8, 9, 10)):
                coefs[i, rows, COLS:LANES] = found[r]
            return carry

        lax.fori_loop(0, WX // 16, body, 0, unroll=4)

    side(False)
    side(True)

    def couplings(s):
        found = coupling_rows(*(strip(coefs, i, 0) for i in (s, s + 1, s - 1)))
        for r, value in enumerate(found):
            put(coefs, s, value, 1 + r)

    inner_strips(couplings)
    field = applied_rows(tables)
    inner_strips(lambda s: step(m0, m1, s, s + 1, s - 1, coefs, s, field))


def steps_kernel(
    first0, first1, coefs, halo_xh, halo_xl, tables, sum_z, *rest
):
    moment, payload, m0, m1, rim, raw = rest[-6:]
    tabs = grain_tables([tables[r : r + 1, :] for r in range(4)])
    for i in range(3):
        raw[i, 0:4, :] = halo_xh[i]
        raw[i, 4:8, :] = halo_xl[i]
    start, found = cell_rows(raw[0], raw[1], raw[2], tabs)
    for c in range(3):
        m0[c, 0:16, :] = first0[c, 0:16, :]
        m0[c, WX - 16 : WX, :] = first0[c, WX - 16 : WX, :]
        m0[c, WX:ROWS, :] = start[c]
        m1[c, 8 : WX - 8, :] = first1[c, 8 : WX - 8, :]
    for r, i in enumerate((0, 8, 9, 10)):
        rim[i, 0:8, :] = coefs[i, WX - 8 : WX, :]
        rim[i, 8:16, :] = found[r]
        rim[i, 16:24, :] = coefs[i, 0:8, :]
    stiff = [coefs[0, WX - 16 : WX - 8, :]]
    stiff += [rim[0, 8 * i : 8 * i + 8, :] for i in range(3)] + [coefs[0, 8:16, :]]
    for i in range(3):
        for r, value in enumerate(coupling_rows(stiff[i + 1], stiff[i + 2], stiff[i])):
            rim[1 + r, 8 * i : 8 * i + 8, :] = value
    field = applied_rows(tables)

    def outer(src, dst, width=LANES):
        for i, s in enumerate((LAST, LAST + 1, 0)):
            if s > LAST and width < LANES:
                continue
            after, before = (s + 1) % STRIPS, (s - 1) % STRIPS
            step(src, dst, s, after, before, rim, i, field, width)

    def inner(src, dst, width=LANES):
        inner_strips(lambda s: step(src, dst, s, s + 1, s - 1, coefs, s, field, width))

    outer(m0, m1)
    for src, dst in ((m1, m0), (m0, m1)):
        outer(src, dst)
        inner(src, dst)
    outer(m1, moment, COLS)
    inner(m1, moment, COLS)

    m = jnp.concatenate([moment[c] for c in range(3)], axis=0)
    hi, lo = split(m)
    out = mm(hi, sum_z[...]) + mm(lo, sum_z[...])
    block = iota((16, 128), 1) // 32
    for half in range(2):
        for c in range(3):
            rows = [
                out[c * WX + 16 * g : c * WX + 16 * g + 16, half * 128 : half * 128 + 128]
                for g in range(4)
            ]
            merged = rows[3]
            for g in range(3):
                merged = jnp.where(block == (g + c) % 4, rows[g], merged)
            for peer in range(8 * half, 8 * half + 8):
                payload[peer * 48 + 16 * c : peer * 48 + 16 * c + 16, :] = merged


def cross(first, second):
    return [
        first[1] * second[2] - first[2] * second[1],
        first[2] * second[0] - first[0] * second[2],
        first[0] * second[1] - first[1] * second[0],
    ]


def x_kernel(got, waves_hi, waves_lo, out, d_hi, d_lo):
    pair = lax.axis_index("gx") % 8
    turn = (pair * iota((16, 128), 0) + 8) % 16 - 8
    sine, cosine = sincos(turn.astype(jnp.float32) * (math.pi / 8.0))
    block = iota((16, 128), 1) // 32

    def unpack(source, carry):
        parts = []
        for c in range(3):
            start = pl.multiple_of(source * 48 + 16 * c, 16)
            parts.append(got[pl.ds(start, 16), :])
        for g in range(4):
            d = jnp.where(
                block == g, parts[0], jnp.where(block == (g + 1) % 4, parts[1], parts[2])
            )
            if g:
                d = pltpu.roll(d, 128 - 32 * g, 1)
            start = pl.multiple_of(source * 64 + 16 * g, 16)
            for i, factor in enumerate((cosine, sine)):
                hi, lo = split(d * factor)
                d_hi[pl.ds(start, 16), 128 * i : 128 * i + 128] = hi
                d_lo[pl.ds(start, 16), 128 * i : 128 * i + 128] = lo
        return carry

    lax.fori_loop(0, 16, unpack, 0, unroll=4)
    both = mm(waves_hi[...], d_hi[...]) + (
        mm(waves_hi[...], d_lo[...]) + mm(waves_lo[...], d_hi[...])
    )
    sign = jnp.where(iota((8, 128), 0) < 4, 1.0, -1.0)
    for t in range(32):
        rows = slice(8 * t, 8 * t + 8)
        out[rows, :] = both[rows, 0:128] + sign * pltpu.roll(both[rows, 128:256], 4, 0)


def y_kernel(
    got, waves_hi, waves_lo, twiddle, last_hi, last_lo,
    spin_flip, non_flip, flat, placed,
):
    parts = []
    for ri in range(2):
        rows = [got[pl.ds(4 * ri + low, 32, stride=8), :] for low in range(4)]
        hi, lo = split(jnp.concatenate(rows, axis=0).T[0:96, :])
        parts.append(
            mm(hi, waves_hi[...]) + (mm(lo, waves_hi[...]) + mm(hi, waves_lo[...]))
        )
    re = parts[0][:, 0:128] + parts[1][:, 128:256]
    im = parts[1][:, 0:128] - parts[0][:, 128:256]
    cosine, sine = twiddle[0:32, :], twiddle[32:64, :]
    turned = []
    for c in range(3):
        r, i = re[32 * c : 32 * c + 32, :], im[32 * c : 32 * c + 32, :]
        turned.append(
            jnp.concatenate([r * cosine + i * sine, i * cosine - r * sine], axis=0)
        )
    hi, lo = split(jnp.concatenate(turned, axis=1))
    full = mm(last_hi[...], hi) + (mm(last_hi[...], lo) + mm(last_lo[...], hi))
    lane = iota((32, 128), 1)
    kx = lax.axis_index("gx") * WX + lax.axis_index("gy") * 4 + lane // 32
    ky = iota((32, 128), 0) * 32 + lane % 32
    wave_x = jnp.where(kx < 512, kx, kx - 1024).astype(jnp.float32)
    wave_y = jnp.where(ky < 512, ky, ky - 1024).astype(jnp.float32)
    squared = wave_x * wave_x + wave_y * wave_y
    inverse = lax.rsqrt(jnp.maximum(squared, 1.0))
    unit_x = wave_x * inverse
    unit_y = wave_y * inverse
    stop = jnp.where(squared > 0.5, 1.0 / (NZ * 1024.0 * 1024.0), 0.0)
    nf = sf = 0.0
    for ri in range(2):
        sx, sy, sz = (full[32 * ri : 32 * ri + 32, 128 * c : 128 * c + 128] for c in range(3))
        along = unit_x * sx + unit_y * sy
        px = sx - unit_x * along
        py = sy - unit_y * along
        nf = nf + px * px
        sf = sf + (py * py + sz * sz)
    block = iota((8, 128), 1) // 32
    for value, dst in ((sf, spin_flip), (nf, non_flip)):
        flat[...] = value * stop
        for low in range(4):
            row = None
            for u in range(4):
                piece = flat[pl.ds(u, 8, stride=4), :]
                if u != low:
                    piece = pltpu.roll(piece, (u - low) % 4 * 32, 1)
                row = piece if row is None else jnp.where(block == u, piece, row)
            placed[pl.ds(low, 8, stride=4), :] = row
        for t in range(8):
            dst[:, 128 * t : 128 * t + 128] = placed[4 * t : 4 * t + 4, :]


def pieces(x):
    hi = x.astype(jnp.bfloat16)
    lo = (x - hi.astype(np.float64)).astype(jnp.bfloat16)
    return jnp.asarray(hi), jnp.asarray(lo)


def sum_matrix():
    y = np.arange(COLS) // NZ
    col = np.arange(256)
    return jnp.asarray(
        (y[:, None] == (col // 128 * 32 + col % 32)[None, :]).astype(jnp.bfloat16)
    )


def x_tables():
    row = np.arange(256)
    k = row // 128 * 512 + row // 8 % 16 * 4 + row % 4
    phase = 2.0 * np.pi * (np.outer(k, np.arange(1024)) % 1024) / 1024.0
    real = (row % 8 < 4)[:, None]
    return pieces(np.where(real, np.cos(phase), -np.sin(phase)))


def y_tables():
    lane = np.arange(128)
    block = 2 * (lane % 16) + lane % 32 // 16
    k = np.arange(128)
    phase = 2.0 * np.pi * (np.outer(block, k % 32) % 32) / 32.0
    same = (lane // 32)[:, None] == (k // 32)[None, :]
    waves = pieces(
        np.concatenate([np.where(same, np.cos(phase), 0.0), np.where(same, np.sin(phase), 0.0)], axis=1)
    )
    q = np.arange(32)
    phase = 2.0 * np.pi * np.outer(q, k % 32) / 1024.0
    twiddle = np.concatenate([np.cos(phase), np.sin(phase)]).astype(np.float32)
    phase = 2.0 * np.pi * (np.outer(q, q) % 32) / 32.0
    c, s = np.cos(phase), np.sin(phase)
    return (*waves, jnp.asarray(twiddle), *pieces(np.block([[c, s], [-s, c]])))


def f32(*shape):
    return jax.ShapeDtypeStruct(shape, jnp.float32)


def vmem(n):
    return [pl.BlockSpec(memory_space=pltpu.VMEM)] * n


def shards(polar, azimuth, grains, stiffness, anisotropy, axis_polar, axis_azimuth, applied_field):
    even_pairs = [(i, i ^ 1) for i in range(16)]
    odd_pairs = [(i, (i + 1) % 16) if i % 2 else (i, (i - 1) % 16) for i in range(16)]
    at_x = lax.axis_index("gx").astype(jnp.int32)
    at_y = lax.axis_index("gy").astype(jnp.int32)
    even_x = at_x % 2 == 0
    even_y = at_y % 2 == 0
    fields = (polar, azimuth, grains)
    params = pltpu.CompilerParams(vmem_limit_bytes=16 << 20)
    smem = [pl.BlockSpec(memory_space=pltpu.SMEM)]
    per_grain = [
        v.reshape(1, NGRAIN) for v in (stiffness, anisotropy, axis_polar, axis_azimuth)
    ]
    first = pl.BlockSpec((WX, 128), lambda i: (0, 0))
    last = pl.BlockSpec((WX, 128), lambda i: (0, COLS // 128 - 1))
    to_first, to_second, tables = pl.pallas_call(
        edges_kernel,
        grid=(1,),
        out_shape=(f32(3 * WX // 2, 128), f32(3 * WX // 2, 128), f32(8, NGRAIN)),
        in_specs=[first] * 3 + [last] * 3 + vmem(4) + smem,
        out_specs=tuple(vmem(3)),
        name="edges",
    )(*fields, *fields, *per_grain, applied_field)
    got_second = lax.ppermute(to_second, "gy", odd_pairs)
    got_first = lax.ppermute(to_first, "gy", even_pairs)
    from_high = jnp.where(even_y, got_first, got_second)
    from_low = jnp.where(even_y, got_second, got_first)

    cells, props, ends, tables = pl.pallas_call(
        cells_kernel,
        out_shape=(f32(3, WX, COLS), f32(4, WX, COLS), f32(2, 3, 4, COLS), f32(8, NGRAIN)),
        in_specs=vmem(4),
        out_specs=tuple(vmem(4)),
        compiler_params=params,
        name="cells",
    )(*fields, tables)

    def edge(end, row, high, low):
        blank = jnp.zeros((4, 32), jnp.float32)
        parts = []
        for i in range(3):
            halo = slice(i * WX // 2 + row, i * WX // 2 + row + 4)
            parts.append(
                jnp.concatenate(
                    [
                        ends[end, i],
                        from_high[halo, high : high + 48],
                        blank,
                        from_low[halo, low : low + 48],
                    ],
                    axis=1,
                )
            )
        return jnp.stack(parts)

    low_edge = edge(0, 0, 0, 80)
    high_edge = edge(1, WX // 2 - 4, 48, 32)
    got_second = lax.ppermute(jnp.where(even_x, low_edge, high_edge), "gx", odd_pairs)
    got_first = lax.ppermute(jnp.where(even_x, high_edge, low_edge), "gx", even_pairs)
    halo_xh = jnp.where(even_x, got_first, got_second)
    halo_xl = jnp.where(even_x, got_second, got_first)
    first0, first1, coefs = pl.pallas_call(
        inner_kernel,
        out_shape=(f32(3, WX, LANES), f32(3, WX, LANES), f32(COEFS, WX, LANES)),
        in_specs=vmem(5),
        out_specs=tuple(vmem(3)),
        compiler_params=params,
        name="inner",
    )(cells, props, from_high, from_low, tables)
    tables_x, tables_y = x_tables(), y_tables()
    moment, payload = pl.pallas_call(
        steps_kernel,
        out_shape=(f32(3, WX, COLS), f32(16 * 48, 128)),
        in_specs=vmem(7 + len(tables_x) + len(tables_y)),
        out_specs=tuple(vmem(2)),
        scratch_shapes=[pltpu.VMEM((3, ROWS, LANES), jnp.float32)] * 2
        + [pltpu.VMEM((COEFS, 24, LANES), jnp.float32)]
        + [pltpu.VMEM((3, 8, LANES), jnp.float32)],
        compiler_params=params,
        name="steps",
    )(first0, first1, coefs, halo_xh, halo_xl, tables, sum_matrix(), *tables_x, *tables_y)

    columns = lax.all_to_all(
        payload.reshape(16, 48, 128), "gx", split_axis=0, concat_axis=0, tiled=True
    ).reshape(16 * 48, 128)
    rows = pl.pallas_call(
        x_kernel,
        out_shape=f32(256, 128),
        in_specs=vmem(3),
        out_specs=vmem(1)[0],
        scratch_shapes=[pltpu.VMEM((1024, 256), jnp.bfloat16)] * 2,
        compiler_params=params,
        name="along_x",
    )(columns, *tables_x)
    groups = [
        [gx * 16 + gy for gx in (base, base + 8) for gy in range(16)] for base in range(8)
    ]
    mine = lax.all_to_all(
        rows.reshape(32, 8, 128), ("gx", "gy"), split_axis=0, concat_axis=0, tiled=True,
        axis_index_groups=groups,
    ).reshape(256, 128)
    spin_flip, non_flip = pl.pallas_call(
        y_kernel,
        out_shape=(f32(4, 1024), f32(4, 1024)),
        in_specs=vmem(6),
        out_specs=tuple(vmem(2)),
        scratch_shapes=[pltpu.VMEM((32, 128), jnp.float32)] * 2,
        compiler_params=params,
        name="along_y",
    )(mine, *tables_y)
    return (moment, spin_flip, non_flip)


def solution(mesh):
    in_specs = (P("gx", "gy"), P("gx", "gy"), P("gx", "gy"), P(), P(), P(), P(), P())
    out_specs = (P(None, "gx", "gy"), P(("gx", "gy"), None), P(("gx", "gy"), None))
    return jax.shard_map(shards, mesh=mesh, in_specs=in_specs, out_specs=out_specs, check_vma=False)
```

```python
import math

import jax
import jax.numpy as jnp
import numpy as np
from jax import lax
from jax.experimental import pallas as pl
from jax.experimental.pallas import tpu as pltpu
from jax.sharding import PartitionSpec as P

NZ = 12
STEPS = 4
DAMPING = 0.5
TIME_STEP = 0.12
GAIN = TIME_STEP / (1.0 + DAMPING * DAMPING)

WX = 64
WY = 64
COLS = WY * NZ
LANES = COLS + 128
ROWS = WX + 8
STRIPS = ROWS // 8
NGRAIN = 256

COS_POLY = (
    1.0,
    -0.5,
    0.0416666641831398,
    -0.0013888862449675798,
    2.4800550818326883e-05,
    -2.753476167072222e-07,
    2.060329462594268e-09,
    -9.721622812319808e-12,
)
SIN_POLY = (
    1.0,
    -0.1666666567325592,
    0.008333321660757065,
    -0.00019840530876535922,
    2.7535795652511297e-06,
    -2.472832427713456e-08,
    1.361144114087054e-10,
)


def poly(coefs, t):
    acc = coefs[-1] * t + coefs[-2]
    for c in coefs[-3::-1]:
        acc = acc * t + c
    return acc


def sincos(x):
    t = x * x
    return x * poly(SIN_POLY, t), poly(COS_POLY, t)


def split(x):
    hi = x.astype(jnp.bfloat16)
    lo = (x - hi.astype(jnp.float32)).astype(jnp.bfloat16)
    return hi, lo


def mm(a, b):
    return jnp.dot(a, b, preferred_element_type=jnp.float32)


def iota(shape, dim):
    return lax.broadcasted_iota(jnp.int32, shape, dim)


def strip(ref, s, *lead):
    return ref[(*lead, pl.ds(pl.multiple_of(s * 8, 8), 8), slice(None))]


def put(ref, s, value, *lead):
    ref[(*lead, pl.ds(pl.multiple_of(s * 8, 8), 8), slice(None))] = value


def up(cur, following):
    return pltpu.roll(jnp.where(iota(cur.shape, 0) == 0, following, cur), 7, 0)


def down(cur, previous):
    return pltpu.roll(jnp.where(iota(cur.shape, 0) == 7, previous, cur), 1, 0)


def grain_tables(rows):
    return [
        [jnp.broadcast_to(row[:, h * 128 : h * 128 + 128], (8, 128)) for h in range(2)]
        for row in rows
    ]


def look_up(pair, labels):
    low = labels & 127
    first = labels < 128
    parts = []
    for t in range(labels.shape[1] // 128):
        sl = slice(128 * t, 128 * t + 128)
        a = jnp.take_along_axis(pair[0], low[:, sl], axis=1, mode="promise_in_bounds")
        b = jnp.take_along_axis(pair[1], low[:, sl], axis=1, mode="promise_in_bounds")
        parts.append(jnp.where(first[:, sl], a, b))
    return jnp.concatenate(parts, axis=1)


def start_cells(polar, azimuth):
    sp, cp = sincos(polar)
    sa, ca = sincos(azimuth)
    return sp * ca, sp * sa, cp


def couple(p, q):
    return (2.0 * GAIN) * p * q / (p + q)


def edges_kernel(
    p_low, a_low, g_low, p_high, a_high, g_high,
    stiffness, anisotropy, axis_polar, axis_azimuth, applied,
    first, second, tables,
):
    ax, ay, az = start_cells(axis_polar[...], axis_azimuth[...])
    root = jnp.sqrt(GAIN * anisotropy[...])
    for r, row in enumerate((stiffness[...], root * ax, root * ay, root * az)):
        tables[r : r + 1, :] = row
    for c in range(3):
        tables[4 + c : 5 + c, :] = jnp.full((1, NGRAIN), GAIN * applied[c])

    half = WX // 2
    lane = iota((half, 128), 1)
    even = lax.axis_index("gy") % 2 == 0
    for i, (l, h) in enumerate(((p_low, p_high), (a_low, a_high), (g_low, g_high))):
        l, h = l[...].astype(jnp.float32), h[...].astype(jnp.float32)
        l = jnp.where(lane < 48, l[0:half, :], pltpu.roll(l[half:WX, :], 48, 1))
        h = jnp.where(lane >= 80, h[0:half, :], pltpu.roll(h[half:WX, :], 80, 1))
        first[i * half : (i + 1) * half, :] = jnp.where(even, h, l)
        second[i * half : (i + 1) * half, :] = jnp.where(even, l, h)


def cells_kernel(polar, azimuth, grains, tables, cells, props, ends, same_tables):
    same_tables[...] = tables[...]
    tabs = grain_tables([tables[r : r + 1, :] for r in range(4)])
    for i, src in enumerate((polar, azimuth, grains)):
        ends[0, i] = src[0:4, :].astype(jnp.float32)
        ends[1, i] = src[WX - 4 : WX, :].astype(jnp.float32)

    def body(s, carry):
        start = start_cells(strip(polar, s), strip(azimuth, s))
        for c in range(3):
            put(cells, s, start[c], c)
        labels = strip(grains, s)
        for r in range(4):
            put(props, s, look_up(tabs[r], labels), r)
        return carry

    lax.fori_loop(0, WX // 8, body, 0, unroll=2)


def cell_rows(polar, azimuth, labels, tabs):
    labels = labels.astype(jnp.int32)
    return start_cells(polar, azimuth), [look_up(tab, labels) for tab in tabs]


def coupling_rows(w, after, before):
    xu = couple(w, up(w, after))
    xd = couple(w, down(w, before))
    yu = couple(w, pltpu.roll(w, LANES - NZ, 1))
    yd = pltpu.roll(yu, NZ, 1)
    lane = iota(w.shape, 1)
    depth = jnp.where(lane < COLS + 64, lane, lane - LANES + 6 * NZ + COLS) % NZ
    zu = jnp.where(depth != NZ - 1, couple(w, pltpu.roll(w, LANES - 1, 1)), 0.0)
    zd = pltpu.roll(zu, 1, 1)
    return xu, xd, yu, yd, zu, zd, (xu + xd) + (yu + yd) + (zu + zd)


def applied_rows(tables):
    return [jnp.broadcast_to(tables[4 + c : 5 + c, 0:1], (8, LANES)) for c in range(3)]


def step(src, dst, s, after, before, coefs, row, field, width=LANES):
    whole = [strip(src, s, c) for c in range(3)]
    m = [v[:, 0:width] for v in whole]
    xu, xd, yu, yd, zu, zd, total, *u = (
        strip(coefs, row, r)[:, 0:width] for r in range(1, COEFS)
    )
    proj = u[0] * m[0] + u[1] * m[1] + u[2] * m[2]
    h = []
    for c in range(3):
        f = yu * pltpu.roll(whole[c], LANES - NZ, 1)[:, 0:width]
        f = f + yd * pltpu.roll(whole[c], NZ, 1)[:, 0:width]
        f = f + zu * pltpu.roll(whole[c], LANES - 1, 1)[:, 0:width]
        f = f + zd * pltpu.roll(whole[c], 1, 1)[:, 0:width]
        f = f + xu * up(m[c], strip(src, after, c)[:, 0:width])
        f = f + xd * down(m[c], strip(src, before, c)[:, 0:width])
        h.append(f - total * m[c] + proj * u[c] + field[c][:, 0:width])
    t = cross(m, h)
    d = cross(m, t)
    v = [m[c] - (t[c] + DAMPING * d[c]) for c in range(3)]
    r = lax.rsqrt(v[0] * v[0] + v[1] * v[1] + v[2] * v[2])
    for c in range(3):
        put(dst, s, v[c] * r, c)


COEFS = 11
LAST = WX // 8 - 1


def inner_strips(body):
    def one(s, carry):
        body(s)
        return carry

    lax.fori_loop(1, LAST, one, 0, unroll=6)


def inner_kernel(cells, props, from_high, from_low, tables, m0, m1, coefs):
    tabs = grain_tables([tables[r : r + 1, :] for r in range(4)])
    for c in range(3):
        m0[c, :, 0:COLS] = cells[c]
    for r, i in enumerate((0, 8, 9, 10)):
        coefs[i, :, 0:COLS] = props[r]
    near = iota((8, 128), 1) < 64

    def side(bottom):
        def body(s, carry):
            values = []
            for i in range(3):
                high = strip(from_high, s + i * (WX // 16))
                low = strip(from_low, s + i * (WX // 16))
                if bottom:
                    high, low = pltpu.roll(high, 80, 1), pltpu.roll(low, 48, 1)
                values.append(jnp.where(near, high, low))
            start, found = cell_rows(*values, tabs)
            first = s + (WX // 16 if bottom else 0)
            rows = pl.ds(pl.multiple_of(first * 8, 8), 8)
            for c in range(3):
                m0[c, rows, COLS:LANES] = start[c]
            for r, i in enumerate((0, 8, 9, 10)):
                coefs[i, rows, COLS:LANES] = found[r]
            return carry

        lax.fori_loop(0, WX // 16, body, 0, unroll=4)

    side(False)
    side(True)

    def couplings(s):
        found = coupling_rows(*(strip(coefs, i, 0) for i in (s, s + 1, s - 1)))
        for r, value in enumerate(found):
            put(coefs, s, value, 1 + r)

    inner_strips(couplings)
    field = applied_rows(tables)
    inner_strips(lambda s: step(m0, m1, s, s + 1, s - 1, coefs, s, field))


def steps_kernel(
    first0, first1, coefs, halo_xh, halo_xl, tables, sum_z, *rest
):
    moment, payload, m0, m1, rim, raw = rest[-6:]
    tabs = grain_tables([tables[r : r + 1, :] for r in range(4)])
    for i in range(3):
        raw[i, 0:4, :] = halo_xh[i]
        raw[i, 4:8, :] = halo_xl[i]
    start, found = cell_rows(raw[0], raw[1], raw[2], tabs)
    for c in range(3):
        m0[c, 0:16, :] = first0[c, 0:16, :]
        m0[c, WX - 16 : WX, :] = first0[c, WX - 16 : WX, :]
        m0[c, WX:ROWS, :] = start[c]
        m1[c, 8 : WX - 8, :] = first1[c, 8 : WX - 8, :]
    for r, i in enumerate((0, 8, 9, 10)):
        rim[i, 0:8, :] = coefs[i, WX - 8 : WX, :]
        rim[i, 8:16, :] = found[r]
        rim[i, 16:24, :] = coefs[i, 0:8, :]
    stiff = [coefs[0, WX - 16 : WX - 8, :]]
    stiff += [rim[0, 8 * i : 8 * i + 8, :] for i in range(3)] + [coefs[0, 8:16, :]]
    for i in range(3):
        for r, value in enumerate(coupling_rows(stiff[i + 1], stiff[i + 2], stiff[i])):
            rim[1 + r, 8 * i : 8 * i + 8, :] = value
    field = applied_rows(tables)

    def outer(src, dst, width=LANES):
        for i, s in enumerate((LAST, LAST + 1, 0)):
            if s > LAST and width < LANES:
                continue
            after, before = (s + 1) % STRIPS, (s - 1) % STRIPS
            step(src, dst, s, after, before, rim, i, field, width)

    def inner(src, dst, width=LANES):
        inner_strips(lambda s: step(src, dst, s, s + 1, s - 1, coefs, s, field, width))

    outer(m0, m1)
    for src, dst in ((m1, m0), (m0, m1)):
        outer(src, dst)
        inner(src, dst)
    outer(m1, moment, COLS)
    inner(m1, moment, COLS)

    m = jnp.concatenate([moment[c] for c in range(3)], axis=0)
    hi, lo = split(m)
    out = mm(hi, sum_z[...]) + mm(lo, sum_z[...])
    block = iota((16, 128), 1) // 32
    for half in range(2):
        for c in range(3):
            rows = [
                out[c * WX + 16 * g : c * WX + 16 * g + 16, half * 128 : half * 128 + 128]
                for g in range(4)
            ]
            merged = rows[3]
            for g in range(3):
                merged = jnp.where(block == (g + c) % 4, rows[g], merged)
            for peer in range(8 * half, 8 * half + 8):
                payload[peer * 48 + 16 * c : peer * 48 + 16 * c + 16, :] = merged


def cross(first, second):
    return [
        first[1] * second[2] - first[2] * second[1],
        first[2] * second[0] - first[0] * second[2],
        first[0] * second[1] - first[1] * second[0],
    ]


def x_kernel(got, waves_hi, waves_lo, out, d_hi, d_lo):
    pair = lax.axis_index("gx") % 8
    turn = (pair * iota((16, 128), 0) + 8) % 16 - 8
    sine, cosine = sincos(turn.astype(jnp.float32) * (math.pi / 8.0))
    block = iota((16, 128), 1) // 32

    def unpack(source, carry):
        parts = []
        for c in range(3):
            start = pl.multiple_of(source * 48 + 16 * c, 16)
            parts.append(got[pl.ds(start, 16), :])
        for g in range(4):
            d = jnp.where(
                block == g, parts[0], jnp.where(block == (g + 1) % 4, parts[1], parts[2])
            )
            if g:
                d = pltpu.roll(d, 128 - 32 * g, 1)
            start = pl.multiple_of(source * 64 + 16 * g, 16)
            for i, factor in enumerate((cosine, sine)):
                hi, lo = split(d * factor)
                d_hi[pl.ds(start, 16), 128 * i : 128 * i + 128] = hi
                d_lo[pl.ds(start, 16), 128 * i : 128 * i + 128] = lo
        return carry

    lax.fori_loop(0, 16, unpack, 0, unroll=4)
    both = mm(waves_hi[...], d_hi[...]) + (
        mm(waves_hi[...], d_lo[...]) + mm(waves_lo[...], d_hi[...])
    )
    sign = jnp.where(iota((8, 128), 0) < 4, 1.0, -1.0)
    for t in range(32):
        rows = slice(8 * t, 8 * t + 8)
        out[rows, :] = both[rows, 0:128] + sign * pltpu.roll(both[rows, 128:256], 4, 0)


def y_kernel(
    got, waves_hi, waves_lo, twiddle, last_hi, last_lo,
    spin_flip, non_flip, flat, placed,
):
    parts = []
    for ri in range(2):
        rows = [got[pl.ds(4 * ri + low, 32, stride=8), :] for low in range(4)]
        hi, lo = split(jnp.concatenate(rows, axis=0).T[0:96, :])
        parts.append(
            mm(hi, waves_hi[...]) + (mm(lo, waves_hi[...]) + mm(hi, waves_lo[...]))
        )
    re = parts[0][:, 0:128] + parts[1][:, 128:256]
    im = parts[1][:, 0:128] - parts[0][:, 128:256]
    cosine, sine = twiddle[0:32, :], twiddle[32:64, :]
    turned = []
    for c in range(3):
        r, i = re[32 * c : 32 * c + 32, :], im[32 * c : 32 * c + 32, :]
        turned.append(
            jnp.concatenate([r * cosine + i * sine, i * cosine - r * sine], axis=0)
        )
    hi, lo = split(jnp.concatenate(turned, axis=1))
    full = mm(last_hi[...], hi) + (mm(last_hi[...], lo) + mm(last_lo[...], hi))
    lane = iota((32, 128), 1)
    kx = lax.axis_index("gx") * WX + lax.axis_index("gy") * 4 + lane // 32
    ky = iota((32, 128), 0) * 32 + lane % 32
    wave_x = jnp.where(kx < 512, kx, kx - 1024).astype(jnp.float32)
    wave_y = jnp.where(ky < 512, ky, ky - 1024).astype(jnp.float32)
    squared = wave_x * wave_x + wave_y * wave_y
    inverse = lax.rsqrt(jnp.maximum(squared, 1.0))
    unit_x = wave_x * inverse
    unit_y = wave_y * inverse
    stop = jnp.where(squared > 0.5, 1.0 / (NZ * 1024.0 * 1024.0), 0.0)
    nf = sf = 0.0
    for ri in range(2):
        sx, sy, sz = (full[32 * ri : 32 * ri + 32, 128 * c : 128 * c + 128] for c in range(3))
        along = unit_x * sx + unit_y * sy
        px = sx - unit_x * along
        py = sy - unit_y * along
        nf = nf + px * px
        sf = sf + (py * py + sz * sz)
    block = iota((8, 128), 1) // 32
    for value, dst in ((sf, spin_flip), (nf, non_flip)):
        flat[...] = value * stop
        for low in range(4):
            row = None
            for u in range(4):
                piece = flat[pl.ds(u, 8, stride=4), :]
                if u != low:
                    piece = pltpu.roll(piece, (u - low) % 4 * 32, 1)
                row = piece if row is None else jnp.where(block == u, piece, row)
            placed[pl.ds(low, 8, stride=4), :] = row
        for t in range(8):
            dst[:, 128 * t : 128 * t + 128] = placed[4 * t : 4 * t + 4, :]


def pieces(x):
    hi = x.astype(jnp.bfloat16)
    lo = (x - hi.astype(np.float64)).astype(jnp.bfloat16)
    return jnp.asarray(hi), jnp.asarray(lo)


def sum_matrix():
    y = np.arange(COLS) // NZ
    col = np.arange(256)
    return jnp.asarray(
        (y[:, None] == (col // 128 * 32 + col % 32)[None, :]).astype(jnp.bfloat16)
    )


def x_tables():
    row = np.arange(256)
    k = row // 128 * 512 + row // 8 % 16 * 4 + row % 4
    phase = 2.0 * np.pi * (np.outer(k, np.arange(1024)) % 1024) / 1024.0
    real = (row % 8 < 4)[:, None]
    return pieces(np.where(real, np.cos(phase), -np.sin(phase)))


def y_tables():
    lane = np.arange(128)
    block = 2 * (lane % 16) + lane % 32 // 16
    k = np.arange(128)
    phase = 2.0 * np.pi * (np.outer(block, k % 32) % 32) / 32.0
    same = (lane // 32)[:, None] == (k // 32)[None, :]
    waves = pieces(
        np.concatenate([np.where(same, np.cos(phase), 0.0), np.where(same, np.sin(phase), 0.0)], axis=1)
    )
    q = np.arange(32)
    phase = 2.0 * np.pi * np.outer(q, k % 32) / 1024.0
    twiddle = np.concatenate([np.cos(phase), np.sin(phase)]).astype(np.float32)
    phase = 2.0 * np.pi * (np.outer(q, q) % 32) / 32.0
    c, s = np.cos(phase), np.sin(phase)
    return (*waves, jnp.asarray(twiddle), *pieces(np.block([[c, s], [-s, c]])))


def f32(*shape):
    return jax.ShapeDtypeStruct(shape, jnp.float32)


def vmem(n):
    return [pl.BlockSpec(memory_space=pltpu.VMEM)] * n


def shards(polar, azimuth, grains, stiffness, anisotropy, axis_polar, axis_azimuth, applied_field):
    even_pairs = [(i, i ^ 1) for i in range(16)]
    odd_pairs = [(i, (i + 1) % 16) if i % 2 else (i, (i - 1) % 16) for i in range(16)]
    at_x = lax.axis_index("gx").astype(jnp.int32)
    at_y = lax.axis_index("gy").astype(jnp.int32)
    even_x = at_x % 2 == 0
    even_y = at_y % 2 == 0
    fields = (polar, azimuth, grains)
    params = pltpu.CompilerParams(vmem_limit_bytes=16 << 20)
    smem = [pl.BlockSpec(memory_space=pltpu.SMEM)]
    per_grain = [
        v.reshape(1, NGRAIN) for v in (stiffness, anisotropy, axis_polar, axis_azimuth)
    ]
    first = pl.BlockSpec((WX, 128), lambda i: (0, 0))
    last = pl.BlockSpec((WX, 128), lambda i: (0, COLS // 128 - 1))
    to_first, to_second, tables = pl.pallas_call(
        edges_kernel,
        grid=(1,),
        out_shape=(f32(3 * WX // 2, 128), f32(3 * WX // 2, 128), f32(8, NGRAIN)),
        in_specs=[first] * 3 + [last] * 3 + vmem(4) + smem,
        out_specs=tuple(vmem(3)),
        name="edges",
    )(*fields, *fields, *per_grain, applied_field)
    got_second = lax.ppermute(to_second, "gy", odd_pairs)
    got_first = lax.ppermute(to_first, "gy", even_pairs)
    from_high = jnp.where(even_y, got_first, got_second)
    from_low = jnp.where(even_y, got_second, got_first)

    cells, props, ends, tables = pl.pallas_call(
        cells_kernel,
        out_shape=(f32(3, WX, COLS), f32(4, WX, COLS), f32(2, 3, 4, COLS), f32(8, NGRAIN)),
        in_specs=vmem(4),
        out_specs=tuple(vmem(4)),
        compiler_params=params,
        name="cells",
    )(*fields, tables)

    def edge(end, row, high, low):
        blank = jnp.zeros((4, 32), jnp.float32)
        parts = []
        for i in range(3):
            halo = slice(i * WX // 2 + row, i * WX // 2 + row + 4)
            parts.append(
                jnp.concatenate(
                    [
                        ends[end, i],
                        from_high[halo, high : high + 48],
                        blank,
                        from_low[halo, low : low + 48],
                    ],
                    axis=1,
                )
            )
        return jnp.stack(parts)

    low_edge = edge(0, 0, 0, 80)
    high_edge = edge(1, WX // 2 - 4, 48, 32)
    got_second = lax.ppermute(jnp.where(even_x, low_edge, high_edge), "gx", odd_pairs)
    got_first = lax.ppermute(jnp.where(even_x, high_edge, low_edge), "gx", even_pairs)
    halo_xh = jnp.where(even_x, got_first, got_second)
    halo_xl = jnp.where(even_x, got_second, got_first)
    first0, first1, coefs = pl.pallas_call(
        inner_kernel,
        out_shape=(f32(3, WX, LANES), f32(3, WX, LANES), f32(COEFS, WX, LANES)),
        in_specs=vmem(5),
        out_specs=tuple(vmem(3)),
        compiler_params=params,
        name="inner",
    )(cells, props, from_high, from_low, tables)
    tables_x, tables_y = x_tables(), y_tables()
    moment, payload = pl.pallas_call(
        steps_kernel,
        out_shape=(f32(3, WX, COLS), f32(16 * 48, 128)),
        in_specs=vmem(7 + len(tables_x) + len(tables_y)),
        out_specs=tuple(vmem(2)),
        scratch_shapes=[pltpu.VMEM((3, ROWS, LANES), jnp.float32)] * 2
        + [pltpu.VMEM((COEFS, 24, LANES), jnp.float32)]
        + [pltpu.VMEM((3, 8, LANES), jnp.float32)],
        compiler_params=params,
        name="steps",
    )(first0, first1, coefs, halo_xh, halo_xl, tables, sum_matrix(), *tables_x, *tables_y)

    columns = lax.all_to_all(
        payload.reshape(16, 48, 128), "gx", split_axis=0, concat_axis=0, tiled=True
    ).reshape(16 * 48, 128)
    rows = pl.pallas_call(
        x_kernel,
        out_shape=f32(256, 128),
        in_specs=vmem(3),
        out_specs=vmem(1)[0],
        scratch_shapes=[pltpu.VMEM((1024, 256), jnp.bfloat16)] * 2,
        compiler_params=params,
        name="along_x",
    )(columns, *tables_x)
    groups = [
        [gx * 16 + gy for gx in (base, base + 8) for gy in range(16)] for base in range(8)
    ]
    mine = lax.all_to_all(
        rows.reshape(32, 8, 128), ("gx", "gy"), split_axis=0, concat_axis=0, tiled=True,
        axis_index_groups=groups,
    ).reshape(256, 128)
    spin_flip, non_flip = pl.pallas_call(
        y_kernel,
        out_shape=(f32(4, 1024), f32(4, 1024)),
        in_specs=vmem(6),
        out_specs=tuple(vmem(2)),
        scratch_shapes=[pltpu.VMEM((32, 128), jnp.float32)] * 2,
        compiler_params=params,
        name="along_y",
    )(mine, *tables_y)
    return (moment, spin_flip, non_flip)


def solution(mesh):
    in_specs = (P("gx", "gy"), P("gx", "gy"), P("gx", "gy"), P(), P(), P(), P(), P())
    out_specs = (P(None, "gx", "gy"), P(("gx", "gy"), None), P(("gx", "gy"), None))
    return jax.shard_map(shards, mesh=mesh, in_specs=in_specs, out_specs=out_specs, check_vma=False)
```

```python
import math

import jax
import jax.numpy as jnp
import numpy as np
from jax import lax
from jax.experimental import pallas as pl
from jax.experimental.pallas import tpu as pltpu
from jax.sharding import PartitionSpec as P

NZ = 12
STEPS = 4
DAMPING = 0.5
TIME_STEP = 0.12
GAIN = TIME_STEP / (1.0 + DAMPING * DAMPING)

WX = 64
WY = 64
COLS = WY * NZ
LANES = COLS + 128
ROWS = WX + 8
STRIPS = ROWS // 8
NGRAIN = 256

COS_POLY = (
    1.0,
    -0.5,
    0.0416666641831398,
    -0.0013888862449675798,
    2.4800550818326883e-05,
    -2.753476167072222e-07,
    2.060329462594268e-09,
    -9.721622812319808e-12,
)
SIN_POLY = (
    1.0,
    -0.1666666567325592,
    0.008333321660757065,
    -0.00019840530876535922,
    2.7535795652511297e-06,
    -2.472832427713456e-08,
    1.361144114087054e-10,
)


def poly(coefs, t):
    acc = coefs[-1] * t + coefs[-2]
    for c in coefs[-3::-1]:
        acc = acc * t + c
    return acc


def sincos(x):
    t = x * x
    return x * poly(SIN_POLY, t), poly(COS_POLY, t)


def split(x):
    hi = x.astype(jnp.bfloat16)
    lo = (x - hi.astype(jnp.float32)).astype(jnp.bfloat16)
    return hi, lo


def mm(a, b):
    return jnp.dot(a, b, preferred_element_type=jnp.float32)


def iota(shape, dim):
    return lax.broadcasted_iota(jnp.int32, shape, dim)


def strip(ref, s, *lead):
    return ref[(*lead, pl.ds(pl.multiple_of(s * 8, 8), 8), slice(None))]


def put(ref, s, value, *lead):
    ref[(*lead, pl.ds(pl.multiple_of(s * 8, 8), 8), slice(None))] = value


def up(cur, following):
    return pltpu.roll(jnp.where(iota(cur.shape, 0) == 0, following, cur), 7, 0)


def down(cur, previous):
    return pltpu.roll(jnp.where(iota(cur.shape, 0) == 7, previous, cur), 1, 0)


def grain_tables(rows):
    return [
        [jnp.broadcast_to(row[:, h * 128 : h * 128 + 128], (8, 128)) for h in range(2)]
        for row in rows
    ]


def look_up(pair, labels):
    low = labels & 127
    first = labels < 128
    parts = []
    for t in range(labels.shape[1] // 128):
        sl = slice(128 * t, 128 * t + 128)
        a = jnp.take_along_axis(pair[0], low[:, sl], axis=1, mode="promise_in_bounds")
        b = jnp.take_along_axis(pair[1], low[:, sl], axis=1, mode="promise_in_bounds")
        parts.append(jnp.where(first[:, sl], a, b))
    return jnp.concatenate(parts, axis=1)


def start_cells(polar, azimuth):
    sp, cp = sincos(polar)
    sa, ca = sincos(azimuth)
    return sp * ca, sp * sa, cp


def couple(p, q):
    return (2.0 * GAIN) * p * q / (p + q)


def edges_kernel(
    p_low, a_low, g_low, p_high, a_high, g_high,
    stiffness, anisotropy, axis_polar, axis_azimuth, applied,
    first, second, tables,
):
    ax, ay, az = start_cells(axis_polar[...], axis_azimuth[...])
    root = jnp.sqrt(GAIN * anisotropy[...])
    for r, row in enumerate((stiffness[...], root * ax, root * ay, root * az)):
        tables[r : r + 1, :] = row
    for c in range(3):
        tables[4 + c : 5 + c, :] = jnp.full((1, NGRAIN), GAIN * applied[c])

    half = WX // 2
    lane = iota((half, 128), 1)
    even = lax.axis_index("gy") % 2 == 0
    for i, (l, h) in enumerate(((p_low, p_high), (a_low, a_high), (g_low, g_high))):
        l, h = l[...].astype(jnp.float32), h[...].astype(jnp.float32)
        l = jnp.where(lane < 48, l[0:half, :], pltpu.roll(l[half:WX, :], 48, 1))
        h = jnp.where(lane >= 80, h[0:half, :], pltpu.roll(h[half:WX, :], 80, 1))
        first[i * half : (i + 1) * half, :] = jnp.where(even, h, l)
        second[i * half : (i + 1) * half, :] = jnp.where(even, l, h)


def cells_kernel(polar, azimuth, grains, tables, cells, props, ends, same_tables):
    same_tables[...] = tables[...]
    tabs = grain_tables([tables[r : r + 1, :] for r in range(4)])
    for i, src in enumerate((polar, azimuth, grains)):
        ends[0, i] = src[0:4, :].astype(jnp.float32)
        ends[1, i] = src[WX - 4 : WX, :].astype(jnp.float32)

    def body(s, carry):
        start = start_cells(strip(polar, s), strip(azimuth, s))
        for c in range(3):
            put(cells, s, start[c], c)
        labels = strip(grains, s)
        for r in range(4):
            put(props, s, look_up(tabs[r], labels), r)
        return carry

    lax.fori_loop(0, WX // 8, body, 0, unroll=4)


def cell_rows(polar, azimuth, labels, tabs):
    labels = labels.astype(jnp.int32)
    return start_cells(polar, azimuth), [look_up(tab, labels) for tab in tabs]


def coupling_rows(w, after, before):
    xu = couple(w, up(w, after))
    xd = couple(w, down(w, before))
    yu = couple(w, pltpu.roll(w, LANES - NZ, 1))
    yd = pltpu.roll(yu, NZ, 1)
    lane = iota(w.shape, 1)
    depth = jnp.where(lane < COLS + 64, lane, lane - LANES + 6 * NZ + COLS) % NZ
    zu = jnp.where(depth != NZ - 1, couple(w, pltpu.roll(w, LANES - 1, 1)), 0.0)
    zd = pltpu.roll(zu, 1, 1)
    return xu, xd, yu, yd, zu, zd, (xu + xd) + (yu + yd) + (zu + zd)


def applied_rows(tables):
    return [jnp.broadcast_to(tables[4 + c : 5 + c, 0:1], (8, LANES)) for c in range(3)]


def step(src, dst, s, after, before, coefs, row, field, width=LANES):
    whole = [strip(src, s, c) for c in range(3)]
    m = [v[:, 0:width] for v in whole]
    xu, xd, yu, yd, zu, zd, total, *u = (
        strip(coefs, row, r)[:, 0:width] for r in range(1, COEFS)
    )
    proj = u[0] * m[0] + u[1] * m[1] + u[2] * m[2]
    h = []
    for c in range(3):
        f = yu * pltpu.roll(whole[c], LANES - NZ, 1)[:, 0:width]
        f = f + yd * pltpu.roll(whole[c], NZ, 1)[:, 0:width]
        f = f + zu * pltpu.roll(whole[c], LANES - 1, 1)[:, 0:width]
        f = f + zd * pltpu.roll(whole[c], 1, 1)[:, 0:width]
        f = f + xu * up(m[c], strip(src, after, c)[:, 0:width])
        f = f + xd * down(m[c], strip(src, before, c)[:, 0:width])
        h.append(f - total * m[c] + proj * u[c] + field[c][:, 0:width])
    t = cross(m, h)
    d = cross(m, t)
    v = [m[c] - (t[c] + DAMPING * d[c]) for c in range(3)]
    r = lax.rsqrt(v[0] * v[0] + v[1] * v[1] + v[2] * v[2])
    for c in range(3):
        put(dst, s, v[c] * r, c)


COEFS = 11
LAST = WX // 8 - 1


def inner_strips(body):
    def one(s, carry):
        body(s)
        return carry

    lax.fori_loop(1, LAST, one, 0, unroll=6)


def inner_kernel(cells, props, from_high, from_low, tables, m0, m1, coefs):
    tabs = grain_tables([tables[r : r + 1, :] for r in range(4)])
    for c in range(3):
        m0[c, :, 0:COLS] = cells[c]
    for r, i in enumerate((0, 8, 9, 10)):
        coefs[i, :, 0:COLS] = props[r]
    near = iota((8, 128), 1) < 64

    def side(bottom):
        def body(s, carry):
            values = []
            for i in range(3):
                high = strip(from_high, s + i * (WX // 16))
                low = strip(from_low, s + i * (WX // 16))
                if bottom:
                    high, low = pltpu.roll(high, 80, 1), pltpu.roll(low, 48, 1)
                values.append(jnp.where(near, high, low))
            start, found = cell_rows(*values, tabs)
            first = s + (WX // 16 if bottom else 0)
            rows = pl.ds(pl.multiple_of(first * 8, 8), 8)
            for c in range(3):
                m0[c, rows, COLS:LANES] = start[c]
            for r, i in enumerate((0, 8, 9, 10)):
                coefs[i, rows, COLS:LANES] = found[r]
            return carry

        lax.fori_loop(0, WX // 16, body, 0, unroll=4)

    side(False)
    side(True)

    def couplings(s):
        found = coupling_rows(*(strip(coefs, i, 0) for i in (s, s + 1, s - 1)))
        for r, value in enumerate(found):
            put(coefs, s, value, 1 + r)

    inner_strips(couplings)
    field = applied_rows(tables)
    inner_strips(lambda s: step(m0, m1, s, s + 1, s - 1, coefs, s, field))


def steps_kernel(
    first0, first1, coefs, halo_xh, halo_xl, tables, sum_z, *rest
):
    moment, payload, m0, m1, rim, raw = rest[-6:]
    tabs = grain_tables([tables[r : r + 1, :] for r in range(4)])
    for i in range(3):
        raw[i, 0:4, :] = halo_xh[i]
        raw[i, 4:8, :] = halo_xl[i]
    start, found = cell_rows(raw[0], raw[1], raw[2], tabs)
    for c in range(3):
        m0[c, 0:16, :] = first0[c, 0:16, :]
        m0[c, WX - 16 : WX, :] = first0[c, WX - 16 : WX, :]
        m0[c, WX:ROWS, :] = start[c]
        m1[c, 8 : WX - 8, :] = first1[c, 8 : WX - 8, :]
    for r, i in enumerate((0, 8, 9, 10)):
        rim[i, 0:8, :] = coefs[i, WX - 8 : WX, :]
        rim[i, 8:16, :] = found[r]
        rim[i, 16:24, :] = coefs[i, 0:8, :]
    stiff = [coefs[0, WX - 16 : WX - 8, :]]
    stiff += [rim[0, 8 * i : 8 * i + 8, :] for i in range(3)] + [coefs[0, 8:16, :]]
    for i in range(3):
        for r, value in enumerate(coupling_rows(stiff[i + 1], stiff[i + 2], stiff[i])):
            rim[1 + r, 8 * i : 8 * i + 8, :] = value
    field = applied_rows(tables)

    def outer(src, dst, width=LANES):
        for i, s in enumerate((LAST, LAST + 1, 0)):
            if s > LAST and width < LANES:
                continue
            after, before = (s + 1) % STRIPS, (s - 1) % STRIPS
            step(src, dst, s, after, before, rim, i, field, width)

    def inner(src, dst, width=LANES):
        inner_strips(lambda s: step(src, dst, s, s + 1, s - 1, coefs, s, field, width))

    outer(m0, m1)
    for src, dst in ((m1, m0), (m0, m1)):
        outer(src, dst)
        inner(src, dst)
    outer(m1, moment, COLS)
    inner(m1, moment, COLS)

    m = jnp.concatenate([moment[c] for c in range(3)], axis=0)
    hi, lo = split(m)
    out = mm(hi, sum_z[...]) + mm(lo, sum_z[...])
    block = iota((16, 128), 1) // 32
    for half in range(2):
        for c in range(3):
            rows = [
                out[c * WX + 16 * g : c * WX + 16 * g + 16, half * 128 : half * 128 + 128]
                for g in range(4)
            ]
            merged = rows[3]
            for g in range(3):
                merged = jnp.where(block == (g + c) % 4, rows[g], merged)
            for peer in range(8 * half, 8 * half + 8):
                payload[peer * 48 + 16 * c : peer * 48 + 16 * c + 16, :] = merged


def cross(first, second):
    return [
        first[1] * second[2] - first[2] * second[1],
        first[2] * second[0] - first[0] * second[2],
        first[0] * second[1] - first[1] * second[0],
    ]


def x_kernel(got, waves_hi, waves_lo, out, d_hi, d_lo):
    pair = lax.axis_index("gx") % 8
    turn = (pair * iota((16, 128), 0) + 8) % 16 - 8
    sine, cosine = sincos(turn.astype(jnp.float32) * (math.pi / 8.0))
    block = iota((16, 128), 1) // 32

    def unpack(source, carry):
        parts = []
        for c in range(3):
            start = pl.multiple_of(source * 48 + 16 * c, 16)
            parts.append(got[pl.ds(start, 16), :])
        for g in range(4):
            d = jnp.where(
                block == g, parts[0], jnp.where(block == (g + 1) % 4, parts[1], parts[2])
            )
            if g:
                d = pltpu.roll(d, 128 - 32 * g, 1)
            start = pl.multiple_of(source * 64 + 16 * g, 16)
            for i, factor in enumerate((cosine, sine)):
                hi, lo = split(d * factor)
                d_hi[pl.ds(start, 16), 128 * i : 128 * i + 128] = hi
                d_lo[pl.ds(start, 16), 128 * i : 128 * i + 128] = lo
        return carry

    lax.fori_loop(0, 16, unpack, 0, unroll=8)
    both = mm(waves_hi[...], d_hi[...]) + (
        mm(waves_hi[...], d_lo[...]) + mm(waves_lo[...], d_hi[...])
    )
    sign = jnp.where(iota((8, 128), 0) < 4, 1.0, -1.0)
    for t in range(32):
        rows = slice(8 * t, 8 * t + 8)
        out[rows, :] = both[rows, 0:128] + sign * pltpu.roll(both[rows, 128:256], 4, 0)


def y_kernel(
    got, waves_hi, waves_lo, twiddle, last_hi, last_lo,
    spin_flip, non_flip, flat, placed,
):
    parts = []
    for ri in range(2):
        rows = [got[pl.ds(4 * ri + low, 32, stride=8), :] for low in range(4)]
        hi, lo = split(jnp.concatenate(rows, axis=0).T[0:96, :])
        parts.append(
            mm(hi, waves_hi[...]) + (mm(lo, waves_hi[...]) + mm(hi, waves_lo[...]))
        )
    re = parts[0][:, 0:128] + parts[1][:, 128:256]
    im = parts[1][:, 0:128] - parts[0][:, 128:256]
    cosine, sine = twiddle[0:32, :], twiddle[32:64, :]
    turned = []
    for c in range(3):
        r, i = re[32 * c : 32 * c + 32, :], im[32 * c : 32 * c + 32, :]
        turned.append(
            jnp.concatenate([r * cosine + i * sine, i * cosine - r * sine], axis=0)
        )
    hi, lo = split(jnp.concatenate(turned, axis=1))
    full = mm(last_hi[...], hi) + (mm(last_hi[...], lo) + mm(last_lo[...], hi))
    lane = iota((32, 128), 1)
    kx = lax.axis_index("gx") * WX + lax.axis_index("gy") * 4 + lane // 32
    ky = iota((32, 128), 0) * 32 + lane % 32
    wave_x = jnp.where(kx < 512, kx, kx - 1024).astype(jnp.float32)
    wave_y = jnp.where(ky < 512, ky, ky - 1024).astype(jnp.float32)
    squared = wave_x * wave_x + wave_y * wave_y
    inverse = lax.rsqrt(jnp.maximum(squared, 1.0))
    unit_x = wave_x * inverse
    unit_y = wave_y * inverse
    stop = jnp.where(squared > 0.5, 1.0 / (NZ * 1024.0 * 1024.0), 0.0)
    nf = sf = 0.0
    for ri in range(2):
        sx, sy, sz = (full[32 * ri : 32 * ri + 32, 128 * c : 128 * c + 128] for c in range(3))
        along = unit_x * sx + unit_y * sy
        px = sx - unit_x * along
        py = sy - unit_y * along
        nf = nf + px * px
        sf = sf + (py * py + sz * sz)
    block = iota((8, 128), 1) // 32
    for value, dst in ((sf, spin_flip), (nf, non_flip)):
        flat[...] = value * stop
        for low in range(4):
            row = None
            for u in range(4):
                piece = flat[pl.ds(u, 8, stride=4), :]
                if u != low:
                    piece = pltpu.roll(piece, (u - low) % 4 * 32, 1)
                row = piece if row is None else jnp.where(block == u, piece, row)
            placed[pl.ds(low, 8, stride=4), :] = row
        for t in range(8):
            dst[:, 128 * t : 128 * t + 128] = placed[4 * t : 4 * t + 4, :]


def pieces(x):
    hi = x.astype(jnp.bfloat16)
    lo = (x - hi.astype(np.float64)).astype(jnp.bfloat16)
    return jnp.asarray(hi), jnp.asarray(lo)


def sum_matrix():
    y = np.arange(COLS) // NZ
    col = np.arange(256)
    return jnp.asarray(
        (y[:, None] == (col // 128 * 32 + col % 32)[None, :]).astype(jnp.bfloat16)
    )


def x_tables():
    row = np.arange(256)
    k = row // 128 * 512 + row // 8 % 16 * 4 + row % 4
    phase = 2.0 * np.pi * (np.outer(k, np.arange(1024)) % 1024) / 1024.0
    real = (row % 8 < 4)[:, None]
    return pieces(np.where(real, np.cos(phase), -np.sin(phase)))


def y_tables():
    lane = np.arange(128)
    block = 2 * (lane % 16) + lane % 32 // 16
    k = np.arange(128)
    phase = 2.0 * np.pi * (np.outer(block, k % 32) % 32) / 32.0
    same = (lane // 32)[:, None] == (k // 32)[None, :]
    waves = pieces(
        np.concatenate([np.where(same, np.cos(phase), 0.0), np.where(same, np.sin(phase), 0.0)], axis=1)
    )
    q = np.arange(32)
    phase = 2.0 * np.pi * np.outer(q, k % 32) / 1024.0
    twiddle = np.concatenate([np.cos(phase), np.sin(phase)]).astype(np.float32)
    phase = 2.0 * np.pi * (np.outer(q, q) % 32) / 32.0
    c, s = np.cos(phase), np.sin(phase)
    return (*waves, jnp.asarray(twiddle), *pieces(np.block([[c, s], [-s, c]])))


def f32(*shape):
    return jax.ShapeDtypeStruct(shape, jnp.float32)


def vmem(n):
    return [pl.BlockSpec(memory_space=pltpu.VMEM)] * n


def shards(polar, azimuth, grains, stiffness, anisotropy, axis_polar, axis_azimuth, applied_field):
    even_pairs = [(i, i ^ 1) for i in range(16)]
    odd_pairs = [(i, (i + 1) % 16) if i % 2 else (i, (i - 1) % 16) for i in range(16)]
    at_x = lax.axis_index("gx").astype(jnp.int32)
    at_y = lax.axis_index("gy").astype(jnp.int32)
    even_x = at_x % 2 == 0
    even_y = at_y % 2 == 0
    fields = (polar, azimuth, grains)
    params = pltpu.CompilerParams(vmem_limit_bytes=16 << 20)
    smem = [pl.BlockSpec(memory_space=pltpu.SMEM)]
    per_grain = [
        v.reshape(1, NGRAIN) for v in (stiffness, anisotropy, axis_polar, axis_azimuth)
    ]
    first = pl.BlockSpec((WX, 128), lambda i: (0, 0))
    last = pl.BlockSpec((WX, 128), lambda i: (0, COLS // 128 - 1))
    to_first, to_second, tables = pl.pallas_call(
        edges_kernel,
        grid=(1,),
        out_shape=(f32(3 * WX // 2, 128), f32(3 * WX // 2, 128), f32(8, NGRAIN)),
        in_specs=[first] * 3 + [last] * 3 + vmem(4) + smem,
        out_specs=tuple(vmem(3)),
        name="edges",
    )(*fields, *fields, *per_grain, applied_field)
    got_second = lax.ppermute(to_second, "gy", odd_pairs)
    got_first = lax.ppermute(to_first, "gy", even_pairs)
    from_high = jnp.where(even_y, got_first, got_second)
    from_low = jnp.where(even_y, got_second, got_first)

    cells, props, ends, tables = pl.pallas_call(
        cells_kernel,
        out_shape=(f32(3, WX, COLS), f32(4, WX, COLS), f32(2, 3, 4, COLS), f32(8, NGRAIN)),
        in_specs=vmem(4),
        out_specs=tuple(vmem(4)),
        compiler_params=params,
        name="cells",
    )(*fields, tables)

    def edge(end, row, high, low):
        blank = jnp.zeros((4, 32), jnp.float32)
        parts = []
        for i in range(3):
            halo = slice(i * WX // 2 + row, i * WX // 2 + row + 4)
            parts.append(
                jnp.concatenate(
                    [
                        ends[end, i],
                        from_high[halo, high : high + 48],
                        blank,
                        from_low[halo, low : low + 48],
                    ],
                    axis=1,
                )
            )
        return jnp.stack(parts)

    low_edge = edge(0, 0, 0, 80)
    high_edge = edge(1, WX // 2 - 4, 48, 32)
    got_second = lax.ppermute(jnp.where(even_x, low_edge, high_edge), "gx", odd_pairs)
    got_first = lax.ppermute(jnp.where(even_x, high_edge, low_edge), "gx", even_pairs)
    halo_xh = jnp.where(even_x, got_first, got_second)
    halo_xl = jnp.where(even_x, got_second, got_first)
    first0, first1, coefs = pl.pallas_call(
        inner_kernel,
        out_shape=(f32(3, WX, LANES), f32(3, WX, LANES), f32(COEFS, WX, LANES)),
        in_specs=vmem(5),
        out_specs=tuple(vmem(3)),
        compiler_params=params,
        name="inner",
    )(cells, props, from_high, from_low, tables)
    tables_x, tables_y = x_tables(), y_tables()
    moment, payload = pl.pallas_call(
        steps_kernel,
        out_shape=(f32(3, WX, COLS), f32(16 * 48, 128)),
        in_specs=vmem(7 + len(tables_x) + len(tables_y)),
        out_specs=tuple(vmem(2)),
        scratch_shapes=[pltpu.VMEM((3, ROWS, LANES), jnp.float32)] * 2
        + [pltpu.VMEM((COEFS, 24, LANES), jnp.float32)]
        + [pltpu.VMEM((3, 8, LANES), jnp.float32)],
        compiler_params=params,
        name="steps",
    )(first0, first1, coefs, halo_xh, halo_xl, tables, sum_matrix(), *tables_x, *tables_y)

    columns = lax.all_to_all(
        payload.reshape(16, 48, 128), "gx", split_axis=0, concat_axis=0, tiled=True
    ).reshape(16 * 48, 128)
    rows = pl.pallas_call(
        x_kernel,
        out_shape=f32(256, 128),
        in_specs=vmem(3),
        out_specs=vmem(1)[0],
        scratch_shapes=[pltpu.VMEM((1024, 256), jnp.bfloat16)] * 2,
        compiler_params=params,
        name="along_x",
    )(columns, *tables_x)
    groups = [
        [gx * 16 + gy for gx in (base, base + 8) for gy in range(16)] for base in range(8)
    ]
    mine = lax.all_to_all(
        rows.reshape(32, 8, 128), ("gx", "gy"), split_axis=0, concat_axis=0, tiled=True,
        axis_index_groups=groups,
    ).reshape(256, 128)
    spin_flip, non_flip = pl.pallas_call(
        y_kernel,
        out_shape=(f32(4, 1024), f32(4, 1024)),
        in_specs=vmem(6),
        out_specs=tuple(vmem(2)),
        scratch_shapes=[pltpu.VMEM((32, 128), jnp.float32)] * 2,
        compiler_params=params,
        name="along_y",
    )(mine, *tables_y)
    return (moment, spin_flip, non_flip)


def solution(mesh):
    in_specs = (P("gx", "gy"), P("gx", "gy"), P("gx", "gy"), P(), P(), P(), P(), P())
    out_specs = (P(None, "gx", "gy"), P(("gx", "gy"), None), P(("gx", "gy"), None))
    return jax.shard_map(shards, mesh=mesh, in_specs=in_specs, out_specs=out_specs, check_vma=False)
```
